32 devices in a mesh: dp: 8 (over z, y), tp: 4 (over x, core).
Axes of the slice: x: 2, y: 2, z: 4, core: 2. Of those that a mesh axis runs over, the one named last changes fastest.
Arguments:
- hidden_in: float32 [2048, 2048], P('dp'), may hold values from -6 to 6
- cotangent: float32 [2048, 2048], P('dp'), may hold values from -6 to 6
- segment_ids: int32 [8, 256], P('dp'), may hold values from 0 to 3, never falling along the last dimension, each value on 1 to 128 neighbouring positions
- expert_ids: int32 [2048, 8], P('dp'), may hold values from 0 to 63, all different within a row; in each aligned block of 256 rows (0 to 255, 256 to 511, ...) at most 48 rows name the same one
- first_gain: bfloat16 [2048], P('dp'), may hold values from 0.5 to 1.5
- query_weight: bfloat16 [2048, 2048], P('dp', 'tp'), may hold values from -4 to 4
- key_weight: bfloat16 [2048, 2048], P('dp', 'tp'), may hold values from -4 to 4
- value_weight: bfloat16 [2048, 2048], P('dp', 'tp'), may hold values from -0.125 to 0.125
- output_weight: bfloat16 [2048, 2048], P('tp', 'dp'), may hold values from -0.375 to 0.375
- query_gain: bfloat16 [16, 128], P('tp', 'dp'), may hold values from 0.5 to 1.5
- key_gain: bfloat16 [16, 128], P('tp', 'dp'), may hold values from 0.5 to 1.5
- second_gain: bfloat16 [2048], P('dp'), may hold values from 0.5 to 1.5
- router_weight: bfloat16 [2048, 64], P('dp'), may hold values from -0.0625 to 0.0625
- gate_weight: bfloat16 [64, 2048, 1024], P('dp', None, 'tp'), may hold values from -0.125 to 0.125
- up_weight: bfloat16 [64, 2048, 1024], P('dp', None, 'tp'), may hold values from -0.125 to 0.125
- down_weight: bfloat16 [64, 1024, 2048], P('dp', 'tp'), may hold values from -6 to 6
Outputs:
- hidden_out: float32 [2048, 2048], P('dp')
- grad_hidden: float32 [2048, 2048], P('dp')
- grad_first_gain: float32 [2048], P('dp')
- grad_query: float32 [2048, 2048], P('dp', 'tp')
- grad_key: float32 [2048, 2048], P('dp', 'tp')
- grad_value: float32 [2048, 2048], P('dp', 'tp')
- grad_output: float32 [2048, 2048], P('tp', 'dp')
- grad_query_gain: float32 [16, 128], P('tp', 'dp')
- grad_key_gain: float32 [16, 128], P('tp', 'dp')
- grad_second_gain: float32 [2048], P('dp')
- grad_router: float32 [2048, 64], P('dp')
- grad_gate: float32 [64, 2048, 1024], P('dp', None, 'tp')
- grad_up: float32 [64, 2048, 1024], P('dp', None, 'tp')
- grad_down: float32 [64, 1024, 2048], P('dp', 'tp')
The draws below stay inside these ranges and needn't reach their ends.
Inputs may be any that keep to these rules, and one draw needn't show every extreme that they name: `expert_ids`: each row names 8 different experts. Within one sequence no expert is named by more than 48 rows, a bound that some block reaches. `segment_ids`: within each sequence the numbers never fall; each document has 1 to 128 tokens and some document has exactly 128.
All inputs are finite; a program needn't handle non-finite values.
Results may differ from the reference program's by a relative error of at most 0.017.
Values may be sent and summed in bfloat16 or wider, within the bound.
No kernel may reach another device: no remote copies, remote signals or barrier semaphores. Data moves between devices by JAX's collectives and lax.ppermute only.
A program may use at most 384 MiB of HBM per device.

```python
import math
import jax
import jax.numpy as jnp
import numpy as np
from jax import lax

D = 2048
HEADS = 16
HD = 128
E = 64
TOPK = 8
FF = 1024
SEQ = 256
CAP = 48
SEQS = 8
TOKENS = 2048
N_TP = 4


def projection(key, salt):
    values = jax.random.normal(jax.random.fold_in(key, salt), (D, D), jnp.float32) / math.sqrt(D)
    return jnp.clip(values, -4.0, 4.0)


def head_gain(key, salt):
    values = 1.0 + 0.1 * jax.random.normal(jax.random.fold_in(key, salt), (HEADS, HD), jnp.float32)
    return jnp.clip(values, 0.5, 1.5)


def draw_hidden_in(key, part):
    values = jax.random.normal(jax.random.fold_in(key, 31), (TOKENS, D), jnp.float32)
    return jnp.clip(values, -6.0, 6.0)


def draw_query_weight(key, part):
    return projection(key, 21).astype(jnp.bfloat16)


def draw_key_weight(key, part):
    return projection(key, 22).astype(jnp.bfloat16)


def draw_query_gain(key, part):
    return head_gain(key, 41).astype(jnp.bfloat16)


def draw_key_gain(key, part):
    return head_gain(key, 51).astype(jnp.bfloat16)


def block_levels(key, extent, split, low, high):
    level, own = 1.0, jax.random.fold_in(key, 6)
    for dim, parts in split:
        draws = jnp.exp(jax.random.uniform(jax.random.fold_in(own, dim), (parts,), jnp.float32, low / len(split), high / len(split)))
        level = level * jnp.repeat(draws, extent[dim] // parts).reshape([-1 if axis == dim else 1 for axis in range(len(extent))])
    return level


def profile(number_of, total, most, lean):
    loads = [(1 << 20) // math.isqrt(standing ** lean) + 1 for standing in range(2, number_of + 1)]
    rest, counts = total - most - (number_of - 1), [1] * (number_of - 1)
    while rest > 0:
        free = [i for i in range(number_of - 1) if counts[i] < most]
        mass, budget = sum([loads[i] for i in free]), rest
        for i in free:
            extra = min(most - counts[i], max(1, budget * loads[i] // mass), rest)
            counts[i] = counts[i] + extra
            rest = rest - extra
    return np.array([most] + counts)


def ragged(rng, count, total, limit, slope):
    if count == 2:
        one = jax.random.randint(rng, (), max(1, total - limit), min(limit, total - 1) + 1)
        return jnp.stack([one, total - one])
    sizes = jnp.asarray(profile(count, total, limit, slope), jnp.int32)
    couples = (count - 1) // 2
    giver, receiver = sizes[1:1 + 2 * couples:2], sizes[2:2 + 2 * couples:2]
    margin = jnp.minimum(giver - 1, limit - receiver)
    passed = jax.random.randint(jax.random.fold_in(rng, 1), (couples,), 0, 1 << 20) % (margin + 1)
    sizes = sizes.at[1:1 + 2 * couples:2].set(giver - passed).at[2:2 + 2 * couples:2].set(receiver + passed)
    return sizes[jax.random.permutation(jax.random.fold_in(rng, 2), count)]


def deal_out(stream_key, own, number, rows, amount, top, bound, lean):
    order = jax.random.permutation(stream_key, amount)
    crowded, common = shares(amount, rows * top, bound, lean, True), shares(amount, rows * top, bound, lean, False)
    places = jnp.arange(amount)

    def named(lengths, offset_by):
        used = int((lengths > 0).sum())
        fixed = max(1, used // 4)
        moved = fixed + (places - fixed + offset_by * (used - fixed)) % max(1, amount - fixed)
        return jnp.zeros((amount,), jnp.int32).at[order[jnp.where(places < fixed, places, moved)]].set(jnp.asarray(lengths, jnp.int32))

    lengths = jnp.where(number % 4 == 0, named(crowded, number // 4), named(common, number - number // 4 - 1))
    mixed = jax.random.permutation(jax.random.fold_in(own, 3), amount)
    donor, taker = mixed[0:amount // 2 * 2:2], mixed[1:amount // 2 * 2:2]
    margin = jnp.minimum(lengths[donor] - 1, bound - lengths[taker]) // 2
    margin = jnp.where((donor == order[0]) | (taker == order[0]) | (lengths[taker] == 0), 0, jnp.maximum(margin, 0))
    moved = jax.random.randint(jax.random.fold_in(own, 4), (amount // 2,), 0, 1 << 20) % (margin + 1)
    lengths = lengths.at[donor].add(-moved).at[taker].add(moved)
    items = jnp.searchsorted(jnp.cumsum(lengths), jnp.arange(rows * top), side="right").astype(jnp.int32)
    grid = items.reshape(top, rows).T
    grid = grid[jax.random.permutation(jax.random.fold_in(own, 1), rows)]
    offset_by = jax.random.randint(jax.random.fold_in(own, 2), (rows, 1), 0, top)
    return jnp.take_along_axis(grid, (jnp.arange(top)[None, :] + offset_by) % top, axis=1)


def shares(count, total, most, skew, full):
    loads = [(1 << 20) // math.isqrt(grade ** skew) + 1 for grade in range(1, count + 1)]
    largest = most if full else min(most, max(-(-total // count), total * loads[0] // sum(loads)))
    least = 1 if total - largest >= count - 1 else 0
    counts, surplus = [largest] + [least] * (count - 1), total - largest - least * (count - 1)
    while surplus > 0:
        candidates = [i for i in range(1, count) if counts[i] < largest] or [i for i in range(1, count) if counts[i] < most]
        pool, budget = sum([loads[i] for i in candidates]), surplus
        for i in candidates:
            addition = min(most - counts[i], max(1, budget * loads[i] // pool), surplus)
            counts[i] = counts[i] + addition
            surplus = surplus - addition
    return np.array(counts)


def centred(key, shape, scale, bound, split=(), held_as=jnp.bfloat16):
    values = jax.random.normal(key, shape, jnp.float32) * scale
    if len(split) > 0:
        values = block_levels(key, shape, split, -0.22, 0.18) * values
    return jnp.clip(values, min=-bound, max=bound).astype(held_as)


def setup_inputs(seed: int = 0) -> dict:
    keys = jax.random.split(jax.random.key(seed), 17)
    hidden_in = draw_hidden_in(jax.random.fold_in(keys[16], 71), 0)
    cotangent = centred(keys[1], (TOKENS, D), 1.0, 6.0, ((0, 8),), jnp.float32)
    segment_ids = jax.vmap(lambda own: jnp.searchsorted(jnp.cumsum(ragged(own, 4, SEQ, SEQ // 2, 2)), jnp.arange(SEQ), side="right"))(jax.random.split(keys[2], SEQS)).reshape((SEQS, SEQ)).astype(jnp.int32)
    expert_ids_keys = jax.random.split(jax.random.fold_in(keys[3], 1), TOKENS // SEQ)
    expert_ids_turns = jax.random.permutation(jax.random.fold_in(keys[3], 3), TOKENS // SEQ)
    expert_ids = jax.vmap(lambda own, number: deal_out(jax.random.fold_in(keys[3], 2), own, number, SEQ, E, TOPK, CAP, 2))(expert_ids_keys, expert_ids_turns).reshape((TOKENS, TOPK))
    first_gain = jnp.clip(1.0 + 0.1 * jax.random.normal(keys[4], (D,), jnp.float32), 0.5, 1.5).astype(jnp.bfloat16)
    query_weight = draw_query_weight(jax.random.fold_in(keys[16], 71), 0)
    key_weight = draw_key_weight(jax.random.fold_in(keys[16], 71), 0)
    value_weight = centred(keys[7], (D, D), D ** -0.5, 0.125, ((0, 8), (1, 4)))
    output_weight = centred(keys[8], (D, D), (D // 8) ** -0.5, 0.375, ((0, 4), (1, 8)))
    query_gain = draw_query_gain(jax.random.fold_in(keys[16], 71), 0)
    key_gain = draw_key_gain(jax.random.fold_in(keys[16], 71), 0)
    second_gain = jnp.clip(1.0 + 0.1 * jax.random.normal(keys[11], (D,), jnp.float32), 0.5, 1.5).astype(jnp.bfloat16)
    router_weight = centred(keys[12], (D, E), (4 * D) ** -0.5, 0.0625, ((0, 8),))
    gate_weight = centred(keys[13], (E, D, FF), D ** -0.5, 0.125, ((0, 8), (2, 4)))
    up_weight = centred(keys[14], (E, D, FF), D ** -0.5, 0.125, ((0, 8), (2, 4)))
    down_weight = centred(keys[15], (E, FF, D), 1 ** -0.5, 6.0, ((0, 8), (1, 4)))
    return {"hidden_in": hidden_in, "cotangent": cotangent, "segment_ids": segment_ids, "expert_ids": expert_ids, "first_gain": first_gain, "query_weight": query_weight, "key_weight": key_weight, "value_weight": value_weight, "output_weight": output_weight, "query_gain": query_gain, "key_gain": key_gain, "second_gain": second_gain, "router_weight": router_weight, "gate_weight": gate_weight, "up_weight": up_weight, "down_weight": down_weight}


epsilon = 1e-05

def narrow(values):
    return lax.optimization_barrier(values.astype(jnp.bfloat16))

def rms_scale(values):
    return lax.rsqrt(lax.optimization_barrier(jnp.mean(values * values, axis=-1, keepdims=True)) + epsilon)

def rms_back(values, scale, scaled_grad):
    return scale * scaled_grad - values * scale ** 3 * lax.optimization_barrier(jnp.mean(scaled_grad * values, axis=-1, keepdims=True))

def rope_tables(length, head_size):
    half_size = head_size // 2
    inverse = 10000.0 ** (-2.0 * jnp.arange(half_size, dtype=jnp.float32) / head_size)
    angles = jnp.arange(length, dtype=jnp.float32)[:, None] * inverse[None, :]
    return (jnp.cos(angles)[:, None, :], jnp.sin(angles)[:, None, :])

def rotate(values, cosine, sine_table):
    half_size = values.shape[-1] // 2
    leading, second = (values[..., :half_size], values[..., half_size:])
    return jnp.concatenate([leading * cosine - second * sine_table, second * cosine + leading * sine_table], axis=-1)

def unrotate(values, cosine, sine_table):
    half_size = values.shape[-1] // 2
    leading, second = (values[..., :half_size], values[..., half_size:])
    return jnp.concatenate([leading * cosine + second * sine_table, second * cosine - leading * sine_table], axis=-1)

def allowed_mask(segments):
    position = jnp.arange(segments.shape[0], dtype=jnp.int32)
    return (position[None, :] <= position[:, None]) & (segments[:, None] == segments[None, :])

def score_table(queries, key_rows, segments):
    score_scale = 1.0 / math.sqrt(queries.shape[-1])
    scores = jnp.einsum('qhd,khd->hqk', queries.astype(jnp.float32), key_rows.astype(jnp.float32)) * score_scale
    allowed = allowed_mask(segments)[None]
    return (jnp.where(allowed, scores, -1e+30), allowed, score_scale)

def attend(queries, key_rows, value_rows, segments):
    scores, allowed, score_scale = score_table(queries, key_rows, segments)
    largest = lax.optimization_barrier(jnp.max(scores, axis=-1, keepdims=True))
    denominator = lax.optimization_barrier(jnp.sum(jnp.where(allowed, jnp.exp(scores - largest), 0.0), axis=-1, keepdims=True))
    log_total = largest + jnp.log(denominator)
    weights = narrow(jnp.where(allowed, jnp.exp(scores - log_total), 0.0))
    mixture = jnp.einsum('hqk,khd->qhd', weights.astype(jnp.float32), value_rows.astype(jnp.float32))
    return (narrow(mixture), log_total)

def attend_back(queries, key_rows, value_rows, segments, log_total, grad_mixture):
    scores, allowed, score_scale = score_table(queries, key_rows, segments)
    full_probs = jnp.where(allowed, jnp.exp(scores - log_total), 0.0)
    low_probs = narrow(full_probs)
    grad_values = jnp.einsum('hqk,qhd->khd', low_probs.astype(jnp.float32), grad_mixture.astype(jnp.float32))
    grad_attn = jnp.einsum('qhd,khd->hqk', grad_mixture.astype(jnp.float32), value_rows.astype(jnp.float32))
    row_dot = lax.optimization_barrier(jnp.sum(full_probs * grad_attn, axis=-1, keepdims=True))
    grad_scores = narrow(full_probs * (grad_attn - row_dot) * score_scale).astype(jnp.float32)
    grad_queries = jnp.einsum('hqk,khd->qhd', grad_scores, key_rows.astype(jnp.float32))
    grad_keys = jnp.einsum('hqk,qhd->khd', grad_scores, queries.astype(jnp.float32))
    return (grad_queries, grad_keys, grad_values)

def slot_table(expert_ids, experts, capacity):
    flat_ids = expert_ids.reshape(-1)
    assignments = flat_ids.shape[0]
    matches = (flat_ids[:, None] == jnp.arange(experts, dtype=jnp.int32)[None, :]).astype(jnp.int32)
    earlier = lax.optimization_barrier(jnp.sum((jnp.cumsum(matches, axis=0) - matches) * matches, axis=1))
    places = (flat_ids * capacity + earlier).astype(jnp.int32)
    slot_owner = jnp.full((experts * capacity,), assignments, jnp.int32).at[places].set(jnp.arange(assignments, dtype=jnp.int32))
    return (slot_owner, places.reshape(expert_ids.shape))

def reference(hidden_in, cotangent, segment_ids, expert_ids, first_gain, query_weight, key_weight, value_weight, output_weight, query_gain, key_gain, second_gain, router_weight, gate_weight, up_weight, down_weight):
    first_scale = rms_scale(hidden_in)
    gain_one = first_gain.astype(jnp.float32)
    normed_one = narrow(hidden_in * first_scale * gain_one)
    queries = jnp.dot(normed_one, query_weight, preferred_element_type=jnp.float32)
    key_proj = jnp.dot(normed_one, key_weight, preferred_element_type=jnp.float32)
    value_proj = narrow(jnp.dot(normed_one, value_weight, preferred_element_type=jnp.float32))
    query_scale = rms_scale(queries)
    key_scale = rms_scale(key_proj)
    query_gains = query_gain.astype(jnp.float32).reshape(D)
    key_gains = key_gain.astype(jnp.float32).reshape(D)
    query_normed = queries * query_scale * query_gains
    key_normed = key_proj * key_scale * key_gains
    cosine, sine_table = rope_tables(SEQ, HD)
    query_rot = narrow(rotate(query_normed.reshape(SEQS, SEQ, HEADS, HD), cosine, sine_table))
    key_rot = narrow(rotate(key_normed.reshape(SEQS, SEQ, HEADS, HD), cosine, sine_table))
    value_heads = value_proj.reshape(SEQS, SEQ, HEADS, HD)
    attended, log_totals = lax.map(lambda packed: attend(packed[0], packed[1], packed[2], packed[3]), (query_rot, key_rot, value_heads, segment_ids))
    attended = attended.reshape(TOKENS, D)
    middle = hidden_in + jnp.dot(attended, output_weight, preferred_element_type=jnp.float32)
    second_scale = rms_scale(middle)
    gain_two = second_gain.astype(jnp.float32)
    normed_two = narrow(middle * second_scale * gain_two)
    logits = jnp.dot(normed_two, router_weight, preferred_element_type=jnp.float32)
    router_probs = jax.nn.softmax(logits, axis=-1)
    chosen = expert_ids[:, :, None] == jnp.arange(E, dtype=jnp.int32)[None, None, :]
    mix_weights = lax.optimization_barrier(jnp.sum(jnp.where(chosen, router_probs[:, None, :], 0.0), axis=-1))
    owners, places = jax.vmap(lambda ids: slot_table(ids, E, CAP))(expert_ids.reshape(SEQS, SEQ, TOPK))
    offsets = jnp.arange(SEQS, dtype=jnp.int32)[:, None] * (SEQ * TOPK)
    global_owner = jnp.where(owners < SEQ * TOPK, owners + offsets, TOKENS * TOPK).astype(jnp.int32)
    by_expert = global_owner.reshape(SEQS, E, CAP).transpose(1, 0, 2).reshape(E, SEQS * CAP)
    normed_pad = jnp.concatenate([normed_two, jnp.zeros((1, D), jnp.bfloat16)], axis=0)
    weight_pad = jnp.concatenate([mix_weights.reshape(-1), jnp.zeros((1,), jnp.float32)])
    grad_pad = jnp.concatenate([cotangent, jnp.zeros((1, D), jnp.float32)], axis=0)
    quarter_size = FF // N_TP

    def expert_rows(assigned, gate_matrix, up_matrix, down_matrix):
        tokens_of = (assigned // TOPK).astype(jnp.int32)
        row_inputs = normed_pad[tokens_of]
        gate_act = jnp.dot(row_inputs, gate_matrix, preferred_element_type=jnp.float32)
        up_act = jnp.dot(row_inputs, up_matrix, preferred_element_type=jnp.float32)
        hidden_act = narrow(jax.nn.silu(gate_act) * up_act)
        output_rows = jnp.zeros((row_inputs.shape[0], D), jnp.float32)
        for quarter in range(N_TP):
            column_start = quarter * quarter_size
            piece_out = jnp.dot(hidden_act[:, column_start:column_start + quarter_size], down_matrix[column_start:column_start + quarter_size], preferred_element_type=jnp.float32)
            output_rows = output_rows + narrow(piece_out).astype(jnp.float32)
        return (tokens_of, row_inputs, gate_act, up_act, hidden_act, output_rows)

    def forward_step(accumulated, packed):
        assigned, gate_matrix, up_matrix, down_matrix = packed
        tokens_of, row_inputs, gate_act, up_act, hidden_act, output_rows = expert_rows(assigned, gate_matrix, up_matrix, down_matrix)
        return (accumulated.at[tokens_of].add(weight_pad[assigned][:, None] * output_rows), None)
    moe_sum, _ = lax.scan(forward_step, jnp.zeros((TOKENS + 1, D), jnp.float32), (by_expert, gate_weight, up_weight, down_weight))
    hidden_out = middle + moe_sum[:TOKENS]

    def backward_step(carried, packed):
        grad_rows_sum, grad_mix_sum = carried
        assigned, gate_matrix, up_matrix, down_matrix = packed
        tokens_of, row_inputs, gate_act, up_act, hidden_act, output_rows = expert_rows(assigned, gate_matrix, up_matrix, down_matrix)
        token_grads = grad_pad[tokens_of]
        grad_mix_sum = grad_mix_sum.at[assigned].add(lax.optimization_barrier(jnp.sum(token_grads * output_rows, axis=-1)))
        grad_rows = narrow(weight_pad[assigned][:, None] * token_grads)
        grad_hidden_act = jnp.dot(grad_rows, down_matrix.T, preferred_element_type=jnp.float32)
        grad_down_e = jnp.dot(hidden_act.T, grad_rows, preferred_element_type=jnp.float32)
        sigmoid_gate = jax.nn.sigmoid(gate_act)
        grad_gate_act = narrow(grad_hidden_act * up_act * sigmoid_gate * (1.0 + gate_act * (1.0 - sigmoid_gate)))
        grad_up_act = narrow(grad_hidden_act * gate_act * sigmoid_gate)
        grad_gate_e = jnp.dot(row_inputs.T, grad_gate_act, preferred_element_type=jnp.float32)
        grad_up_e = jnp.dot(row_inputs.T, grad_up_act, preferred_element_type=jnp.float32)
        grad_inputs = jnp.zeros((row_inputs.shape[0], D), jnp.float32)
        for quarter in range(N_TP):
            column_start = quarter * quarter_size
            piece_grad = jnp.dot(grad_gate_act[:, column_start:column_start + quarter_size], gate_matrix[:, column_start:column_start + quarter_size].T, preferred_element_type=jnp.float32)
            piece_grad = piece_grad + jnp.dot(grad_up_act[:, column_start:column_start + quarter_size], up_matrix[:, column_start:column_start + quarter_size].T, preferred_element_type=jnp.float32)
            grad_inputs = grad_inputs + narrow(piece_grad).astype(jnp.float32)
        grad_rows_sum = grad_rows_sum.at[tokens_of].add(grad_inputs)
        return ((grad_rows_sum, grad_mix_sum), (grad_gate_e, grad_up_e, grad_down_e))
    start_carry = (jnp.zeros((TOKENS + 1, D), jnp.float32), jnp.zeros((TOKENS * TOPK + 1,), jnp.float32))
    (grad_rows_sum, grad_mix_sum), (grad_gate, grad_up, grad_down) = lax.scan(backward_step, start_carry, (by_expert, gate_weight, up_weight, down_weight))
    grad_mix = grad_mix_sum[:TOKENS * TOPK].reshape(TOKENS, TOPK)
    grad_probs = lax.optimization_barrier(jnp.sum(jnp.where(chosen, grad_mix[:, :, None], 0.0), axis=1))
    grad_logits = router_probs * (grad_probs - lax.optimization_barrier(jnp.sum(router_probs * grad_probs, axis=-1, keepdims=True)))
    router_wide = router_weight.astype(jnp.float32)
    grad_normed_two = grad_rows_sum[:TOKENS] + jnp.dot(grad_logits, router_wide.T, precision=lax.Precision.HIGHEST)
    grad_router = jnp.dot(normed_two.astype(jnp.float32).T, grad_logits, precision=lax.Precision.HIGHEST)
    grad_second_gain = lax.optimization_barrier(jnp.sum(grad_normed_two * middle * second_scale, axis=0))
    grad_middle = cotangent + rms_back(middle, second_scale, grad_normed_two * gain_two)
    grad_middle_low = narrow(grad_middle)
    grad_output = jnp.dot(attended.T, grad_middle_low, preferred_element_type=jnp.float32)
    grad_attended = narrow(jnp.dot(grad_middle_low, output_weight.T, preferred_element_type=jnp.float32))
    grad_query_rot, grad_key_rot, grad_values = lax.map(lambda packed: attend_back(packed[0], packed[1], packed[2], packed[3], packed[4], packed[5]), (query_rot, key_rot, value_heads, segment_ids, log_totals, grad_attended.reshape(SEQS, SEQ, HEADS, HD)))
    grad_query_normed = unrotate(grad_query_rot, cosine, sine_table).reshape(TOKENS, D)
    grad_key_normed = unrotate(grad_key_rot, cosine, sine_table).reshape(TOKENS, D)
    grad_query_gain = lax.optimization_barrier(jnp.sum(grad_query_normed * queries * query_scale, axis=0)).reshape(HEADS, HD)
    grad_key_gain = lax.optimization_barrier(jnp.sum(grad_key_normed * key_proj * key_scale, axis=0)).reshape(HEADS, HD)
    grad_queries = narrow(rms_back(queries, query_scale, grad_query_normed * query_gains))
    grad_keys = narrow(rms_back(key_proj, key_scale, grad_key_normed * key_gains))
    grad_values_low = narrow(grad_values.reshape(TOKENS, D))
    grad_query = jnp.dot(normed_one.T, grad_queries, preferred_element_type=jnp.float32)
    grad_key = jnp.dot(normed_one.T, grad_keys, preferred_element_type=jnp.float32)
    grad_value = jnp.dot(normed_one.T, grad_values_low, preferred_element_type=jnp.float32)
    grad_normed_one = jnp.dot(grad_queries, query_weight.T, preferred_element_type=jnp.float32)
    grad_normed_one = grad_normed_one + jnp.dot(grad_keys, key_weight.T, preferred_element_type=jnp.float32)
    grad_normed_one = grad_normed_one + jnp.dot(grad_values_low, value_weight.T, preferred_element_type=jnp.float32)
    grad_first_gain = lax.optimization_barrier(jnp.sum(grad_normed_one * hidden_in * first_scale, axis=0))
    grad_hidden = grad_middle + rms_back(hidden_in, first_scale, grad_normed_one * gain_one)
    return (hidden_out, grad_hidden, grad_first_gain, grad_query, grad_key, grad_value, grad_output, grad_query_gain, grad_key_gain, grad_second_gain, grad_router, grad_gate, grad_up, grad_down)
```

```python
import math

import jax
import jax.numpy as jnp
from jax import lax
from jax.experimental import pallas as pl
from jax.experimental.pallas import tpu as pltpu
from jax.sharding import PartitionSpec as P

D = 2048
HD = 128
E = 64
TOPK = 8
CAP = 48
EXTRA = 2 * E

bf16 = jnp.bfloat16
f32 = jnp.float32

epsilon = 1e-05


def hop(values, move):
    dp, tp = lax.axis_size("dp"), lax.axis_size("tp")
    pairs = []
    for a in range(dp):
        for b in range(tp):
            c, e = move(a, b)
            pairs.append((a * tp + b, c * tp + e))
    return lax.ppermute(values, ("dp", "tp"), pairs)


def over_z(values, steps=1):
    half = lax.axis_size("dp") // 2
    return hop(values, lambda a, b: ((a // 2 + steps) % half * 2 + a % 2, b))


def over_y(values):
    return hop(values, lambda a, b: (a ^ 1, b))


def over_x(values):
    return hop(values, lambda a, b: (a, b ^ 2))


def over_core(values):
    return hop(values, lambda a, b: (a, b ^ 1))


def gather_dp(values):
    half = lax.axis_size("dp") // 2
    line = [values]
    for _ in range(half - 1):
        line.append(over_z(line[-1]))
    return line + [over_y(v) for v in line]


def gather_all(values):
    line = gather_dp(values)
    both = [(v, over_x(v)) for v in line]
    return [(a, over_core(a), b, over_core(b)) for a, b in both]


def absolute_dp(pieces):
    dp = lax.axis_size("dp")
    half = dp // 2
    me = lax.axis_index("dp")
    stack = jnp.stack(pieces).reshape((2, half) + pieces[0].shape)
    stack = jnp.where(me % 2 == 1, stack[::-1], stack)[:, ::-1]
    twice = jnp.concatenate([stack, stack], axis=1)
    turned = lax.dynamic_slice_in_dim(twice, half - 1 - me // 2, half, 1)
    return jnp.swapaxes(turned, 0, 1).reshape((dp,) + pieces[0].shape)


def absolute_tp(pieces, axis=0):
    me = lax.axis_index("tp")
    first = [jnp.where(me % 2 == 1, pieces[i ^ 1], pieces[i]) for i in range(4)]
    second = [jnp.where(me // 2 == 1, first[i ^ 2], first[i]) for i in range(4)]
    return jnp.concatenate(second, axis=axis)


def gather_tp(values):
    other = over_x(values)
    return [values, over_core(values), other, over_core(other)]


def added(*terms):
    total = terms[0].astype(f32)
    for term in terms[1:]:
        total = total + term.astype(f32)
    return total


def scatter_tp(values):
    tp = lax.axis_size("tp")
    me = lax.axis_index("tp")
    share = values.shape[0] // tp
    values = values.astype(bf16)
    part = [lax.dynamic_slice_in_dim(values, (me ^ q) * share, share, 0) for q in range(4)]
    mine = over_core(part[1])
    far = over_core(part[3])
    return added(part[0], mine, over_x(added(part[2], far).astype(bf16)))


def scatter_all(parts):
    half = lax.axis_size("dp") // 2
    share = parts[0].shape[0] // (2 * half)
    mine, far = over_core(parts[1]), over_core(parts[3])
    from_x = over_x(added(parts[2], far).astype(bf16))
    total = added(parts[0], mine, from_x)
    near = total[: half * share]
    from_y = over_y(total[half * share :].astype(bf16))
    line = near + from_y.astype(f32)
    moving = line[(half - 1) * share :]
    for dz in reversed(range(half - 1)):
        moving = line[dz * share : (dz + 1) * share] + over_z(moving.astype(bf16), -1).astype(f32)
    return moving


def chosen_slots(table):
    experts, tokens = table.shape
    place = lax.broadcasted_iota(jnp.int32, (experts, CAP, tokens), 1)
    hit = place == table[:, None, :]
    return jnp.where(hit, 1.0, 0.0).astype(bf16).reshape(experts * CAP, tokens)


def rows_of_slots(pieces, table):
    sequences, experts, tokens = table.shape
    flat = [piece for group in pieces for piece in group]
    share, width = flat[0].shape
    groups = len(flat) // sequences

    def kernel(table_ref, *refs):
        sources, (out_ref, buffer, arrived) = refs[: len(flat)], refs[len(flat) :]
        step = pl.program_id(0)

        @pl.when(step == 0)
        def _():
            for i, source in enumerate(sources):
                pltpu.make_async_copy(
                    source, buffer.at[i // groups, pl.ds(i % groups * share, share)], arrived.at[i]
                ).start()

        for i in range(groups):
            pltpu.make_async_copy(
                sources[i], buffer.at[step, pl.ds(i * share, share)], arrived.at[step * groups + i]
            ).wait()
        picked = jnp.dot(chosen_slots(table_ref[0]), buffer[step], preferred_element_type=f32)
        out_ref[...] = picked.astype(bf16).reshape(experts, CAP, width)

    return pl.pallas_call(
        kernel,
        grid=(sequences,),
        in_specs=[pl.BlockSpec((1, experts, tokens), lambda s: (s, 0, 0))]
        + [pl.BlockSpec(memory_space=pl.ANY)] * len(flat),
        out_specs=pl.BlockSpec((experts, CAP, width), lambda s: (0, s, 0)),
        out_shape=jax.ShapeDtypeStruct((experts, sequences * CAP, width), bf16),
        scratch_shapes=[
            pltpu.VMEM((sequences, tokens, width), bf16),
            pltpu.SemaphoreType.DMA((len(flat),)),
        ],
        compiler_params=pltpu.CompilerParams(vmem_limit_bytes=48 << 20),
        cost_estimate=pl.CostEstimate(
            flops=2 * experts * CAP * sequences * tokens * width,
            bytes_accessed=2 * sequences * (tokens + experts * CAP) * width,
            transcendentals=0,
        ),
        name="rows_of_slots",
    )(table, *flat)


def tokens_of_slots(rows, table):
    sequences, experts, tokens = table.shape
    width = rows.shape[-1]
    share = tokens // 4

    def kernel(table_ref, rows_ref, *outs):
        picked = chosen_slots(table_ref[0])
        total = lax.dot_general(
            picked,
            rows_ref[...].reshape(experts * CAP, width),
            (((0,), (0,)), ((), ())),
            preferred_element_type=f32,
        ).astype(bf16)
        for q, out in enumerate(outs):
            out[...] = total[q * share : (q + 1) * share]

    return pl.pallas_call(
        kernel,
        grid=(sequences,),
        in_specs=[
            pl.BlockSpec((1, experts, tokens), lambda s: (s, 0, 0)),
            pl.BlockSpec((experts, CAP, width), lambda s: (0, s, 0)),
        ],
        out_specs=[pl.BlockSpec((share, width), lambda s: (s, 0))] * 4,
        out_shape=[jax.ShapeDtypeStruct((sequences * share, width), bf16)] * 4,
        compiler_params=pltpu.CompilerParams(vmem_limit_bytes=48 << 20),
        cost_estimate=pl.CostEstimate(
            flops=2 * experts * CAP * sequences * tokens * width,
            bytes_accessed=2 * sequences * (tokens + experts * CAP) * width,
            transcendentals=0,
        ),
        name="tokens_of_slots",
    )(table, rows)


def dot_last(a, b):
    return lax.dot_general(a, b, (((1,), (1,)), ((), ())), preferred_element_type=f32)


def dot_first(a, b):
    return lax.dot_general(a, b, (((0,), (0,)), ((), ())), preferred_element_type=f32)


def per_expert(kernel, experts, ins, outs, flops, name, scalars=()):
    whole = lambda shape: pl.BlockSpec((1,) + tuple(shape[1:]), lambda e: (e, 0, 0))
    in_specs = [pl.BlockSpec(memory_space=pltpu.SMEM)] * len(scalars)
    moved = 0
    for array, block in ins:
        in_specs.append(pl.BlockSpec((1,) + block, lambda e: (e, 0, 0)))
        moved += experts * math.prod(block) * array.dtype.itemsize
    moved += sum(math.prod(o.shape) * o.dtype.itemsize for o in outs)
    return pl.pallas_call(
        kernel,
        grid=(experts,),
        in_specs=in_specs,
        out_specs=[whole(o.shape) for o in outs],
        out_shape=list(outs),
        compiler_params=pltpu.CompilerParams(vmem_limit_bytes=48 << 20),
        cost_estimate=pl.CostEstimate(flops=flops, bytes_accessed=moved, transcendentals=0),
        name=name,
    )(*scalars, *[array for array, _ in ins])


def grad_of_hidden(cot_rows, down_weight):
    experts, rows, width = cot_rows.shape
    hidden = down_weight.shape[1]

    def kernel(cot_ref, down_ref, out_ref):
        out_ref[0] = dot_last(cot_ref[0], down_ref[0])

    return per_expert(
        kernel,
        experts,
        [(cot_rows, (rows, width)), (down_weight, (hidden, width))],
        [jax.ShapeDtypeStruct((experts, rows, hidden), f32)],
        2 * experts * rows * width * hidden,
        "grad_of_hidden",
    )[0]


def expert_step(x_rows, gate_weight, up_weight, hidden_grad, first_expert):
    experts, rows, wide = x_rows.shape
    width, hidden = gate_weight.shape[1:]

    def kernel(base_ref, x_ref, gate_ref, up_ref, grad_ref, back_ref, act_ref, gate_grad_ref, up_grad_ref):
        mine = base_ref[0] + pl.program_id(0)
        x = x_ref[0, :, :width]
        lane = lax.broadcasted_iota(jnp.int32, (rows, EXTRA), 1)
        probs = x_ref[0, :, width:].astype(f32)
        mix = jnp.sum(
            jnp.where((lane == mine) | (lane == mine + E), probs, 0.0), axis=1, keepdims=True
        )
        gate_act = jnp.dot(x, gate_ref[0], preferred_element_type=f32)
        up_act = jnp.dot(x, up_ref[0], preferred_element_type=f32)
        raw = grad_ref[0]
        sig = jax.nn.sigmoid(gate_act)
        silu = gate_act * sig
        act = silu * up_act
        grad_mix = jnp.sum(act * raw, axis=1, keepdims=True)
        act_ref[0] = (mix * act).astype(bf16)
        weighted = mix * raw
        gate_grad = (weighted * up_act * sig * (1.0 + gate_act * (1.0 - sig))).astype(bf16)
        up_grad = (weighted * silu).astype(bf16)
        gate_grad_ref[0] = gate_grad
        up_grad_ref[0] = up_grad
        back_ref[0, :, :width] = (
            dot_last(gate_grad, gate_ref[0]) + dot_last(up_grad, up_ref[0])
        ).astype(bf16)
        coarse = grad_mix.astype(bf16).astype(f32)
        fine = grad_mix - coarse
        back_ref[0, :, width:] = jnp.where(
            lane == mine, coarse, jnp.where(lane == mine + E, fine, 0.0)
        ).astype(bf16)

    small = jax.ShapeDtypeStruct((experts, rows, hidden), bf16)
    return per_expert(
        kernel,
        experts,
        [
            (x_rows, (rows, wide)),
            (gate_weight, (width, hidden)),
            (up_weight, (width, hidden)),
            (hidden_grad, (rows, hidden)),
        ],
        [jax.ShapeDtypeStruct((experts, rows, wide), bf16), small, small, small],
        8 * experts * rows * width * hidden,
        "expert_step",
        (first_expert,),
    )


def expert_out(act, down_weight):
    experts, rows, hidden = act.shape
    width = down_weight.shape[2]

    def kernel(act_ref, down_ref, out_ref):
        out_ref[0] = jnp.dot(act_ref[0], down_ref[0], preferred_element_type=f32).astype(bf16)

    return per_expert(
        kernel,
        experts,
        [(act, (rows, hidden)), (down_weight, (hidden, width))],
        [jax.ShapeDtypeStruct((experts, rows, width), bf16)],
        2 * experts * rows * width * hidden,
        "expert_out",
    )[0]


def expert_weight_grads(x_rows, cot_rows, act, gate_grad, up_grad, width):
    experts, rows, hidden = act.shape

    def kernel(x_ref, cot_ref, act_ref, gate_ref, up_ref, gate_out, up_out, down_out):
        gate_out[0] = dot_first(x_ref[0], gate_ref[0])
        up_out[0] = dot_first(x_ref[0], up_ref[0])
        down_out[0] = dot_first(act_ref[0], cot_ref[0])

    return per_expert(
        kernel,
        experts,
        [
            (x_rows, (rows, width)),
            (cot_rows, (rows, width)),
            (act, (rows, hidden)),
            (gate_grad, (rows, hidden)),
            (up_grad, (rows, hidden)),
        ],
        [
            jax.ShapeDtypeStruct((experts, width, hidden), f32),
            jax.ShapeDtypeStruct((experts, width, hidden), f32),
            jax.ShapeDtypeStruct((experts, hidden, width), f32),
        ],
        6 * experts * rows * width * hidden,
        "expert_weight_grads",
    )


def rms_scale(values):
    return lax.rsqrt(jnp.mean(values * values, axis=-1, keepdims=True) + epsilon)


def rms_back(values, scale, scaled_grad):
    return scale * scaled_grad - values * scale**3 * jnp.mean(
        scaled_grad * values, axis=-1, keepdims=True
    )


def rope_tables(length, head_size):
    half_size = head_size // 2
    inverse = 10000.0 ** (-2.0 * jnp.arange(half_size, dtype=jnp.float32) / head_size)
    angles = jnp.arange(length, dtype=jnp.float32)[:, None] * inverse[None, :]
    return (jnp.cos(angles)[:, None, :], jnp.sin(angles)[:, None, :])


def rotate(values, cosine, sine_table):
    half_size = values.shape[-1] // 2
    leading, second = (values[..., :half_size], values[..., half_size:])
    return jnp.concatenate(
        [leading * cosine - second * sine_table, second * cosine + leading * sine_table], axis=-1
    )


def unrotate(values, cosine, sine_table):
    half_size = values.shape[-1] // 2
    leading, second = (values[..., :half_size], values[..., half_size:])
    return jnp.concatenate(
        [leading * cosine + second * sine_table, second * cosine - leading * sine_table], axis=-1
    )


def allowed_mask(segments):
    position = jnp.arange(segments.shape[0], dtype=jnp.int32)
    return (position[None, :] <= position[:, None]) & (segments[:, None] == segments[None, :])


def score_table(queries, key_rows, segments):
    score_scale = 1.0 / math.sqrt(queries.shape[-1])
    scores = (
        jnp.einsum("qhd,khd->hqk", queries, key_rows, preferred_element_type=jnp.float32)
        * score_scale
    )
    allowed = allowed_mask(segments)[None]
    return (jnp.where(allowed, scores, -1e30), allowed, score_scale)


def attend_local(queries, key_rows, value_rows, segments):
    scores, allowed, score_scale = score_table(queries, key_rows, segments)
    largest = jnp.max(scores, axis=-1, keepdims=True)
    denominator = jnp.sum(
        jnp.where(allowed, jnp.exp(scores - largest), 0.0), axis=-1, keepdims=True
    )
    log_total = largest + jnp.log(denominator)
    weights = jnp.where(allowed, jnp.exp(scores - log_total), 0.0).astype(jnp.bfloat16)
    mixture = jnp.einsum("hqk,khd->qhd", weights, value_rows, preferred_element_type=jnp.float32)
    return (mixture.astype(jnp.bfloat16), log_total)


def attend_local_back(queries, key_rows, value_rows, segments, log_total, grad_mixture):
    scores, allowed, score_scale = score_table(queries, key_rows, segments)
    full_probs = jnp.where(allowed, jnp.exp(scores - log_total), 0.0)
    low_probs = full_probs.astype(jnp.bfloat16)
    grad_values = jnp.einsum(
        "hqk,qhd->khd", low_probs, grad_mixture, preferred_element_type=jnp.float32
    )
    grad_attn = jnp.einsum(
        "qhd,khd->hqk", grad_mixture, value_rows, preferred_element_type=jnp.float32
    )
    row_dot = jnp.sum(full_probs * grad_attn, axis=-1, keepdims=True)
    grad_scores = (full_probs * (grad_attn - row_dot) * score_scale).astype(jnp.bfloat16)
    grad_queries = jnp.einsum(
        "hqk,khd->qhd", grad_scores, key_rows, preferred_element_type=jnp.float32
    )
    grad_keys = jnp.einsum("hqk,qhd->khd", grad_scores, queries, preferred_element_type=jnp.float32)
    return (grad_queries, grad_keys, grad_values)


def coarse_and_fine(values):
    coarse = lax.reduce_precision(values, 8, 7)
    return jnp.concatenate([coarse, values - coarse], axis=-1).astype(bf16)


def slot_tables(expert_ids, local_experts):
    data_size, tensor_size = lax.axis_size("dp"), lax.axis_size("tp")
    ids = jnp.stack(gather_dp(expert_ids.T))
    sequences, top, tokens = ids.shape
    share = tokens // tensor_size
    ids = absolute_tp([ids[:, :, q * share : (q + 1) * share] for q in range(4)], axis=2)
    mine = lax.axis_index("dp") * local_experts + jnp.arange(local_experts, dtype=jnp.int32)
    named = jnp.any(ids[:, None] == mine[None, :, None, None], axis=2)
    position = jnp.arange(tokens, dtype=jnp.int32)
    before = (position[:, None] < position[None, :]).astype(bf16)
    slot = jnp.einsum("set,tu->seu", named.astype(bf16), before, preferred_element_type=f32)
    return jnp.where(named, slot.astype(jnp.int32), -1)


def slabs_of(values):
    dp = lax.axis_size("dp")
    half = dp // 2
    me = lax.axis_index("dp")
    slab = values.shape[1] // dp
    got = []
    for dy in range(2):
        for dz in range(half):
            target = (me // 2 + dz) % half * 2 + (me % 2 ^ dy)
            part = lax.dynamic_slice_in_dim(values, target * slab, slab, 1)
            if dy or dz:
                part = hop(
                    part,
                    lambda a, b, dy=dy, dz=dz: ((a // 2 + dz) % half * 2 + (a % 2 ^ dy), b),
                )
            got.append(part)
    return absolute_tp(gather_tp(jnp.stack(got)), axis=1)


def per_device(
    hidden_in,
    cotangent,
    segment_ids,
    expert_ids,
    first_gain,
    query_weight,
    key_weight,
    value_weight,
    output_weight,
    query_gain,
    key_gain,
    second_gain,
    router_weight,
    gate_weight,
    up_weight,
    down_weight,
):
    data_size = lax.axis_size("dp")
    tensor_size = lax.axis_size("tp")
    seq_len, width = hidden_in.shape
    share = seq_len // tensor_size
    me_dp, me_tp = lax.axis_index("dp"), lax.axis_index("tp")
    own = lambda values: lax.dynamic_slice_in_dim(values, me_tp * share, share, 0)
    local_experts = E // data_size

    table = slot_tables(expert_ids, local_experts)

    rows_full = lambda pieces: absolute_dp(pieces).reshape(width, -1)
    query_full = rows_full(gather_dp(query_weight))
    key_full = rows_full(gather_dp(key_weight))
    value_full = rows_full(gather_dp(value_weight))
    output_full = jnp.swapaxes(absolute_dp(gather_dp(output_weight)), 0, 1).reshape(
        output_weight.shape[0], width
    )
    small = jnp.concatenate(
        [
            router_weight.reshape(-1),
            first_gain,
            second_gain,
            query_gain.reshape(-1),
            key_gain.reshape(-1),
        ]
    )
    small = absolute_dp(gather_dp(small))
    slab = width // data_size
    cut = slab * E
    router_full = small[:, :cut].reshape(width, E)
    gain_one = small[:, cut : cut + slab].reshape(-1).astype(f32)
    gain_two = small[:, cut + slab : cut + 2 * slab].reshape(-1).astype(f32)
    heads_local = query_gain.shape[0]
    piece = heads_local * query_gain.shape[1]
    cut = cut + 2 * slab
    spread = lambda v: jnp.swapaxes(v.reshape(data_size, heads_local, -1), 0, 1).reshape(-1).astype(f32)
    query_gains = spread(small[:, cut : cut + piece])
    key_gains = spread(small[:, cut + piece : cut + 2 * piece])

    cot_own = own(cotangent)
    cot_rows = rows_of_slots(gather_all(cot_own.astype(bf16)), table)
    hidden_grad = grad_of_hidden(cot_rows, down_weight)

    segments = segment_ids[0]
    first_scale = rms_scale(hidden_in)
    normed_one = (hidden_in * first_scale * gain_one).astype(jnp.bfloat16)
    queries = jnp.dot(normed_one, query_full, preferred_element_type=jnp.float32)
    key_proj = jnp.dot(normed_one, key_full, preferred_element_type=jnp.float32)
    value_proj = jnp.dot(normed_one, value_full, preferred_element_type=jnp.float32).astype(
        jnp.bfloat16
    )
    query_squares, key_squares = lax.psum(
        (jnp.sum(queries * queries, axis=-1), jnp.sum(key_proj * key_proj, axis=-1)), "tp"
    )
    query_scale = lax.rsqrt(query_squares[:, None] / D + epsilon)
    key_scale = lax.rsqrt(key_squares[:, None] / D + epsilon)
    query_normed = queries * query_scale * query_gains
    key_normed = key_proj * key_scale * key_gains
    cosine, sine_table = rope_tables(seq_len, HD)
    query_rot = rotate(query_normed.reshape(seq_len, heads_local, HD), cosine, sine_table).astype(
        jnp.bfloat16
    )
    key_rot = rotate(key_normed.reshape(seq_len, heads_local, HD), cosine, sine_table).astype(
        jnp.bfloat16
    )
    value_heads = value_proj.reshape(seq_len, heads_local, HD)
    attended_heads, log_total = attend_local(query_rot, key_rot, value_heads, segments)
    attended = attended_heads.reshape(seq_len, heads_local * HD)
    middle = own(hidden_in) + scatter_tp(
        jnp.dot(attended, output_full, preferred_element_type=jnp.float32)
    )
    second_scale = rms_scale(middle)
    normed_two = (middle * second_scale * gain_two).astype(jnp.bfloat16)
    logits = jnp.dot(normed_two, router_full, preferred_element_type=jnp.float32)
    router_probs = jax.nn.softmax(logits, axis=-1)

    x_pieces = gather_all(jnp.concatenate([normed_two, coarse_and_fine(router_probs)], axis=1))
    x_rows = rows_of_slots(x_pieces, table)
    first_expert = (me_dp * local_experts).astype(jnp.int32).reshape(1)
    back_rows, act, gate_grad, up_grad = expert_step(
        x_rows, gate_weight, up_weight, hidden_grad, first_expert
    )
    back = scatter_all(tokens_of_slots(back_rows, table))
    moe = scatter_all(tokens_of_slots(expert_out(act, down_weight), table))
    grad_gate, grad_up, grad_down = expert_weight_grads(
        x_rows, cot_rows, act, gate_grad, up_grad, width
    )
    hidden_out = absolute_tp(gather_tp(middle + moe))

    grad_probs = back[:, width : width + E] + back[:, width + E :]
    grad_logits = router_probs * (
        grad_probs - jnp.sum(router_probs * grad_probs, axis=-1, keepdims=True)
    )
    grad_normed_two = back[:, :width] + jnp.dot(
        grad_logits, router_full.astype(jnp.float32).T, precision=lax.Precision.HIGHEST
    )
    grad_router = jnp.dot(
        normed_two.astype(jnp.float32).T, grad_logits, precision=lax.Precision.HIGHEST
    )
    grad_second_gain = jnp.sum(grad_normed_two * middle * second_scale, axis=0)
    grad_middle = cot_own + rms_back(middle, second_scale, grad_normed_two * gain_two)
    grad_middle_low = grad_middle.astype(jnp.bfloat16)
    grad_middle_all = absolute_tp(gather_tp(grad_middle_low))
    grad_attended = jnp.dot(
        grad_middle_all, output_full.T, preferred_element_type=jnp.float32
    ).astype(jnp.bfloat16)
    grad_query_rot, grad_key_rot, grad_values = attend_local_back(
        query_rot,
        key_rot,
        value_heads,
        segments,
        log_total,
        grad_attended.reshape(seq_len, heads_local, HD),
    )
    grad_query_normed = unrotate(grad_query_rot, cosine, sine_table).reshape(seq_len, -1)
    grad_key_normed = unrotate(grad_key_rot, cosine, sine_table).reshape(seq_len, -1)
    grad_query_gain = jnp.sum(grad_query_normed * queries * query_scale, axis=0).reshape(
        heads_local, HD
    )
    grad_key_gain = jnp.sum(grad_key_normed * key_proj * key_scale, axis=0).reshape(heads_local, HD)
    query_scaled_grad = grad_query_normed * query_gains
    key_scaled_grad = grad_key_normed * key_gains
    query_inner, key_inner = lax.psum(
        (
            jnp.sum(query_scaled_grad * queries, axis=-1),
            jnp.sum(key_scaled_grad * key_proj, axis=-1),
        ),
        "tp",
    )
    grad_queries = (
        query_scale * query_scaled_grad - queries * query_scale**3 * (query_inner[:, None] / D)
    ).astype(jnp.bfloat16)
    grad_keys = (
        key_scale * key_scaled_grad - key_proj * key_scale**3 * (key_inner[:, None] / D)
    ).astype(jnp.bfloat16)
    grad_values_low = grad_values.reshape(seq_len, -1).astype(jnp.bfloat16)

    stacked = lambda v: jnp.stack(gather_dp(v)).reshape(-1, v.shape[1])
    flat = lambda v: v.reshape(-1, v.shape[2])
    one_slab = flat(slabs_of(own(normed_one)))
    middle_slab = flat(slabs_of(grad_middle_low))
    grad_output = dot_first(stacked(attended), middle_slab)
    grad_query = dot_first(one_slab, stacked(grad_queries))
    grad_key = dot_first(one_slab, stacked(grad_keys))
    grad_value = dot_first(one_slab, stacked(grad_values_low))

    grad_normed_local = dot_last(grad_queries, query_full)
    grad_normed_local = grad_normed_local + dot_last(grad_keys, key_full)
    grad_normed_local = grad_normed_local + dot_last(grad_values_low, value_full)
    grad_normed_one = scatter_tp(grad_normed_local)
    hidden_own = own(hidden_in)
    scale_own = own(first_scale)
    grad_first_gain = jnp.sum(grad_normed_one * hidden_own * scale_own, axis=0)
    grad_hidden = absolute_tp(
        gather_tp(grad_middle + rms_back(hidden_own, scale_own, grad_normed_one * gain_one))
    )

    tokenwise = lax.psum_scatter(
        jnp.concatenate([grad_router.T, grad_first_gain[None], grad_second_gain[None]]),
        "dp",
        scatter_dimension=1,
        tiled=True,
    )
    tokenwise = lax.psum(tokenwise, "tp")
    grad_router = tokenwise[:E].T
    grad_first_gain = tokenwise[E]
    grad_second_gain = tokenwise[E + 1]
    headwise = lax.psum_scatter(
        jnp.concatenate([grad_query_gain, grad_key_gain]), "dp", scatter_dimension=1, tiled=True
    )
    return (
        hidden_out,
        grad_hidden,
        grad_first_gain,
        grad_query,
        grad_key,
        grad_value,
        grad_output,
        headwise[:heads_local],
        headwise[heads_local:],
        grad_second_gain,
        grad_router,
        grad_gate,
        grad_up,
        grad_down,
    )


def solution(mesh):
    return jax.shard_map(
        per_device,
        mesh=mesh,
        in_specs=(
            P("dp", None),
            P("dp", None),
            P("dp", None),
            P("dp", None),
            P("dp"),
            P("dp", "tp"),
            P("dp", "tp"),
            P("dp", "tp"),
            P("tp", "dp"),
            P("tp", "dp"),
            P("tp", "dp"),
            P("dp"),
            P("dp", None),
            P("dp", None, "tp"),
            P("dp", None, "tp"),
            P("dp", "tp", None),
        ),
        out_specs=(
            P("dp", None),
            P("dp", None),
            P("dp"),
            P("dp", "tp"),
            P("dp", "tp"),
            P("dp", "tp"),
            P("tp", "dp"),
            P("tp", "dp"),
            P("tp", "dp"),
            P("dp"),
            P("dp", None),
            P("dp", None, "tp"),
            P("dp", None, "tp"),
            P("dp", "tp", None),
        ),
        check_vma=False,
    )
```

```python
import math

import jax
import jax.numpy as jnp
from jax import lax
from jax.experimental import pallas as pl
from jax.experimental.pallas import tpu as pltpu
from jax.sharding import PartitionSpec as P

D = 2048
HD = 128
E = 64
TOPK = 8
CAP = 48
EXTRA = 2 * E

bf16 = jnp.bfloat16
f32 = jnp.float32

epsilon = 1e-05


def hop(values, move):
    dp, tp = lax.axis_size("dp"), lax.axis_size("tp")
    pairs = []
    for a in range(dp):
        for b in range(tp):
            c, e = move(a, b)
            pairs.append((a * tp + b, c * tp + e))
    return lax.ppermute(values, ("dp", "tp"), pairs)


def over_z(values, steps=1):
    half = lax.axis_size("dp") // 2
    return hop(values, lambda a, b: ((a // 2 + steps) % half * 2 + a % 2, b))


def over_y(values):
    return hop(values, lambda a, b: (a ^ 1, b))


def over_x(values):
    return hop(values, lambda a, b: (a, b ^ 2))


def over_core(values):
    return hop(values, lambda a, b: (a, b ^ 1))


def gather_dp(values):
    half = lax.axis_size("dp") // 2
    line = [values]
    for _ in range(half - 1):
        line.append(over_z(line[-1]))
    return line + [over_y(v) for v in line]


def gather_all(values):
    line = gather_dp(values)
    both = [(v, over_x(v)) for v in line]
    return [(a, over_core(a), b, over_core(b)) for a, b in both]


def absolute_dp(pieces):
    dp = lax.axis_size("dp")
    half = dp // 2
    me = lax.axis_index("dp")
    backwards = [(half - 1 - i) % half for i in range(2 * half - 1)]
    near = jnp.stack([pieces[dz] for dz in backwards])
    far = jnp.stack([pieces[half + dz] for dz in backwards])
    start = half - 1 - me // 2
    near = lax.dynamic_slice_in_dim(near, start, half, 0)
    far = lax.dynamic_slice_in_dim(far, start, half, 0)
    odd = me % 2 == 1
    both = jnp.stack([jnp.where(odd, far, near), jnp.where(odd, near, far)], axis=1)
    return both.reshape((dp,) + pieces[0].shape)


def absolute_tp(pieces, axis=0):
    me = lax.axis_index("tp")
    first = [jnp.where(me % 2 == 1, pieces[i ^ 1], pieces[i]) for i in range(4)]
    second = [jnp.where(me // 2 == 1, first[i ^ 2], first[i]) for i in range(4)]
    return jnp.concatenate(second, axis=axis)


def gather_tp(values):
    other = over_x(values)
    return [values, over_core(values), other, over_core(other)]


def added(*terms):
    total = terms[0].astype(f32)
    for term in terms[1:]:
        total = total + term.astype(f32)
    return total


def scatter_tp(parts):
    mine, far = over_core(parts[1]), over_core(parts[3])
    return parts[0], mine, over_x(added(parts[2], far).astype(bf16))


def after(values, *others):
    return lax.optimization_barrier((values,) + others)[0]


def scatter_near(parts, wait=()):
    first = after(parts[1], *wait) if wait else parts[1]
    mine, far = over_core(first), over_core(parts[3])
    crossing = added(parts[2], far).astype(bf16)
    return added(parts[0], mine, over_x(crossing)), crossing


def scatter_line(near, far_line, between=()):
    half = lax.axis_size("dp") // 2
    share = near.shape[0] // half
    between = list(between)
    gate = lambda values: after(values, *between.pop(0)) if between else values
    line = near + over_y(gate(far_line.astype(bf16))).astype(f32)
    moving = line[(half - 1) * share :]
    for dz in reversed(range(1, half - 1)):
        moving = gate(moving.astype(bf16))
        moving = line[dz * share : (dz + 1) * share] + over_z(moving, -1).astype(f32)
    return line[:share], over_z(gate(moving.astype(bf16)), -1)


def owner(pos):
    half = lax.axis_size("dp") // 2
    me = lax.axis_index("dp")
    return (me // 2 - pos % half) % half * 2 + (me % 2 ^ pos // half)


def reduce_dp(values):
    dp = lax.axis_size("dp")
    half = dp // 2
    slab = values.shape[1] // dp
    part = [lax.dynamic_slice_in_dim(values, owner(i) * slab, slab, 1) for i in range(dp)]
    line = jnp.stack(part[:half]) + over_y(jnp.stack(part[half:]))
    moving = line[half - 1]
    for dz in reversed(range(half - 1)):
        moving = line[dz] + over_z(moving, -1)
    return moving


def reduce_tp(values):
    values = values + over_core(values)
    return values + over_x(values)


def chosen_slots(table):
    experts, tokens = table.shape
    place = lax.broadcasted_iota(jnp.int32, (experts, CAP, tokens), 1)
    hit = place == table[:, None, :]
    return jnp.where(hit, 1.0, 0.0).astype(bf16).reshape(experts * CAP, tokens)


def rows_of_slots(pieces, table):
    sequences, experts, tokens = table.shape
    flat = [piece for group in pieces for piece in group]
    share, width = flat[0].shape
    groups = len(flat) // sequences

    def kernel(table_ref, *refs):
        sources, (out_ref, buffer, arrived) = refs[: len(flat)], refs[len(flat) :]
        step = pl.program_id(0)

        @pl.when(step == 0)
        def _():
            for i, source in enumerate(sources):
                pltpu.make_async_copy(
                    source, buffer.at[i // groups, pl.ds(i % groups * share, share)], arrived.at[i]
                ).start()

        for i in range(groups):
            pltpu.make_async_copy(
                sources[i], buffer.at[step, pl.ds(i * share, share)], arrived.at[step * groups + i]
            ).wait()
        picked = jnp.dot(chosen_slots(table_ref[0]), buffer[step], preferred_element_type=f32)
        out_ref[...] = picked.astype(bf16).reshape(experts, CAP, width)

    return pl.pallas_call(
        kernel,
        grid=(sequences,),
        in_specs=[pl.BlockSpec((1, experts, tokens), lambda s: (s, 0, 0))]
        + [pl.BlockSpec(memory_space=pl.ANY)] * len(flat),
        out_specs=pl.BlockSpec((experts, CAP, width), lambda s: (0, s, 0)),
        out_shape=jax.ShapeDtypeStruct((experts, sequences * CAP, width), bf16),
        scratch_shapes=[
            pltpu.VMEM((sequences, tokens, width), bf16),
            pltpu.SemaphoreType.DMA((len(flat),)),
        ],
        compiler_params=pltpu.CompilerParams(vmem_limit_bytes=48 << 20),
        cost_estimate=pl.CostEstimate(
            flops=2 * experts * CAP * sequences * tokens * width,
            bytes_accessed=2 * sequences * (tokens + experts * CAP) * width,
            transcendentals=0,
        ),
        name="rows_of_slots",
    )(table, *flat)


def tokens_of_slots(rows, table):
    sequences, experts, tokens = table.shape
    width = rows.shape[-1]
    share = tokens // 4

    def kernel(table_ref, rows_ref, *outs):
        picked = chosen_slots(table_ref[0])
        total = lax.dot_general(
            picked,
            rows_ref[...].reshape(experts * CAP, width),
            (((0,), (0,)), ((), ())),
            preferred_element_type=f32,
        ).astype(bf16)
        for q, out in enumerate(outs):
            out[...] = total[q * share : (q + 1) * share]

    return pl.pallas_call(
        kernel,
        grid=(sequences,),
        in_specs=[
            pl.BlockSpec((1, experts, tokens), lambda s: (s, 0, 0)),
            pl.BlockSpec((experts, CAP, width), lambda s: (0, s, 0)),
        ],
        out_specs=[pl.BlockSpec((share, width), lambda s: (s, 0))] * 4,
        out_shape=[jax.ShapeDtypeStruct((sequences * share, width), bf16)] * 4,
        compiler_params=pltpu.CompilerParams(vmem_limit_bytes=48 << 20),
        cost_estimate=pl.CostEstimate(
            flops=2 * experts * CAP * sequences * tokens * width,
            bytes_accessed=2 * sequences * (tokens + experts * CAP) * width,
            transcendentals=0,
        ),
        name="tokens_of_slots",
    )(table, rows)


def dot_last(a, b):
    return lax.dot_general(a, b, (((1,), (1,)), ((), ())), preferred_element_type=f32)


def dot_first(a, b):
    return lax.dot_general(a, b, (((0,), (0,)), ((), ())), preferred_element_type=f32)


def per_expert(kernel, experts, ins, outs, flops, name, scalars=()):
    whole = lambda shape: pl.BlockSpec((1,) + tuple(shape[1:]), lambda e: (e, 0, 0))
    in_specs = [pl.BlockSpec(memory_space=pltpu.SMEM)] * len(scalars)
    moved = 0
    for array, block in ins:
        in_specs.append(pl.BlockSpec((1,) + block, lambda e: (e, 0, 0)))
        moved += experts * math.prod(block) * array.dtype.itemsize
    moved += sum(math.prod(o.shape) * o.dtype.itemsize for o in outs)
    return pl.pallas_call(
        kernel,
        grid=(experts,),
        in_specs=in_specs,
        out_specs=[whole(o.shape) for o in outs],
        out_shape=list(outs),
        compiler_params=pltpu.CompilerParams(vmem_limit_bytes=48 << 20),
        cost_estimate=pl.CostEstimate(flops=flops, bytes_accessed=moved, transcendentals=0),
        name=name,
    )(*scalars, *[array for array, _ in ins])


def grad_of_hidden(cot_rows, down_weight):
    experts, rows, width = cot_rows.shape
    hidden = down_weight.shape[1]

    def kernel(cot_ref, down_ref, out_ref):
        out_ref[0] = dot_last(cot_ref[0], down_ref[0])

    return per_expert(
        kernel,
        experts,
        [(cot_rows, (rows, width)), (down_weight, (hidden, width))],
        [jax.ShapeDtypeStruct((experts, rows, hidden), f32)],
        2 * experts * rows * width * hidden,
        "grad_of_hidden",
    )[0]


def expert_step(x_rows, gate_weight, up_weight, hidden_grad, first_expert):
    experts, rows, wide = x_rows.shape
    width, hidden = gate_weight.shape[1:]

    def kernel(base_ref, x_ref, gate_ref, up_ref, grad_ref, back_ref, act_ref, gate_grad_ref, up_grad_ref):
        mine = base_ref[0] + pl.program_id(0)
        x = x_ref[0, :, :width]
        lane = lax.broadcasted_iota(jnp.int32, (rows, EXTRA), 1)
        probs = x_ref[0, :, width:].astype(f32)
        mix = jnp.sum(
            jnp.where((lane == mine) | (lane == mine + E), probs, 0.0), axis=1, keepdims=True
        )
        gate_act = jnp.dot(x, gate_ref[0], preferred_element_type=f32)
        up_act = jnp.dot(x, up_ref[0], preferred_element_type=f32)
        raw = grad_ref[0]
        sig = jax.nn.sigmoid(gate_act)
        silu = gate_act * sig
        act = silu * up_act
        grad_mix = jnp.sum(act * raw, axis=1, keepdims=True)
        act_ref[0] = (mix * act).astype(bf16)
        weighted = mix * raw
        gate_grad = (weighted * up_act * sig * (1.0 + gate_act * (1.0 - sig))).astype(bf16)
        up_grad = (weighted * silu).astype(bf16)
        gate_grad_ref[0] = gate_grad
        up_grad_ref[0] = up_grad
        back_ref[0, :, :width] = (
            dot_last(gate_grad, gate_ref[0]) + dot_last(up_grad, up_ref[0])
        ).astype(bf16)
        coarse = grad_mix.astype(bf16).astype(f32)
        fine = grad_mix - coarse
        back_ref[0, :, width:] = jnp.where(
            lane == mine, coarse, jnp.where(lane == mine + E, fine, 0.0)
        ).astype(bf16)

    small = jax.ShapeDtypeStruct((experts, rows, hidden), bf16)
    return per_expert(
        kernel,
        experts,
        [
            (x_rows, (rows, wide)),
            (gate_weight, (width, hidden)),
            (up_weight, (width, hidden)),
            (hidden_grad, (rows, hidden)),
        ],
        [jax.ShapeDtypeStruct((experts, rows, wide), bf16), small, small, small],
        8 * experts * rows * width * hidden,
        "expert_step",
        (first_expert,),
    )


def expert_out(act, down_weight):
    experts, rows, hidden = act.shape
    width = down_weight.shape[2]

    def kernel(act_ref, down_ref, out_ref):
        out_ref[0] = jnp.dot(act_ref[0], down_ref[0], preferred_element_type=f32).astype(bf16)

    return per_expert(
        kernel,
        experts,
        [(act, (rows, hidden)), (down_weight, (hidden, width))],
        [jax.ShapeDtypeStruct((experts, rows, width), bf16)],
        2 * experts * rows * width * hidden,
        "expert_out",
    )[0]


def expert_weight_grad(left, right, name):
    experts = left[0].shape[0]
    rows = sum(half.shape[1] for half in left)
    width, columns = min(left[0].shape[2], D), min(right[0].shape[2], D)

    def kernel(a_ref, b_ref, c_ref, d_ref, out_ref):
        out_ref[0] = dot_first(
            jnp.concatenate([a_ref[0], b_ref[0]]), jnp.concatenate([c_ref[0], d_ref[0]])
        )

    return per_expert(
        kernel,
        experts,
        [(half, (half.shape[1], width)) for half in left]
        + [(half, (half.shape[1], columns)) for half in right],
        [jax.ShapeDtypeStruct((experts, width, columns), f32)],
        2 * experts * rows * width * columns,
        name,
    )[0]


def kernel_call(kernel, name, scalars, ins, outs, flops, scratch=()):
    moved = sum(a.size * a.dtype.itemsize for a in ins)
    moved += sum(math.prod(o.shape) * o.dtype.itemsize for o in outs)
    return pl.pallas_call(
        kernel,
        in_specs=[pl.BlockSpec(memory_space=pltpu.SMEM)] * len(scalars)
        + [pl.BlockSpec(memory_space=pltpu.VMEM)] * len(ins),
        out_specs=[pl.BlockSpec(memory_space=pltpu.VMEM)] * len(outs),
        out_shape=list(outs),
        scratch_shapes=list(scratch),
        compiler_params=pltpu.CompilerParams(vmem_limit_bytes=48 << 20),
        cost_estimate=pl.CostEstimate(flops=flops, bytes_accessed=moved, transcendentals=0),
        name=name,
    )(*scalars, *ins)


def shape_of(shape, dtype):
    return jax.ShapeDtypeStruct(shape, dtype)


def project(x_slabs, pieces, places, dtype, other=None):
    _, tokens, _ = x_slabs.shape
    columns = pieces[0].shape[1]

    def kernel(place_ref, x_ref, *refs):
        out_ref = refs[len(pieces) + (other is not None)]
        total = None
        for i in range(len(pieces)):
            part = jnp.dot(x_ref[place_ref[i]], refs[i][...], preferred_element_type=f32)
            total = part if total is None else total + part
        out_ref[...] = total.astype(dtype)
        if other is not None:
            first = refs[len(pieces)][...]
            lane = lax.broadcasted_iota(jnp.int32, (tokens, 128), 1)
            refs[-1][...] = jnp.where(
                lane < 64,
                jnp.sum(first * first, axis=1, keepdims=True),
                jnp.sum(total * total, axis=1, keepdims=True),
            )

    outs = [shape_of((tokens, columns), dtype)]
    extra = []
    if other is not None:
        outs.append(shape_of((tokens, 128), f32))
        extra = [other]
    return kernel_call(
        kernel, "project", [places], [x_slabs, *pieces, *extra], outs, 2 * x_slabs.size * columns
    )


def turned(values):
    return pltpu.roll(values, HD // 2, 1)


def attend(queries, key_proj, squares, values, gains, tables, bias, pieces, places):
    tokens, columns = queries.shape
    heads = columns // HD
    dp = len(pieces)
    slab = pieces[0].shape[1]
    share = tokens // 4
    lanes = 128 // heads

    def kernel(place_ref, q_ref, k_ref, sq_ref, v_ref, gain_ref, table_ref, bias_ref, *refs):
        weights = refs[:dp]
        q_out, k_out, log_out, att_out = refs[dp : dp + 4]
        parts, scratch = refs[dp + 4 : dp + 8], refs[dp + 8]
        cosine, sine = table_ref[0], table_ref[1]
        bias_value = bias_ref[...]
        lane = lax.broadcasted_iota(jnp.int32, (tokens, 128), 1)
        q_scale = lax.rsqrt(sq_ref[:, 0:1] / D + epsilon)
        k_scale = lax.rsqrt(sq_ref[:, 64:65] / D + epsilon)
        logs = jnp.zeros((tokens, 128), f32)
        for h in range(heads):
            cut = slice(h * HD, (h + 1) * HD)
            q = q_ref[:, cut] * q_scale * gain_ref[0:1, cut]
            k = k_ref[:, cut] * k_scale * gain_ref[1:2, cut]
            q = (q * cosine + turned(q) * sine).astype(bf16)
            k = (k * cosine + turned(k) * sine).astype(bf16)
            q_out[:, cut] = q
            k_out[:, cut] = k
            scores = dot_last(q, k) * (1.0 / math.sqrt(HD)) + bias_value
            largest = jnp.max(scores, axis=1, keepdims=True)
            raised = jnp.exp(scores - largest)
            total = jnp.sum(raised, axis=1, keepdims=True)
            logs = jnp.where(lane // lanes == h, largest + jnp.log(total), logs)
            probs = (raised / total).astype(bf16)
            att_out[:, cut] = jnp.dot(probs, v_ref[:, cut], preferred_element_type=f32).astype(bf16)
        log_out[...] = logs
        attended = att_out[...]
        for i in range(dp):
            scratch[place_ref[i]] = jnp.dot(
                attended, weights[i][...], preferred_element_type=f32
            ).astype(bf16)
        for q, part in enumerate(parts):
            start = pl.multiple_of((place_ref[dp] ^ q) * share, share)
            for i in range(dp):
                part[:, i * slab : (i + 1) * slab] = scratch[i, pl.ds(start, share), :]

    low = shape_of((tokens, columns), bf16)
    return kernel_call(
        kernel,
        "attend",
        [places],
        [queries, key_proj, squares, values, gains, tables, bias, *pieces],
        [low, low, shape_of((tokens, 128), f32), low] + [shape_of((share, slab * dp), bf16)] * 4,
        4 * tokens * tokens * columns + 2 * tokens * columns * slab * dp,
        [pltpu.VMEM((dp, tokens, slab), bf16)],
    )


def route(terms, hidden, gain, router):
    share, width = hidden.shape

    def kernel(a_ref, b_ref, c_ref, hidden_ref, gain_ref, router_ref, middle_ref, x_ref, probs_ref):
        middle = hidden_ref[...] + added(a_ref[...], b_ref[...], c_ref[...])
        middle_ref[...] = middle
        scale = lax.rsqrt(jnp.mean(middle * middle, axis=1, keepdims=True) + epsilon)
        normed = (middle * scale * gain_ref[...]).astype(bf16)
        x_ref[:, :width] = normed
        logits = dot_last(normed, router_ref[...])
        raised = jnp.exp(logits - jnp.max(logits, axis=1, keepdims=True))
        probs = raised / (0.5 * jnp.sum(raised, axis=1, keepdims=True))
        probs_ref[...] = probs
        coarse = probs.astype(bf16).astype(f32)
        lane = lax.broadcasted_iota(jnp.int32, probs.shape, 1)
        x_ref[:, width:] = jnp.where(lane < E, coarse, probs - coarse).astype(bf16)

    return kernel_call(
        kernel,
        "route",
        [],
        [*terms, hidden, gain, router],
        [
            shape_of((share, width), f32),
            shape_of((share, width + EXTRA), bf16),
            shape_of((share, EXTRA), f32),
        ],
        2 * share * width * EXTRA,
    )


def route_back(terms, middle, x_piece, probs, cotangent, gain, router):
    share, width = middle.shape

    def kernel(a_ref, b_ref, middle_ref, x_ref, probs_ref, cot_ref, gain_ref, router_ref, *outs):
        grad_ref, low_ref, router_out, gain_out = outs
        pair = added(a_ref[:, width:], b_ref[:, width:])
        grad_probs = pair + pltpu.roll(pair, E, 1)
        probs = probs_ref[...]
        inner = 0.5 * jnp.sum(probs * grad_probs, axis=1, keepdims=True)
        grad_logits = probs * (grad_probs - inner)
        middle = middle_ref[...]
        scale = lax.rsqrt(jnp.mean(middle * middle, axis=1, keepdims=True) + epsilon)
        lane = lax.broadcasted_iota(jnp.int32, probs.shape, 1)
        once = jnp.where(lane < E, grad_logits, 0.0)
        normed_grad = added(a_ref[:, :width], b_ref[:, :width]) + lax.dot_general(
            once,
            router_ref[...].astype(f32),
            (((1,), (0,)), ((), ())),
            precision=lax.Precision.HIGHEST,
            preferred_element_type=f32,
        )
        router_out[...] = lax.dot_general(
            once,
            x_ref[:, :width].astype(f32),
            (((0,), (0,)), ((), ())),
            precision=lax.Precision.HIGHEST,
            preferred_element_type=f32,
        )
        gain_out[...] = jnp.sum(normed_grad * middle * scale, axis=0, keepdims=True)
        scaled = normed_grad * gain_ref[...]
        grad = (
            cot_ref[...]
            + scale * scaled
            - middle * (scale * scale * scale) * jnp.mean(scaled * middle, axis=1, keepdims=True)
        )
        grad_ref[...] = grad
        low_ref[...] = grad.astype(bf16)

    return kernel_call(
        kernel,
        "route_back",
        [],
        [*terms, middle, x_piece, probs, cotangent, gain, router],
        [
            shape_of((share, width), f32),
            shape_of((share, width), bf16),
            shape_of((EXTRA, width), f32),
            shape_of((1, width), f32),
        ],
        24 * share * width * EXTRA,
    )


def attend_back(low_pieces, pieces, places, q_rot, k_rot, values, logs, queries, key_proj, squares, gains, tables, bias):
    tokens, columns = queries.shape
    heads = columns // HD
    dp = len(pieces)
    slab = pieces[0].shape[1]
    share = tokens // 4
    lanes = 128 // heads

    def kernel(place_ref, *refs):
        lows, weights = refs[:4], refs[4 : 4 + dp]
        qr_ref, kr_ref, v_ref, log_ref, q_ref, k_ref, sq_ref, gain_ref, table_ref, bias_ref = refs[
            4 + dp : 14 + dp
        ]
        gv_ref, gq_ref, gk_ref, inner_ref, gains_ref, scratch = refs[14 + dp :]
        for q, low in enumerate(lows):
            start = pl.multiple_of((place_ref[dp] ^ q) * share, share)
            for i in range(dp):
                scratch[i, pl.ds(start, share), :] = low[:, i * slab : (i + 1) * slab]
        total = None
        for i in range(dp):
            part = dot_last(scratch[place_ref[i]], weights[i][...])
            total = part if total is None else total + part
        grad_att = total.astype(bf16)
        cosine, sine = table_ref[0], table_ref[1]
        bias_value = bias_ref[...]
        q_scale = lax.rsqrt(sq_ref[:, 0:1] / D + epsilon)
        k_scale = lax.rsqrt(sq_ref[:, 64:65] / D + epsilon)
        q_inner = jnp.zeros((tokens, 1), f32)
        k_inner = jnp.zeros((tokens, 1), f32)
        for h in range(heads):
            cut = slice(h * HD, (h + 1) * HD)
            qr, kr, v, grad = qr_ref[:, cut], kr_ref[:, cut], v_ref[:, cut], grad_att[:, cut]
            scores = dot_last(qr, kr) * (1.0 / math.sqrt(HD)) + bias_value
            probs = jnp.exp(scores - log_ref[:, h * lanes : h * lanes + 1])
            gv_ref[:, cut] = dot_first(probs.astype(bf16), grad).astype(bf16)
            grad_probs = dot_last(grad, v)
            dots = jnp.sum(probs * grad_probs, axis=1, keepdims=True)
            grad_scores = (probs * (grad_probs - dots) * (1.0 / math.sqrt(HD))).astype(bf16)
            gq = jnp.dot(grad_scores, kr, preferred_element_type=f32)
            gk = dot_first(grad_scores, qr)
            gq = gq * cosine - turned(gq) * sine
            gk = gk * cosine - turned(gk) * sine
            q, k = q_ref[:, cut], k_ref[:, cut]
            gains_ref[0:1, cut] = jnp.sum(gq * q * q_scale, axis=0, keepdims=True)
            gains_ref[1:2, cut] = jnp.sum(gk * k * k_scale, axis=0, keepdims=True)
            gq = gq * gain_ref[0:1, cut]
            gk = gk * gain_ref[1:2, cut]
            gq_ref[:, cut] = gq
            gk_ref[:, cut] = gk
            q_inner = q_inner + jnp.sum(gq * q, axis=1, keepdims=True)
            k_inner = k_inner + jnp.sum(gk * k, axis=1, keepdims=True)
        lane = lax.broadcasted_iota(jnp.int32, (tokens, 128), 1)
        inner_ref[...] = jnp.where(lane < 64, q_inner, k_inner)

    return kernel_call(
        kernel,
        "attend_back",
        [places],
        [*low_pieces, *pieces, q_rot, k_rot, values, logs, queries, key_proj, squares, gains, tables, bias],
        [
            shape_of((tokens, columns), bf16),
            shape_of((tokens, columns), f32),
            shape_of((tokens, columns), f32),
            shape_of((tokens, 128), f32),
            shape_of((2, columns), f32),
        ],
        10 * tokens * tokens * columns + 2 * tokens * columns * slab * dp,
        [pltpu.VMEM((dp, tokens, slab), bf16)],
    )


def norm_back(gq, gk, queries, key_proj, squares, inner):
    tokens, columns = queries.shape

    def kernel(gq_ref, gk_ref, q_ref, k_ref, sq_ref, inner_ref, q_out, k_out):
        for i, (grad, value, out) in enumerate(((gq_ref, q_ref, q_out), (gk_ref, k_ref, k_out))):
            scale = lax.rsqrt(sq_ref[:, 64 * i : 64 * i + 1] / D + epsilon)
            mean = inner_ref[:, 64 * i : 64 * i + 1] / D
            out[...] = (
                scale * grad[...] - value[...] * (scale * scale * scale) * mean
            ).astype(bf16)

    low = shape_of((tokens, columns), bf16)
    return kernel_call(
        kernel, "norm_back", [], [gq, gk, queries, key_proj, squares, inner], [low, low], 0
    )


def project_back(grads, weights, places):
    tokens, columns = grads[0].shape
    dp = len(weights[0])
    slab = weights[0][0].shape[0]
    share = tokens // 4
    flat = [piece for pieces in weights for piece in pieces]

    def kernel(place_ref, *refs):
        values = [ref[...] for ref in refs[: len(grads)]]
        pieces = refs[len(grads) : len(grads) + len(flat)]
        parts, scratch = refs[len(grads) + len(flat) : -1], refs[-1]
        for i in range(dp):
            total = None
            for j, value in enumerate(values):
                part = dot_last(value, pieces[j * dp + i][...])
                total = part if total is None else total + part
            scratch[place_ref[i]] = total.astype(bf16)
        for q, part in enumerate(parts):
            start = pl.multiple_of((place_ref[dp] ^ q) * share, share)
            for i in range(dp):
                part[:, i * slab : (i + 1) * slab] = scratch[i, pl.ds(start, share), :]

    return kernel_call(
        kernel,
        "project_back",
        [places],
        [*grads, *flat],
        [shape_of((share, slab * dp), bf16)] * 4,
        2 * len(grads) * tokens * columns * slab * dp,
        [pltpu.VMEM((dp, tokens, slab), bf16)],
    )


def hidden_back(terms, hidden, grad_middle, gain):
    share, width = hidden.shape

    def kernel(a_ref, b_ref, c_ref, hidden_ref, grad_ref, gain_ref, out_ref, gain_out):
        normed_grad = added(a_ref[...], b_ref[...], c_ref[...])
        hidden = hidden_ref[...]
        scale = lax.rsqrt(jnp.mean(hidden * hidden, axis=1, keepdims=True) + epsilon)
        gain_out[...] = jnp.sum(normed_grad * hidden * scale, axis=0, keepdims=True)
        scaled = normed_grad * gain_ref[...]
        out_ref[...] = (
            grad_ref[...]
            + scale * scaled
            - hidden * (scale * scale * scale) * jnp.mean(scaled * hidden, axis=1, keepdims=True)
        )

    return kernel_call(
        kernel,
        "hidden_back",
        [],
        [*terms, hidden, grad_middle, gain],
        [shape_of((share, width), f32), shape_of((1, width), f32)],
        0,
    )


def token_product(slabs, whole, places, slab_first):
    sequences, share, slab = slabs[0].shape
    tokens, columns = whole[0].shape

    def kernel(place_ref, *refs):
        parts, wholes, out_ref, scratch = refs[:4], refs[4:-2], refs[-2], refs[-1]
        for q, part in enumerate(parts):
            start = pl.multiple_of((place_ref[sequences] ^ q) * share, share)
            scratch[:, pl.ds(start, share), :] = part[...]
        total = None
        for i in range(sequences):
            pair = (scratch[i], wholes[i][...])
            part = dot_first(*pair) if slab_first else dot_first(*pair[::-1])
            total = part if total is None else total + part
        out_ref[...] = total

    return kernel_call(
        kernel,
        "token_product",
        [places],
        [*slabs, *whole],
        [shape_of((slab, columns) if slab_first else (columns, slab), f32)],
        2 * sequences * tokens * slab * columns,
        [pltpu.VMEM((sequences, tokens, slab), bf16)],
    )[0]


def rope_tables(length, head_size):
    half_size = head_size // 2
    inverse = 10000.0 ** (-2.0 * jnp.arange(half_size, dtype=jnp.float32) / head_size)
    angles = jnp.arange(length, dtype=jnp.float32)[:, None] * inverse[None, :]
    cosine, sine = jnp.cos(angles), jnp.sin(angles)
    return jnp.stack(
        [jnp.concatenate([cosine, cosine], axis=1), jnp.concatenate([-sine, sine], axis=1)]
    )


def score_bias(segments):
    position = jnp.arange(segments.shape[0], dtype=jnp.int32)
    allowed = (position[None, :] <= position[:, None]) & (segments[:, None] == segments[None, :])
    return jnp.where(allowed, 0.0, -1e30).astype(f32)


def slot_tables(expert_ids, local_experts):
    data_size, tensor_size = lax.axis_size("dp"), lax.axis_size("tp")
    ids = jnp.stack(gather_dp(expert_ids.T))
    sequences, top, tokens = ids.shape
    share = tokens // tensor_size
    ids = absolute_tp([ids[:, :, q * share : (q + 1) * share] for q in range(4)], axis=2)
    mine = lax.axis_index("dp") * local_experts + jnp.arange(local_experts, dtype=jnp.int32)
    named = jnp.any(ids[:, None] == mine[None, :, None, None], axis=2)
    position = jnp.arange(tokens, dtype=jnp.int32)
    before = (position[:, None] < position[None, :]).astype(bf16)
    slot = jnp.einsum("set,tu->seu", named.astype(bf16), before, preferred_element_type=f32)
    return jnp.where(named, slot.astype(jnp.int32), -1)


def slabs_of(values):
    dp = lax.axis_size("dp")
    half = dp // 2
    me = lax.axis_index("dp")
    slab = values.shape[1] // dp
    got = []
    for dy in range(2):
        for dz in range(half):
            target = (me // 2 + dz) % half * 2 + (me % 2 ^ dy)
            part = lax.dynamic_slice_in_dim(values, target * slab, slab, 1)
            if dy or dz:
                part = hop(
                    part,
                    lambda a, b, dy=dy, dz=dz: ((a // 2 + dz) % half * 2 + (a % 2 ^ dy), b),
                )
            got.append(part)
    return gather_tp(jnp.stack(got))


def per_device(
    hidden_in,
    cotangent,
    segment_ids,
    expert_ids,
    first_gain,
    query_weight,
    key_weight,
    value_weight,
    output_weight,
    query_gain,
    key_gain,
    second_gain,
    router_weight,
    gate_weight,
    up_weight,
    down_weight,
):
    data_size = lax.axis_size("dp")
    tensor_size = lax.axis_size("tp")
    half = data_size // 2
    seq_len, width = hidden_in.shape
    share = seq_len // tensor_size
    slab = width // data_size
    me_dp, me_tp = lax.axis_index("dp"), lax.axis_index("tp")
    own = lambda values: lax.dynamic_slice_in_dim(values, me_tp * share, share, 0)
    local_experts = E // data_size
    first_expert = (me_dp * local_experts).astype(jnp.int32).reshape(1)
    places = jnp.concatenate([owner(jnp.arange(data_size, dtype=jnp.int32)), me_tp[None]]).astype(
        jnp.int32
    )

    hidden_own, cot_own = own(hidden_in), own(cotangent)
    small = jnp.concatenate(
        [
            router_weight.T.reshape(-1),
            first_gain,
            second_gain,
            query_gain.reshape(-1),
            key_gain.reshape(-1),
        ]
    )
    small = absolute_dp(gather_dp(small))
    cot_pieces = gather_all(cot_own.astype(bf16))
    query_pieces = gather_dp(after(query_weight, cot_pieces[1][0]))
    key_pieces = gather_dp(after(key_weight, query_pieces[1]))
    value_pieces = gather_dp(after(value_weight, key_pieces[1]))
    output_pieces = gather_dp(after(output_weight, value_pieces[1]))
    cut = slab * E
    router = jnp.swapaxes(small[:, :cut].reshape(data_size, E, slab), 0, 1).reshape(E, width)
    router = jnp.concatenate([router, router])
    gain_one = small[:, cut : cut + slab].reshape(1, width).astype(f32)
    gain_two = small[:, cut + slab : cut + 2 * slab].reshape(1, width).astype(f32)
    heads_local = query_gain.shape[0]
    piece = query_gain.size
    cut = cut + 2 * slab
    spread = lambda v: jnp.swapaxes(v.reshape(data_size, heads_local, -1), 0, 1).reshape(-1).astype(f32)
    gains = jnp.stack(
        [spread(small[:, cut : cut + piece]), spread(small[:, cut + piece : cut + 2 * piece])]
    )

    table = slot_tables(expert_ids, local_experts)
    tables = rope_tables(seq_len, HD)
    bias = score_bias(segment_ids[0])

    halves = []
    for pick in (slice(0, half), slice(half, None)):
        cot_rows = rows_of_slots(cot_pieces[pick], table[pick])
        halves.append((pick, cot_rows, grad_of_hidden(cot_rows, down_weight)))

    first_scale = lax.rsqrt(jnp.mean(hidden_in * hidden_in, axis=-1, keepdims=True) + epsilon)
    normed_one = (hidden_in * first_scale * gain_one).astype(bf16)
    x_slabs = jnp.swapaxes(normed_one.reshape(seq_len, data_size, slab), 0, 1)
    (queries,) = project(x_slabs, query_pieces, places, f32)
    key_proj, squares = project(x_slabs, key_pieces, places, f32, queries)
    (values,) = project(x_slabs, value_pieces, places, bf16)
    squares = reduce_tp(squares)
    q_rot, k_rot, logs, attended, *parts = attend(
        queries, key_proj, squares, values, gains, tables, bias, output_pieces, places
    )
    middle, x_piece, probs = route(scatter_tp(parts), hidden_own, gain_two, router)

    x_pieces = gather_all(after(x_piece, halves[0][2], halves[1][2]))
    attended_pieces = gather_dp(after(attended, x_pieces[-1][0]))
    one_slabs = slabs_of(after(own(normed_one), x_pieces[-1][0]))
    near, saved, crossed = [], [], []
    for pick, cot_rows, hidden_grad in halves:
        x_rows = rows_of_slots(x_pieces[pick], table[pick])
        back_rows, act, gate_grad, up_grad = expert_step(
            x_rows, gate_weight, up_weight, hidden_grad, first_expert
        )
        saved.append((x_rows, cot_rows, act, gate_grad, up_grad))
        total, crossing = scatter_near(tokens_of_slots(back_rows, table[pick]))
        near.append(total)
        crossed.append(crossing)
    saved = [list(arrays) for arrays in zip(*saved)]
    outs = [expert_out(after(act, crossed[1]), down_weight) for act in saved[2]]
    sums = [
        tokens_of_slots(rows, table[pick]) for rows, (pick, _, _) in zip(outs, halves, strict=True)
    ]
    back = scatter_line(*near, [outs[:1], outs[1:], sums[0], sums[1]])

    grad_middle, grad_low, router_sum, gain_sum = route_back(
        back, middle, x_piece, probs, cot_own, gain_two, router
    )
    low_pieces = gather_tp(grad_low)
    grad_gate = expert_weight_grad([after(v, grad_low) for v in saved[0]], saved[3], "grad_gate")
    grad_values, gq, gk, inner, gain_sums = attend_back(
        [after(low_pieces[0], grad_gate)] + low_pieces[1:], output_pieces, places, q_rot, k_rot, values, logs, queries,
        key_proj, squares, gains, tables, bias,
    )
    value_grads = gather_dp(grad_values)
    inner = reduce_tp(inner)
    grad_queries, grad_keys = norm_back(gq, gk, queries, key_proj, squares, inner)
    query_grads = gather_dp(after(grad_queries, value_grads[1]))
    key_grads = gather_dp(after(grad_keys, query_grads[1]))
    parts = project_back(
        [grad_queries, grad_keys, grad_values], [query_pieces, key_pieces, value_pieces], places
    )
    grad_hidden, first_sum = hidden_back(scatter_tp(parts), hidden_own, grad_middle, gain_one)
    grad_hidden = absolute_tp(gather_tp(grad_hidden))

    moe_near = [scatter_near(part, (inner,))[0] for part in sums]
    moe = scatter_line(*moe_near)
    hidden_out = absolute_tp(gather_tp(middle + added(*moe)))
    token_sums = jnp.concatenate([router_sum[:E], gain_sum, first_sum])
    token_sums = reduce_tp(reduce_dp(token_sums))
    middle_slabs = slabs_of(after(grad_low, inner))
    head_sums = reduce_dp(gain_sums.reshape(2 * heads_local, HD))
    grad_up = expert_weight_grad([after(v, parts[0]) for v in saved[0]], saved[4], "grad_up")
    grad_down = expert_weight_grad([after(v, parts[0]) for v in saved[2]], saved[1], "grad_down")
    grad_output = token_product(middle_slabs, attended_pieces, places, False)
    grad_value = token_product(one_slabs, value_grads, places, True)
    grad_query = token_product(one_slabs, query_grads, places, True)
    grad_key = token_product(one_slabs, key_grads, places, True)
    return (
        hidden_out,
        grad_hidden,
        token_sums[E + 1],
        grad_query,
        grad_key,
        grad_value,
        grad_output,
        head_sums[:heads_local],
        head_sums[heads_local:],
        token_sums[E],
        token_sums[:E].T,
        grad_gate,
        grad_up,
        grad_down,
    )


def solution(mesh):
    return jax.shard_map(
        per_device,
        mesh=mesh,
        in_specs=(
            P("dp", None),
            P("dp", None),
            P("dp", None),
            P("dp", None),
            P("dp"),
            P("dp", "tp"),
            P("dp", "tp"),
            P("dp", "tp"),
            P("tp", "dp"),
            P("tp", "dp"),
            P("tp", "dp"),
            P("dp"),
            P("dp", None),
            P("dp", None, "tp"),
            P("dp", None, "tp"),
            P("dp", "tp", None),
        ),
        out_specs=(
            P("dp", None),
            P("dp", None),
            P("dp"),
            P("dp", "tp"),
            P("dp", "tp"),
            P("dp", "tp"),
            P("tp", "dp"),
            P("tp", "dp"),
            P("tp", "dp"),
            P("dp"),
            P("dp", None),
            P("dp", None, "tp"),
            P("dp", None, "tp"),
            P("dp", "tp", None),
        ),
        check_vma=False,
    )
```

```python
import math

import jax
import jax.numpy as jnp
from jax import lax
from jax.experimental import pallas as pl
from jax.experimental.pallas import tpu as pltpu
from jax.sharding import PartitionSpec as P

D = 2048
HD = 128
E = 64
TOPK = 8
CAP = 48
EXTRA = 2 * E

bf16 = jnp.bfloat16
f32 = jnp.float32

epsilon = 1e-05


def cost(flops, bytes_accessed, transcendentals):
    return pl.CostEstimate(
        flops=flops // 1000000, bytes_accessed=bytes_accessed // 1000000, transcendentals=0
    )


def swap(values, dp_bits, tp_bits):
    dp, tp = lax.axis_size("dp"), lax.axis_size("tp")
    pairs = [
        (a * tp + b, (a ^ dp_bits) * tp + (b ^ tp_bits)) for a in range(dp) for b in range(tp)
    ]
    return lax.ppermute(values, ("dp", "tp"), pairs)


def over_z(values, bits):
    return swap(values, 2 * bits, 0)


def over_y(values):
    return swap(values, 1, 0)


def over_x(values):
    return swap(values, 0, 2)


def over_core(values):
    return swap(values, 0, 1)


def z_bits():
    half = lax.axis_size("dp") // 2
    return [1 << i for i in range(half.bit_length() - 1)]


def masks_of(bits):
    masks = [0]
    for bit in bits:
        masks = masks + [mask ^ bit for mask in masks]
    return masks


def weight_masks():
    return masks_of([2 * bit for bit in z_bits()] + [1])


def token_masks():
    return masks_of([2 * bit for bit in z_bits()[:-1]] + [1, 2 * z_bits()[-1]])


def owners(masks):
    return lax.axis_index("dp") ^ jnp.array(masks, jnp.int32)


def gather_line(pieces, bits):
    for bit in bits:
        pieces = pieces + [over_z(v, bit) for v in pieces]
    return pieces


def gather_dp(values):
    line = gather_line([values], z_bits())
    return line + [over_y(v) for v in line]


def gather_all(values):
    line = gather_line([values], z_bits())
    pairs = {}
    for mask, near in zip(masks_of([2 * bit for bit in z_bits()]), line, strict=True):
        if mask & 2 * z_bits()[-1]:
            aside = over_x(near)
            pairs[mask], pairs[mask + 1] = (near, aside), (over_y(near), over_y(aside))
        else:
            across = over_y(near)
            pairs[mask], pairs[mask + 1] = (near, over_x(near)), (across, over_x(across))
    return [
        (pairs[m][0], over_core(pairs[m][0]), pairs[m][1], over_core(pairs[m][1]))
        for m in token_masks()
    ]


def gather_tp(values):
    other = over_x(values)
    return [values, over_core(values), other, over_core(other)]


def sorted_by_bits(pieces, me):
    bit = 1
    while bit < len(pieces):
        odd = me & bit != 0
        pieces = [jnp.where(odd, pieces[i ^ bit], pieces[i]) for i in range(len(pieces))]
        bit *= 2
    return pieces


def absolute_dp(pieces):
    dp = len(pieces)
    by_mask = [pieces[i // 2 + i % 2 * (dp // 2)] for i in range(dp)]
    return jnp.stack(sorted_by_bits(by_mask, lax.axis_index("dp")))


def absolute_tp(pieces, axis=0):
    return jnp.concatenate(sorted_by_bits(list(pieces), lax.axis_index("tp")), axis=axis)


def added(*terms):
    total = terms[0].astype(f32)
    for term in terms[1:]:
        total = total + term.astype(f32)
    return total


def combined(terms, cut, waits=(), sent=bf16):
    shape = terms[0].shape
    outs = [shape_of((shape[0] - cut,) + shape[1:], sent)]
    if cut:
        outs.insert(0, shape_of((cut,) + shape[1:], f32))

    def kernel(*refs):
        for out, part in zip(refs[len(terms) :], (slice(0, cut), slice(cut, None))[-len(outs) :]):
            out[...] = added(*[ref[part] for ref in refs[: len(terms)]]).astype(out.dtype)

    result = kernel_call(kernel, "combined", [], list(terms), outs, 0, waits=waits)
    return result if cut else result[0]


def held(arrays, dtype, waits):
    def kernel(*refs):
        at = 0
        for ref in refs[:-1]:
            refs[-1][at : at + ref.shape[0], :] = ref[...].astype(dtype)
            at += ref.shape[0]

    rows = sum(array.shape[0] for array in arrays)
    out = shape_of((rows, arrays[0].shape[1]), dtype)
    return kernel_call(kernel, "held", [], list(arrays), [out], 0, waits=waits)[0]


def scatter_tp(parts):
    mine, far = over_core(parts[1]), over_core(parts[3])
    crossing = combined([parts[2], far], 0)
    return (parts[0], mine, over_x(crossing)), crossing


class TokenSums:
    def __init__(self, first, second):
        self.mid = first[0].shape[0] // 2
        self.first, self.second = first, second
        self.first_core = [over_core(first[1]), over_core(first[3])]
        self.second_core = [over_core(second[1]), over_core(second[3])]

    def start(self, *others):
        first, second = self.first, self.second
        self.b0, b0_far = combined([second[0], self.second_core[0]], self.mid, others)
        self.b1, b1_far = combined([second[2], self.second_core[1]], self.mid, others)
        a1 = combined([first[2], self.first_core[1]], 0, others)
        self.sent = [b0_far, b1_far, a1]
        self.came = [over_y(b0_far), over_y(b1_far), over_x(a1)]
        return self

    def turn(self, *others):
        b = combined([self.b1, self.came[1]], 0, others)
        self.a, a = combined([self.first[0], self.first_core[0], self.came[2]], self.mid, others)
        self.sent = [b, a]
        self.turned = [over_x(b), over_y(a)]
        return self

    def top(self, *others):
        self.sent = [combined([self.b0, self.came[0], self.turned[0]], 0, others)]
        self.from_top = over_z(self.sent[0], z_bits()[-1])
        return self

    def last(self, *others):
        terms = [self.a, self.turned[1], self.from_top]
        for bit in reversed(z_bits()[:-1]):
            near, sent = combined(terms, terms[0].shape[0] // 2, others if bit == 1 else ())
            terms = [near, over_z(sent, bit)]
        self.sent = [sent]
        return terms


def reduce_all(near, far):
    terms = [near, over_y(far)]
    for bit in reversed(z_bits()):
        near, sent = combined(terms, bit, sent=f32)
        terms = [near, over_z(sent, bit)]
    return reduce_tp(added(*terms)[0])


def reduce_tp(values):
    values = values + over_core(values)
    return values + over_x(values)


def reduce_heads(values):
    return reduce_tp(values + over_z(values, 1))


class WeightSums:
    def __init__(self, near, far):
        self.near, self.sent = near, far
        self.came = over_y(far)

    def along_z(self, *others):
        for bit in reversed(z_bits()[1:]):
            self.near, self.sent = combined([self.near, self.came], bit, others)
            self.came = over_z(self.sent, bit)
        return self

    def to_mate(self, *others):
        self.near, self.sent = combined([self.near, self.came], 1, others)
        self.came = over_z(self.sent, 1)
        return self

    def in_order(self, here, count, *others):
        _, rows, columns = self.near.shape
        size = columns // count if count else rows
        shape = (rows, 2 * size) if count else (2 * rows, columns)

        def kernel(here_ref, mine_ref, other_ref, *outs):
            for ref, which in ((mine_ref, here_ref[1]), (other_ref, 1 - here_ref[1])):
                part = pl.ds(pl.multiple_of(which * size, size), size)
                for j, out in enumerate(outs):
                    if count:
                        out[:, part] = ref[0, :, j * size : (j + 1) * size].astype(f32)
                    else:
                        out[part, :] = ref[0].astype(f32)

        return kernel_call(
            kernel,
            "in_order",
            [here],
            [self.near, self.came],
            [shape_of(shape, f32)] * max(count, 1),
            0,
            waits=others,
        )


def chosen_slots(table):
    experts, tokens = table.shape
    place = lax.broadcasted_iota(jnp.int32, (experts, CAP, tokens), 1)
    hit = place == table[:, None, :]
    return jnp.where(hit, 1.0, 0.0).astype(bf16).reshape(experts * CAP, tokens)


def rows_of_slots(pieces, table, waits, order=None):
    sequences, experts, tokens = table.shape
    if order is None:
        flat = [piece for group in pieces for piece in group]
        share, width = flat[0].shape
    else:
        flat = pieces
        share, width = tokens // 4, pieces[0].shape[1]
    count = sequences * 4

    def kernel(*refs):
        table_ref, *sources = refs[:-3]
        out_ref, buffer, arrived = refs[-3:]
        step = pl.program_id(0)

        def piece(i):
            if order is None:
                return sources[i]
            return sources[i % 4].at[pl.ds(order[i // 4] * share, share), :]

        @pl.when(step == 0)
        def _():
            for i in range(count):
                pltpu.make_async_copy(
                    piece(i), buffer.at[i // 4, pl.ds(i % 4 * share, share)], arrived.at[i]
                ).start()

        for i in range(4):
            pltpu.make_async_copy(
                piece(i), buffer.at[step, pl.ds(i * share, share)], arrived.at[step * 4 + i]
            ).wait()
        picked = jnp.dot(chosen_slots(table_ref[0]), buffer[step], preferred_element_type=f32)
        out_ref[...] = picked.astype(bf16).reshape(experts, CAP, width)

    return pl.pallas_call(
        without(kernel, 1 + len(flat), len(waits)),
        grid=(sequences,),
        in_specs=[pl.BlockSpec((1, experts, tokens), lambda s: (s, 0, 0))]
        + [pl.BlockSpec(memory_space=pl.ANY)] * (len(flat) + len(waits)),
        out_specs=pl.BlockSpec((experts, CAP, width), lambda s: (0, s, 0)),
        out_shape=jax.ShapeDtypeStruct((experts, sequences * CAP, width), bf16),
        scratch_shapes=[
            pltpu.VMEM((sequences, tokens, width), bf16),
            pltpu.SemaphoreType.DMA((count,)),
        ],
        compiler_params=pltpu.CompilerParams(vmem_limit_bytes=48 << 20),
        cost_estimate=cost(
            flops=2 * experts * CAP * sequences * tokens * width,
            bytes_accessed=2 * sequences * (tokens + experts * CAP) * width,
            transcendentals=0,
        ),
        name="rows_of_slots",
    )(table, *flat, *waits)


def tokens_of_slots(rows, table, first, waits):
    sequences, experts, tokens = table.shape
    width = rows.shape[-1]
    share = tokens // 4

    def kernel(table_ref, rows_ref, *outs):
        picked = chosen_slots(table_ref[0])
        total = lax.dot_general(
            picked,
            rows_ref[...].reshape(experts * CAP, width),
            (((0,), (0,)), ((), ())),
            preferred_element_type=f32,
        ).astype(bf16)
        for q, out in enumerate(outs):
            out[...] = total[q * share : (q + 1) * share]

    return pl.pallas_call(
        without(kernel, 2, len(waits)),
        grid=(sequences,),
        in_specs=[
            pl.BlockSpec((1, experts, tokens), lambda s: (s, 0, 0)),
            pl.BlockSpec((experts, CAP, width), lambda s: (0, s + first, 0)),
        ]
        + [pl.BlockSpec(memory_space=pl.ANY)] * len(waits),
        out_specs=[pl.BlockSpec((share, width), lambda s: (s, 0))] * 4,
        out_shape=[jax.ShapeDtypeStruct((sequences * share, width), bf16)] * 4,
        compiler_params=pltpu.CompilerParams(vmem_limit_bytes=48 << 20),
        cost_estimate=cost(
            flops=2 * experts * CAP * sequences * tokens * width,
            bytes_accessed=2 * sequences * (tokens + experts * CAP) * width,
            transcendentals=0,
        ),
        name="tokens_of_slots",
    )(table, rows, *waits)


def dot_last(a, b):
    return lax.dot_general(a, b, (((1,), (1,)), ((), ())), preferred_element_type=f32)


def dot_first(a, b):
    return lax.dot_general(a, b, (((0,), (0,)), ((), ())), preferred_element_type=f32)


def per_expert(kernel, experts, ins, outs, flops, name, scalars=(), waits=()):
    whole = lambda shape: pl.BlockSpec((1,) + tuple(shape[1:]), lambda e: (e, 0, 0))
    in_specs = [pl.BlockSpec(memory_space=pltpu.SMEM)] * len(scalars)
    moved = 0
    for array, block in ins:
        in_specs.append(pl.BlockSpec((1,) + block, lambda e: (e, 0, 0)))
        moved += experts * math.prod(block) * array.dtype.itemsize
    moved += sum(math.prod(o.shape) * o.dtype.itemsize for o in outs)
    return pl.pallas_call(
        without(kernel, len(in_specs), len(waits)),
        grid=(experts,),
        in_specs=in_specs + [pl.BlockSpec(memory_space=pl.ANY)] * len(waits),
        out_specs=[whole(o.shape) for o in outs],
        out_shape=list(outs),
        compiler_params=pltpu.CompilerParams(vmem_limit_bytes=48 << 20),
        cost_estimate=cost(flops=flops, bytes_accessed=moved, transcendentals=0),
        name=name,
    )(*scalars, *[array for array, _ in ins], *waits)


def grad_of_hidden(cot_rows, down_weight):
    experts, rows, width = cot_rows.shape
    hidden = down_weight.shape[1]

    def kernel(cot_ref, down_ref, out_ref):
        out_ref[0] = dot_last(cot_ref[0], down_ref[0])

    return per_expert(
        kernel,
        experts,
        [(cot_rows, (rows, width)), (down_weight, (hidden, width))],
        [jax.ShapeDtypeStruct((experts, rows, hidden), f32)],
        2 * experts * rows * width * hidden,
        "grad_of_hidden",
    )[0]


def expert_step(x_halves, gate_weight, up_weight, hidden_grad, first_expert):
    experts, half_rows, wide = x_halves[0].shape
    rows = half_rows * 2
    width, hidden = gate_weight.shape[1:]

    def kernel(base_ref, a_ref, b_ref, gate_ref, up_ref, grad_ref, back_ref, act_ref, gate_grad_ref, up_grad_ref):
        mine = base_ref[0] + pl.program_id(0)
        x = jnp.concatenate([a_ref[0, :, :width], b_ref[0, :, :width]])
        lane = lax.broadcasted_iota(jnp.int32, (rows, EXTRA), 1)
        probs = jnp.concatenate([a_ref[0, :, width:], b_ref[0, :, width:]]).astype(f32)
        mix = jnp.sum(
            jnp.where((lane == mine) | (lane == mine + E), probs, 0.0), axis=1, keepdims=True
        )
        gate_act = jnp.dot(x, gate_ref[0], preferred_element_type=f32)
        up_act = jnp.dot(x, up_ref[0], preferred_element_type=f32)
        raw = grad_ref[0]
        sig = jax.nn.sigmoid(gate_act)
        silu = gate_act * sig
        act = silu * up_act
        grad_mix = jnp.sum(act * raw, axis=1, keepdims=True)
        act_ref[0] = (mix * act).astype(bf16)
        weighted = mix * raw
        gate_grad = (weighted * up_act * sig * (1.0 + gate_act * (1.0 - sig))).astype(bf16)
        up_grad = (weighted * silu).astype(bf16)
        gate_grad_ref[0] = gate_grad
        up_grad_ref[0] = up_grad
        back_ref[0, :, :width] = (
            dot_last(gate_grad, gate_ref[0]) + dot_last(up_grad, up_ref[0])
        ).astype(bf16)
        coarse = grad_mix.astype(bf16).astype(f32)
        fine = grad_mix - coarse
        back_ref[0, :, width:] = jnp.where(
            lane == mine, coarse, jnp.where(lane == mine + E, fine, 0.0)
        ).astype(bf16)

    small = jax.ShapeDtypeStruct((experts, rows, hidden), bf16)
    return per_expert(
        kernel,
        experts,
        [
            (x_halves[0], (half_rows, wide)),
            (x_halves[1], (half_rows, wide)),
            (gate_weight, (width, hidden)),
            (up_weight, (width, hidden)),
            (hidden_grad, (rows, hidden)),
        ],
        [jax.ShapeDtypeStruct((experts, rows, wide), bf16), small, small, small],
        8 * experts * rows * width * hidden,
        "expert_step",
        (first_expert,),
    )


def expert_out(act, down_weight, waits):
    experts, rows, hidden = act.shape
    width = down_weight.shape[2]

    def kernel(act_ref, down_ref, out_ref):
        out_ref[0] = jnp.dot(act_ref[0], down_ref[0], preferred_element_type=f32).astype(bf16)

    return per_expert(
        kernel,
        experts,
        [(act, (rows, hidden)), (down_weight, (hidden, width))],
        [jax.ShapeDtypeStruct((experts, rows, width), bf16)],
        2 * experts * rows * width * hidden,
        "expert_out",
        waits=waits,
    )[0]


def expert_weight_grads(x_halves, cot_rows, act, gate_grad, up_grad, first, count, into, waits):
    experts, rows, hidden = act.shape
    width = cot_rows.shape[2]

    def kernel(a_ref, b_ref, cot_ref, act_ref, gate_ref, up_ref, *refs):
        gate_out, up_out, down_out, mark = refs[-4:]
        mark[...] = jnp.zeros_like(mark)
        x = jnp.concatenate([a_ref[0], b_ref[0]])
        gate_out[0] = dot_first(x, gate_ref[0])
        up_out[0] = dot_first(x, up_ref[0])
        down_out[0] = dot_first(act_ref[0], cot_ref[0])

    block = lambda *shape: pl.BlockSpec((1,) + shape, lambda e: (e + first, 0, 0))
    ins = [*x_halves, cot_rows, act, gate_grad, up_grad]
    return pl.pallas_call(
        kernel,
        grid=(count,),
        in_specs=[block(rows // 2, width)] * 2
        + [block(rows, width)]
        + [block(rows, hidden)] * 3
        + [pl.BlockSpec(memory_space=pl.ANY)] * (len(into) + len(waits)),
        out_specs=[block(width, hidden), block(width, hidden), block(hidden, width)]
        + [pl.BlockSpec((8, 128), lambda e: (0, 0))],
        out_shape=[
            jax.ShapeDtypeStruct((experts, width, hidden), f32),
            jax.ShapeDtypeStruct((experts, width, hidden), f32),
            jax.ShapeDtypeStruct((experts, hidden, width), f32),
            jax.ShapeDtypeStruct((8, 128), f32),
        ],
        input_output_aliases={len(ins) + i: i for i in range(len(into))},
        compiler_params=pltpu.CompilerParams(vmem_limit_bytes=48 << 20),
        cost_estimate=cost(
            flops=6 * count * rows * width * hidden,
            bytes_accessed=count * (4 * rows * (width + hidden) + 12 * width * hidden),
            transcendentals=0,
        ),
        name="expert_weight_grads",
    )(*ins, *into, *waits)


def without(kernel, start, count):
    return lambda *refs: kernel(*refs[:start], *refs[start + count :])


def kernel_call(kernel, name, scalars, ins, outs, flops, scratch=(), waits=()):
    moved = sum(a.size * a.dtype.itemsize for a in ins)
    moved += sum(math.prod(o.shape) * o.dtype.itemsize for o in outs)
    large = [i for i, a in enumerate(ins) if a.size * a.dtype.itemsize >= 1 << 16]
    first, last = len(scalars), len(scalars) + len(ins)
    made = last + len(waits)

    def body(*refs):
        given = list(refs[first:last])
        kept = made + len(outs) + len(scratch)
        copies = []
        for k, i in enumerate(large):
            copies.append(pltpu.make_async_copy(given[i], refs[kept + k], refs[-1].at[k]))
            copies[-1].start()
            given[i] = refs[kept + k]
        for copy in copies:
            copy.wait()
        kernel(*refs[:first], *given, *refs[made:kept])

    places = [pl.ANY if i in large else pltpu.VMEM for i in range(len(ins))]
    return pl.pallas_call(
        body,
        in_specs=[pl.BlockSpec(memory_space=pltpu.SMEM)] * len(scalars)
        + [pl.BlockSpec(memory_space=place) for place in places]
        + [pl.BlockSpec(memory_space=pl.ANY)] * len(waits),
        out_specs=[pl.BlockSpec(memory_space=pltpu.VMEM)] * len(outs),
        out_shape=list(outs),
        scratch_shapes=list(scratch)
        + [pltpu.VMEM(ins[i].shape, ins[i].dtype) for i in large]
        + [pltpu.SemaphoreType.DMA((max(len(large), 1),))],
        compiler_params=pltpu.CompilerParams(vmem_limit_bytes=40 << 20),
        cost_estimate=cost(flops=flops, bytes_accessed=moved, transcendentals=0),
        name=name,
    )(*scalars, *ins, *waits)


def shape_of(shape, dtype):
    return jax.ShapeDtypeStruct(shape, dtype)


def row_of(place_ref, dp, tokens, share, q, mate):
    which = (1 - place_ref[dp + 1]) if mate else place_ref[dp + 1]
    return pl.multiple_of(which * tokens + (place_ref[dp] ^ q) * share, share)


def split_heads(weights, here):
    rows, columns = weights[0].shape
    half = columns // 2

    def kernel(here_ref, *refs):
        keep_ref, give_ref, scratch = refs[len(weights) :]
        for j, ref in enumerate(refs[: len(weights)]):
            for i in range(2):
                scratch[i, :, j * half : (j + 1) * half] = ref[:, i * half : (i + 1) * half]
        keep_ref[...] = scratch[here_ref[1]]
        give_ref[...] = scratch[1 - here_ref[1]]

    shape = (rows, half * len(weights))
    return kernel_call(
        kernel,
        "split_heads",
        [here],
        list(weights),
        [shape_of(shape, bf16)] * 2,
        0,
        [pltpu.VMEM((2,) + shape, bf16)],
    )


def paired(own, mates, places, dp):
    share, width = mates[0].shape
    if len(mates) == 1:
        share = share // 4
    tokens = 4 * share
    slab = width // dp

    def kernel(place_ref, *refs):
        out_ref = refs[-1]
        if len(own) == 1:
            start = pl.multiple_of(place_ref[dp + 1] * tokens, tokens)
            for i in range(dp):
                out_ref[i, pl.ds(start, tokens), :] = refs[0][:, i * slab : (i + 1) * slab]
        for q in range(4):
            sources = []
            if len(own) == 4:
                sources.append((refs[q][...], False))
            if len(mates) == 4:
                sources.append((refs[len(own) + q][...], True))
            else:
                sources.append((refs[len(own)][q * share : (q + 1) * share, :], True))
            for rows, mate in sources:
                start = row_of(place_ref, dp, tokens, share, q, mate)
                for i in range(dp):
                    out_ref[i, pl.ds(start, share), :] = rows[:, i * slab : (i + 1) * slab]

    return kernel_call(
        kernel, "paired", [places], [*own, *mates], [shape_of((dp, 2 * tokens, slab), bf16)], 0
    )[0]


def as_rows(first, second):
    lane = lax.broadcasted_iota(jnp.int32, (first.shape[0], 128), 1)
    return jnp.where(lane < 4, first, second).T[:8]


def as_columns(pair):
    wide = jnp.concatenate([pair] * 16).T
    return wide[:, 0:1], wide[:, 4:5]


def project(x_slabs, pieces, places):
    dp, tokens, _ = x_slabs.shape
    columns = pieces[0].shape[1] // 3

    def kernel(place_ref, x_ref, *refs):
        totals = []
        for j in range(3):
            total = None
            for i in range(dp):
                part = jnp.dot(
                    x_ref[place_ref[i]],
                    refs[i][:, j * columns : (j + 1) * columns],
                    preferred_element_type=f32,
                )
                total = part if total is None else total + part
            totals.append(total)
        queries, keys, values = totals
        qk_out, v_out, squares_out = refs[dp:]
        qk_out[0] = queries
        qk_out[1] = keys
        v_out[...] = values.astype(bf16)
        squares_out[...] = as_rows(
            jnp.sum(queries * queries, axis=1, keepdims=True),
            jnp.sum(keys * keys, axis=1, keepdims=True),
        )

    return kernel_call(
        kernel,
        "project",
        [places],
        [x_slabs, *pieces],
        [
            shape_of((2, tokens, columns), f32),
            shape_of((tokens, columns), bf16),
            shape_of((8, tokens), f32),
        ],
        6 * x_slabs.size * columns,
    )


def turned(values):
    return pltpu.roll(values, HD // 2, 1)


def attend(projected, squares, values, gains, tables, bias, places, dp, waits=()):
    _, rows, columns = projected.shape
    tokens = rows // 2
    heads = columns // HD
    lanes = 128 // heads

    def kernel(place_ref, qk_ref, sq_ref, v_ref, gain_ref, table_ref, bias_ref, *refs):
        turned_out, log_out, att_out, keep_out, give_out = refs
        turned_out[2] = v_ref[...]
        cosine, sine = table_ref[0], table_ref[1]
        lane = lax.broadcasted_iota(jnp.int32, (tokens, 128), 1)
        q_squares, k_squares = as_columns(sq_ref[...])
        for which in range(2):
            row = slice(which * tokens, (which + 1) * tokens)
            q_scale = lax.rsqrt(q_squares[row] / D + epsilon)
            k_scale = lax.rsqrt(k_squares[row] / D + epsilon)
            logs = jnp.zeros((tokens, 128), f32)
            for h in range(heads):
                cut = slice(h * HD, (h + 1) * HD)
                q = qk_ref[0, row, cut] * q_scale * gain_ref[0:1, cut]
                k = qk_ref[1, row, cut] * k_scale * gain_ref[1:2, cut]
                q = (q * cosine + turned(q) * sine).astype(bf16)
                k = (k * cosine + turned(k) * sine).astype(bf16)
                turned_out[0, row, cut] = q
                turned_out[1, row, cut] = k
                scores = dot_last(q, k) * (1.0 / math.sqrt(HD)) + bias_ref[which]
                largest = jnp.max(scores, axis=1, keepdims=True)
                raised = jnp.exp(scores - largest)
                total = jnp.sum(raised, axis=1, keepdims=True)
                logs = jnp.where(lane // lanes == h, largest + jnp.log(total), logs)
                probs = (raised / total).astype(bf16)
                att_out[row, cut] = jnp.dot(
                    probs, v_ref[row, cut], preferred_element_type=f32
                ).astype(bf16)
            log_out[row, :] = logs
        upper = place_ref[dp + 1]
        keep_out[...] = att_out[pl.ds(pl.multiple_of(upper * tokens, tokens), tokens), :]
        give_out[...] = att_out[pl.ds(pl.multiple_of((1 - upper) * tokens, tokens), tokens), :]

    part = shape_of((tokens, columns), bf16)
    return kernel_call(
        kernel,
        "attend",
        [places],
        [projected, squares, values, gains, tables, bias],
        [
            shape_of((3, rows, columns), bf16),
            shape_of((rows, 128), f32),
            shape_of((rows, columns), bf16),
            part,
            part,
        ],
        4 * tokens * rows * columns,
        waits=waits,
    )


def output_project(keep, got, pieces, places, waits=()):
    tokens, columns = keep.shape
    dp = len(pieces)
    slab = pieces[0].shape[1]
    share = tokens // 4

    def kernel(place_ref, keep_ref, got_ref, *refs):
        weights, parts, scratch = refs[:dp], refs[dp:-1], refs[-1]
        upper = place_ref[dp + 1]
        mine = pl.ds(pl.multiple_of(upper * columns, columns), columns)
        other = pl.ds(pl.multiple_of((1 - upper) * columns, columns), columns)
        for i in range(dp):
            scratch[place_ref[i]] = (
                jnp.dot(keep_ref[...], weights[i][mine, :], preferred_element_type=f32)
                + jnp.dot(got_ref[...], weights[i][other, :], preferred_element_type=f32)
            ).astype(bf16)
        for q, part in enumerate(parts):
            start = pl.multiple_of((place_ref[dp] ^ q) * share, share)
            for i in range(dp):
                part[:, i * slab : (i + 1) * slab] = scratch[i, pl.ds(start, share), :]

    return kernel_call(
        kernel,
        "output_project",
        [places],
        [keep, got, *pieces],
        [shape_of((share, slab * dp), bf16)] * 4,
        4 * tokens * columns * slab * dp,
        [pltpu.VMEM((dp, tokens, slab), bf16)],
        waits=waits,
    )


def route(terms, hidden, gain, router, waits=()):
    share, width = hidden.shape

    def kernel(a_ref, b_ref, c_ref, hidden_ref, gain_ref, router_ref, middle_ref, x_ref, probs_ref):
        middle = hidden_ref[...] + added(a_ref[...], b_ref[...], c_ref[...])
        middle_ref[...] = middle
        scale = lax.rsqrt(jnp.mean(middle * middle, axis=1, keepdims=True) + epsilon)
        normed = (middle * scale * gain_ref[...]).astype(bf16)
        x_ref[:, :width] = normed
        logits = dot_last(normed, router_ref[...])
        raised = jnp.exp(logits - jnp.max(logits, axis=1, keepdims=True))
        probs = raised / (0.5 * jnp.sum(raised, axis=1, keepdims=True))
        probs_ref[...] = probs
        coarse = probs.astype(bf16).astype(f32)
        lane = lax.broadcasted_iota(jnp.int32, probs.shape, 1)
        x_ref[:, width:] = jnp.where(lane < E, coarse, probs - coarse).astype(bf16)

    return kernel_call(
        kernel,
        "route",
        [],
        [*terms, hidden, gain, router],
        [
            shape_of((share, width), f32),
            shape_of((share, width + EXTRA), bf16),
            shape_of((share, EXTRA), f32),
        ],
        2 * share * width * EXTRA,
        waits=waits,
    )


def route_back(terms, middle, x_piece, probs, cotangent, gain, router, waits=()):
    share, width = middle.shape

    def kernel(a_ref, b_ref, middle_ref, x_ref, probs_ref, cot_ref, gain_ref, router_ref, *outs):
        grad_ref, low_ref, router_out, gain_out = outs
        pair = added(a_ref[:, width:], b_ref[:, width:])
        grad_probs = pair + pltpu.roll(pair, E, 1)
        probs = probs_ref[...]
        inner = 0.5 * jnp.sum(probs * grad_probs, axis=1, keepdims=True)
        grad_logits = probs * (grad_probs - inner)
        middle = middle_ref[...]
        scale = lax.rsqrt(jnp.mean(middle * middle, axis=1, keepdims=True) + epsilon)
        lane = lax.broadcasted_iota(jnp.int32, probs.shape, 1)
        once = jnp.where(lane < E, grad_logits, 0.0)
        normed_grad = added(a_ref[:, :width], b_ref[:, :width]) + lax.dot_general(
            once,
            router_ref[...].astype(f32),
            (((1,), (0,)), ((), ())),
            precision=lax.Precision.HIGHEST,
            preferred_element_type=f32,
        )
        router_out[...] = lax.dot_general(
            once,
            x_ref[:, :width].astype(f32),
            (((0,), (0,)), ((), ())),
            precision=lax.Precision.HIGHEST,
            preferred_element_type=f32,
        )
        gain_out[...] = jnp.sum(normed_grad * middle * scale, axis=0, keepdims=True)
        scaled = normed_grad * gain_ref[...]
        grad = (
            cot_ref[...]
            + scale * scaled
            - middle * (scale * scale * scale) * jnp.mean(scaled * middle, axis=1, keepdims=True)
        )
        grad_ref[...] = grad
        low_ref[...] = grad.astype(bf16)

    return kernel_call(
        kernel,
        "route_back",
        [],
        [*terms, middle, x_piece, probs, cotangent, gain, router],
        [
            shape_of((share, width), f32),
            shape_of((share, width), bf16),
            shape_of((EXTRA, width), f32),
            shape_of((1, width), f32),
        ],
        24 * share * width * EXTRA,
        waits=waits,
    )


def output_back(low_pieces, pieces, places, waits):
    dp = len(pieces)
    columns, slab = pieces[0].shape
    share = low_pieces[0].shape[0]
    tokens = 4 * share
    half = columns // 2

    def kernel(place_ref, *refs):
        lows, weights, (keep_ref, give_ref, scratch, both) = refs[:4], refs[4 : 4 + dp], refs[4 + dp :]
        for q, low in enumerate(lows):
            start = pl.multiple_of((place_ref[dp] ^ q) * share, share)
            for i in range(dp):
                scratch[i, pl.ds(start, share), :] = low[:, i * slab : (i + 1) * slab]
        total = None
        for i in range(dp):
            part = dot_last(scratch[place_ref[i]], weights[i][...])
            total = part if total is None else total + part
        both[0] = total[:, :half].astype(bf16)
        both[1] = total[:, half:].astype(bf16)
        upper = place_ref[dp + 1]
        keep_ref[...] = both[upper]
        give_ref[...] = both[1 - upper]

    return kernel_call(
        kernel,
        "output_back",
        [places],
        [*low_pieces, *pieces],
        [shape_of((tokens, half), bf16)] * 2,
        2 * tokens * columns * slab * dp,
        [pltpu.VMEM((dp, tokens, slab), bf16), pltpu.VMEM((2, tokens, half), bf16)],
        waits=waits,
    )


def attend_back(keep, got, places, dp, turned_rows, logs, projected, squares, gains, tables, bias, waits):
    _, rows, columns = projected.shape
    tokens = rows // 2
    heads = columns // HD
    lanes = 128 // heads

    def kernel(place_ref, keep_ref, got_ref, *refs):
        turned_ref, log_ref, qk_ref, sq_ref, gain_ref, table_ref, bias_ref = refs[:7]
        gv_ref, gqk_ref, inner_ref, gains_ref, scratch = refs[7:]
        upper = place_ref[dp + 1]
        scratch[upper] = keep_ref[...]
        scratch[1 - upper] = got_ref[...]
        cosine, sine = table_ref[0], table_ref[1]
        q_squares, k_squares = as_columns(sq_ref[...])
        for which in range(2):
            row = slice(which * tokens, (which + 1) * tokens)
            q_scale = lax.rsqrt(q_squares[row] / D + epsilon)
            k_scale = lax.rsqrt(k_squares[row] / D + epsilon)
            inner = [jnp.zeros((tokens, 1), f32), jnp.zeros((tokens, 1), f32)]
            for h in range(heads):
                cut = slice(h * HD, (h + 1) * HD)
                qr, kr, v = (turned_ref[i, row, cut] for i in range(3))
                grad = scratch[which, :, cut]
                scores = dot_last(qr, kr) * (1.0 / math.sqrt(HD)) + bias_ref[which]
                probs = jnp.exp(scores - log_ref[row, h * lanes : h * lanes + 1])
                gv_ref[row, cut] = dot_first(probs.astype(bf16), grad).astype(bf16)
                grad_probs = dot_last(grad, v)
                dots = jnp.sum(probs * grad_probs, axis=1, keepdims=True)
                grad_scores = (probs * (grad_probs - dots) * (1.0 / math.sqrt(HD))).astype(bf16)
                gq = jnp.dot(grad_scores, kr, preferred_element_type=f32)
                gk = dot_first(grad_scores, qr)
                gq = gq * cosine - turned(gq) * sine
                gk = gk * cosine - turned(gk) * sine
                q, k = qk_ref[0, row, cut], qk_ref[1, row, cut]
                for i, (grad_sum, value, scale) in enumerate(((gq, q, q_scale), (gk, k, k_scale))):
                    total = jnp.sum(grad_sum * value * scale, axis=0, keepdims=True)
                    if which:
                        total = total + gains_ref[i : i + 1, cut]
                    gains_ref[i : i + 1, cut] = total
                gq = gq * gain_ref[0:1, cut]
                gk = gk * gain_ref[1:2, cut]
                gqk_ref[0, row, cut] = gq
                gqk_ref[1, row, cut] = gk
                inner[0] = inner[0] + jnp.sum(gq * q, axis=1, keepdims=True)
                inner[1] = inner[1] + jnp.sum(gk * k, axis=1, keepdims=True)
            inner_ref[:, row] = as_rows(*inner)

    return kernel_call(
        kernel,
        "attend_back",
        [places],
        [keep, got, turned_rows, logs, projected, squares, gains, tables, bias],
        [
            shape_of((rows, columns), bf16),
            shape_of((2, rows, columns), f32),
            shape_of((8, rows), f32),
            shape_of((2, columns), f32),
        ],
        10 * tokens * rows * columns,
        [pltpu.VMEM((2, tokens, columns), bf16)],
        waits=waits,
    )


def norm_back(grads, projected, squares, inner, waits=()):
    _, tokens, columns = projected.shape

    def kernel(grad_ref, value_ref, sq_ref, inner_ref, *outs):
        squares, inners = as_columns(sq_ref[...]), as_columns(inner_ref[...])
        for i, out in enumerate(outs):
            scale = lax.rsqrt(squares[i] / D + epsilon)
            mean = inners[i] / D
            out[...] = (
                scale * grad_ref[i] - value_ref[i] * (scale * scale * scale) * mean
            ).astype(bf16)

    low = shape_of((tokens, columns), bf16)
    return kernel_call(
        kernel,
        "norm_back",
        [],
        [grads, projected, squares, inner],
        [low, low],
        0,
        waits=waits,
    )


def project_back(grads, weights, places, waits=()):
    rows, columns = grads[0].shape
    tokens = rows // 2
    dp = len(weights)
    slab = weights[0].shape[0]
    share = tokens // 4

    def kernel(place_ref, *refs):
        values = [ref[...] for ref in refs[: len(grads)]]
        pieces = refs[len(grads) : len(grads) + dp]
        parts, scratch = refs[len(grads) + dp : -1], refs[-1]
        for i in range(dp):
            total = None
            for j, value in enumerate(values):
                part = dot_last(value, pieces[i][:, j * columns : (j + 1) * columns])
                total = part if total is None else total + part
            scratch[place_ref[i]] = total.astype(bf16)
        for q, part in enumerate(parts):
            for mate in range(2):
                start = row_of(place_ref, dp, tokens, share, q, mate)
                for i in range(dp):
                    part[mate * share : (mate + 1) * share, i * slab : (i + 1) * slab] = scratch[
                        i, pl.ds(start, share), :
                    ]

    return kernel_call(
        kernel,
        "project_back",
        [places],
        [*grads, *weights],
        [shape_of((2 * share, slab * dp), bf16)] * 4,
        2 * len(grads) * rows * columns * slab * dp,
        [pltpu.VMEM((dp, rows, slab), bf16)],
        waits=waits,
    )


def weight_parts(slabs, wholes, places, slab_first, waits=()):
    dp, rows, slab = slabs.shape
    columns = wholes[0].shape[1]
    half = dp // 2
    shape = (slab, columns * len(wholes)) if slab_first else (columns, slab)

    def kernel(place_ref, slab_ref, *refs):
        outs = refs[len(wholes) :]
        for i in range(dp):
            left = slab_ref[place_ref[i]]
            for j, whole in enumerate(refs[: len(wholes)]):
                pair = (left, whole[...]) if slab_first else (whole[...], left)
                cut = slice(j * columns, (j + 1) * columns) if slab_first else slice(None)
                outs[i // half][i % half, :, cut] = dot_first(*pair).astype(bf16)

    return kernel_call(
        kernel,
        "weight_parts",
        [places],
        [slabs, *wholes],
        [shape_of((half,) + shape, bf16)] * 2,
        2 * slabs.size * columns * len(wholes),
        waits=waits,
    )


def hidden_back(terms, from_mate, hidden, grad_middle, gain, waits=()):
    share, width = hidden.shape

    def kernel(a_ref, b_ref, c_ref, d_ref, hidden_ref, grad_ref, gain_ref, out_ref, gain_out):
        normed_grad = added(a_ref[:share, :], b_ref[:share, :], c_ref[:share, :], d_ref[...])
        hidden = hidden_ref[...]
        scale = lax.rsqrt(jnp.mean(hidden * hidden, axis=1, keepdims=True) + epsilon)
        gain_out[...] = jnp.sum(normed_grad * hidden * scale, axis=0, keepdims=True)
        scaled = normed_grad * gain_ref[...]
        out_ref[...] = (
            grad_ref[...]
            + scale * scaled
            - hidden * (scale * scale * scale) * jnp.mean(scaled * hidden, axis=1, keepdims=True)
        )

    return kernel_call(
        kernel,
        "hidden_back",
        [],
        [*terms, from_mate, hidden, grad_middle, gain],
        [shape_of((share, width), f32), shape_of((1, width), f32)],
        0,
        waits=waits,
    )


def rope_tables(length, head_size):
    half_size = head_size // 2
    inverse = 10000.0 ** (-2.0 * jnp.arange(half_size, dtype=jnp.float32) / head_size)
    angles = jnp.arange(length, dtype=jnp.float32)[:, None] * inverse[None, :]
    cosine, sine = jnp.cos(angles), jnp.sin(angles)
    return jnp.stack(
        [jnp.concatenate([cosine, cosine], axis=1), jnp.concatenate([-sine, sine], axis=1)]
    )


def unpack(pieces, places, rows, experts, heads, half_heads, token_order, waits=()):
    dp = len(pieces)
    tokens = pieces[0].shape[1]
    at = [0]
    for n in rows:
        at.append(at[-1] + n)
    slab = D // dp
    head_slab = HD // dp
    share = tokens // 4

    def kernel(place_ref, *refs):
        parts = refs[:dp]
        router_ref, one_ref, two_ref, gain_ref, table_ref, bias_ref, wide, heads_at = refs[dp:]
        tp, upper = place_ref[dp], place_ref[dp + 1]
        for i in range(dp):
            wide[place_ref[i]] = parts[i][...].astype(f32)
        for j in range(dp):
            cut = slice(j * slab, (j + 1) * slab)
            weight = wide[j, : at[1], :slab].astype(bf16)
            router_ref[: at[1], cut] = weight
            router_ref[at[1] :, cut] = weight
            one_ref[:, cut] = wide[j, at[1] : at[2], :slab]
            two_ref[:, cut] = wide[j, at[2] : at[3], :slab]
            for i in range(2):
                heads_at[i, :heads, j * head_slab : (j + 1) * head_slab] = wide[
                    j, at[3 + i] : at[4 + i], :head_slab
                ]
        for i in range(2):
            for h in range(half_heads):
                gain_ref[i : i + 1, h * HD : (h + 1) * HD] = heads_at[
                    i, pl.ds(upper * half_heads + h, 1), :
                ]
        row = lax.broadcasted_iota(jnp.int32, (tokens, tokens), 0)
        column = lax.broadcasted_iota(jnp.int32, (tokens, tokens), 1)
        before = jnp.where(row < column, 1.0, 0.0).astype(bf16)
        lane = lax.broadcasted_iota(jnp.int32, (at[6] - at[5], tokens), 1)
        first = place_ref[0] * experts
        for at_tokens, i in enumerate(token_order):
            ids = parts[i][at[5] : at[6], :].astype(f32)
            for bit, step in ((1, share), (2, 2 * share)):
                turned_ids = jnp.where(
                    lane // step % 2 == 0,
                    pltpu.roll(ids, tokens - step, 1),
                    pltpu.roll(ids, step, 1),
                )
                ids = jnp.where((tp & bit) != 0, turned_ids, ids)
            named = jnp.concatenate(
                [
                    jnp.sum(
                        jnp.where(ids == (first + e).astype(f32), 1.0, 0.0), axis=0, keepdims=True
                    )
                    for e in range(experts)
                ]
            )
            slot = jnp.dot(named.astype(bf16), before, preferred_element_type=f32)
            table_ref[at_tokens] = jnp.where(named > 0.5, slot, -1.0).astype(jnp.int32)
        for i in range(2):
            line = parts[i][at[6] : at[7], :].astype(f32)
            segments = jnp.broadcast_to(line, (tokens, tokens))
            allowed = (column <= row) & (segments.T == segments)
            bias_ref[upper ^ i] = jnp.where(allowed, 0.0, -1e30)

    return kernel_call(
        kernel,
        "unpack",
        [places],
        pieces,
        [
            shape_of((2 * at[1], D), bf16),
            shape_of((1, D), f32),
            shape_of((1, D), f32),
            shape_of((2, half_heads * HD), f32),
            shape_of((dp, experts, tokens), jnp.int32),
            shape_of((2, tokens, tokens), f32),
        ],
        0,
        [
            pltpu.VMEM((dp,) + pieces[0].shape, f32),
            pltpu.VMEM((2, 8, HD), f32),
        ],
        waits=waits,
    )


def packed_sums(groups, heads, places, dp, waits=()):
    slab = D // dp
    head_slab = HD // dp
    here = 0 if heads is None else heads.shape[1] // HD
    count = 4 * 2 * here
    rows = sum(-(-group.shape[0] // 8) * 8 for group in groups)

    def kernel(place_ref, *refs):
        scratch, by_head = refs[-2:]
        outs = refs[-4:-2]
        scratch[...] = jnp.zeros_like(scratch)
        if here:
            first = place_ref[dp] * 2 * here + place_ref[dp + 1] * here
            by_head[...] = jnp.zeros_like(by_head)
            for i in range(2):
                for h in range(here):
                    by_head[pl.ds(i * count + first + h, 1), :] = refs[len(groups)][
                        i : i + 1, h * HD : (h + 1) * HD
                    ]
        for j in range(dp):
            at = 0
            for ref in refs[: len(groups)]:
                scratch[j, at : at + ref.shape[0], :] = ref[:, j * slab : (j + 1) * slab]
                at += -(-ref.shape[0] // 8) * 8
            if here:
                scratch[j, at:, :head_slab] = by_head[:, j * head_slab : (j + 1) * head_slab]
        for i in range(dp):
            outs[i // (dp // 2)][i % (dp // 2)] = scratch[place_ref[i]]

    shape = (dp, rows + 2 * count, slab)
    return kernel_call(
        kernel,
        "packed_sums",
        [places],
        [*groups] + ([heads] if here else []),
        [shape_of((dp // 2,) + shape[1:], f32)] * 2,
        0,
        [pltpu.VMEM(shape, f32), pltpu.VMEM((max(2 * count, 8), HD), f32)],
        waits=waits,
    )


def per_device(
    hidden_in,
    cotangent,
    segment_ids,
    expert_ids,
    first_gain,
    query_weight,
    key_weight,
    value_weight,
    output_weight,
    query_gain,
    key_gain,
    second_gain,
    router_weight,
    gate_weight,
    up_weight,
    down_weight,
):
    data_size = lax.axis_size("dp")
    tensor_size = lax.axis_size("tp")
    half = data_size // 2
    seq_len, width = hidden_in.shape
    share = seq_len // tensor_size
    slab = width // data_size
    me_dp, me_tp = lax.axis_index("dp"), lax.axis_index("tp")
    upper = me_dp // 2 % 2
    own = lambda values: lax.dynamic_slice_in_dim(values, me_tp * share, share, 0)
    local_experts = E // data_size
    first_expert = (me_dp * local_experts).astype(jnp.int32).reshape(1)
    here = jnp.stack([me_tp, upper]).astype(jnp.int32)
    places = jnp.concatenate([owners(weight_masks()), here])
    token_order = [weight_masks().index(mask) for mask in token_masks()]

    hidden_own, cot_own = own(hidden_in), own(cotangent)
    heads_local, head_slab = query_gain.shape
    small = [
        router_weight.T,
        first_gain[None],
        second_gain[None],
        query_gain,
        key_gain,
        expert_ids.T.astype(bf16),
        segment_ids.astype(bf16),
    ]
    small_rows = [array.shape[0] for array in small]
    wide = [jnp.pad(array, ((0, 0), (0, seq_len - array.shape[1]))) for array in small]
    small = gather_dp(jnp.concatenate(wide))
    column_half = heads_local * HD // 2
    kept, given = split_heads([query_weight, key_weight, value_weight], here)
    head_line = gather_line([kept, over_z(given, 1)], z_bits()[1:])
    head_pieces = head_line + [over_y(v) for v in head_line]
    cot_line = gather_dp(cot_own.astype(bf16))
    output_pieces = gather_dp(held([output_weight], bf16, [head_line[-1]]))
    router, gain_one, gain_two, gains, table, bias = unpack(
        small,
        places,
        small_rows,
        local_experts,
        heads_local,
        heads_local // 2,
        token_order,
        waits=[head_line[1]],
    )
    tables = rope_tables(seq_len, HD)
    first_scale = lax.rsqrt(jnp.mean(hidden_in * hidden_in, axis=-1, keepdims=True) + epsilon)
    normed_one = (hidden_in * first_scale * gain_one).astype(bf16)
    mates = gather_tp(over_z(own(normed_one), 1))
    x_slabs = paired([normed_one], mates, places, data_size)
    cot_all = gather_tp(held(cot_line, bf16, [mates[2]]))
    cot_rows = rows_of_slots(cot_all, table, [], token_order)
    hidden_grad = grad_of_hidden(cot_rows, down_weight)
    projected, values, squares = project(
        x_slabs, head_pieces, places
    )
    squares = reduce_heads(squares)
    turned_rows, logs, attended, keep, give = attend(
        projected, squares, values, gains, tables, bias, places, data_size, waits=output_pieces[:half]
    )
    parts = output_project(keep, over_z(give, 1), output_pieces, places)
    middle, x_piece, probs = route(scatter_tp(parts)[0], hidden_own, gain_two, router)

    picks = (slice(0, half), slice(half, None))
    x_pieces = gather_all(x_piece)
    x_first = rows_of_slots(x_pieces[picks[0]], table[picks[0]], [hidden_grad])
    x_halves = [x_first, rows_of_slots(x_pieces[picks[1]], table[picks[1]], [x_first])]
    back_rows, act, gate_grad, up_grad = expert_step(
        x_halves, gate_weight, up_weight, hidden_grad, first_expert
    )
    second = tokens_of_slots(back_rows, table[picks[1]], half, [])
    first = tokens_of_slots(back_rows, table[picks[0]], 0, [second[0]])
    back = TokenSums(first, second).start()
    out_rows = expert_out(act, down_weight, back.sent)
    out_second = tokens_of_slots(out_rows, table[picks[1]], half, [])
    back.turn(out_second[0])
    out_first = tokens_of_slots(out_rows, table[picks[0]], 0, back.sent)
    chunk = max(local_experts // 4, 1)
    grads = []

    def some_grads(i, *waits):
        *grads[:], mark = expert_weight_grads(
            x_halves, cot_rows, act, gate_grad, up_grad, i * chunk, chunk, list(grads), waits
        )
        return mark

    mark = some_grads(0, out_first[0])
    back.top(mark)
    moe = TokenSums(out_first, out_second).start(*back.sent)
    mark = some_grads(1, mark, *moe.sent)
    back = back.last(mark)

    grad_middle, grad_low, router_sum, gain_sum = route_back(
        back, middle, x_piece, probs, cot_own, gain_two, router, waits=moe.came
    )
    low_pieces = gather_tp(grad_low)
    keep, give = output_back(low_pieces, output_pieces, places, [])
    moe.turn(keep)
    grad_values, gqk, inner, gain_sums = attend_back(
        keep, over_z(give, 1), places, data_size, turned_rows, logs, projected, squares, gains, tables, bias,
        [],
    )
    moe.top(gain_sums)
    inner = reduce_heads(inner)
    grad_queries, grad_keys = norm_back(gqk, projected, squares, inner, waits=moe.turned)
    head_grads = [grad_queries, grad_keys, grad_values]
    head_sums_at = WeightSums(*weight_parts(x_slabs, head_grads, places, True))
    parts = project_back(head_grads, head_pieces, places, waits=[head_sums_at.sent])
    terms, crossing = scatter_tp(parts)
    for_mate = combined([term[share:] for term in terms], 0)
    from_mate = over_z(for_mate, 1)
    head_sums_at.along_z(moe.from_top)
    mates_low = over_z(held(low_pieces, bf16, [for_mate]), 1)
    mark = some_grads(2, mark, head_sums_at.sent)
    moe = moe.last(head_sums_at.sent)
    low_slabs = paired(low_pieces, [mates_low], places, data_size)
    output_parts = weight_parts(
        low_slabs, [attended], places, False, waits=[head_sums_at.sent]
    )
    output_sums = WeightSums(*output_parts)
    grad_hidden, first_sum = hidden_back(terms, from_mate, hidden_own, grad_middle, gain_one)
    late = packed_sums(
        [router_sum[:E], gain_sum, first_sum],
        gain_sums,
        places,
        data_size,
        [head_sums_at.sent],
    )
    grad_hidden = gather_tp(grad_hidden)
    output_sums.along_z(mark)
    mark = some_grads(3, mark, output_sums.sent)
    head_sums_at.to_mate(output_sums.sent)
    output_sums.to_mate(head_sums_at.sent)
    total = reduce_all(*late)
    grad_hidden = absolute_tp(grad_hidden)
    hidden_out = absolute_tp(gather_tp(combined([middle, *moe], 0, sent=f32)))
    late = total[E + 8 :]
    head_sums = late[8:, :head_slab].reshape(2, heads_local * tensor_size, head_slab)
    head_sums = lax.dynamic_slice_in_dim(head_sums, me_tp * heads_local, heads_local, 1)
    grad_query, grad_key, grad_value = head_sums_at.in_order(here, 3, output_sums.sent)
    (grad_output,) = output_sums.in_order(here, 0)
    return (
        hidden_out,
        grad_hidden,
        late[0],
        grad_query,
        grad_key,
        grad_value,
        grad_output,
        head_sums[0],
        head_sums[1],
        total[E],
        total[:E].T,
        *grads,
    )


def solution(mesh):
    return jax.shard_map(
        per_device,
        mesh=mesh,
        in_specs=(
            P("dp", None),
            P("dp", None),
            P("dp", None),
            P("dp", None),
            P("dp"),
            P("dp", "tp"),
            P("dp", "tp"),
            P("dp", "tp"),
            P("tp", "dp"),
            P("tp", "dp"),
            P("tp", "dp"),
            P("dp"),
            P("dp", None),
            P("dp", None, "tp"),
            P("dp", None, "tp"),
            P("dp", "tp", None),
        ),
        out_specs=(
            P("dp", None),
            P("dp", None),
            P("dp"),
            P("dp", "tp"),
            P("dp", "tp"),
            P("dp", "tp"),
            P("tp", "dp"),
            P("tp", "dp"),
            P("tp", "dp"),
            P("dp"),
            P("dp", None),
            P("dp", None, "tp"),
            P("dp", None, "tp"),
            P("dp", "tp", None),
        ),
        check_vma=False,
    )
```

```python
import math

import jax
import jax.numpy as jnp
from jax import lax
from jax.experimental import pallas as pl
from jax.experimental.pallas import tpu as pltpu
from jax.sharding import PartitionSpec as P

D = 2048
HD = 128
E = 64
TOPK = 8
CAP = 48
EXTRA = 2 * E

bf16 = jnp.bfloat16
f32 = jnp.float32

epsilon = 1e-05


def cost(flops, bytes_accessed, transcendentals):
    return pl.CostEstimate(
        flops=flops // 1000000, bytes_accessed=bytes_accessed // 1000000, transcendentals=0
    )


def swap(values, dp_bits, tp_bits):
    dp, tp = lax.axis_size("dp"), lax.axis_size("tp")
    pairs = [
        (a * tp + b, (a ^ dp_bits) * tp + (b ^ tp_bits)) for a in range(dp) for b in range(tp)
    ]
    return lax.ppermute(values, ("dp", "tp"), pairs)


def over_z(values, bits):
    return swap(values, 2 * bits, 0)


def over_y(values):
    return swap(values, 1, 0)


def over_x(values):
    return swap(values, 0, 2)


def over_core(values):
    return swap(values, 0, 1)


def z_bits():
    half = lax.axis_size("dp") // 2
    return [1 << i for i in range(half.bit_length() - 1)]


def masks_of(bits):
    masks = [0]
    for bit in bits:
        masks = masks + [mask ^ bit for mask in masks]
    return masks


def weight_masks():
    return masks_of([2 * bit for bit in z_bits()] + [1])


def token_masks():
    return masks_of([2 * bit for bit in z_bits()[:-1]] + [1, 2 * z_bits()[-1]])


def owners(masks):
    return lax.axis_index("dp") ^ jnp.array(masks, jnp.int32)


def gather_line(pieces, bits):
    for bit in bits:
        pieces = pieces + [over_z(v, bit) for v in pieces]
    return pieces


def gather_dp(values):
    line = gather_line([values], z_bits())
    return line + [over_y(v) for v in line]


def gather_all(values, first_wait, second_wait):
    *bits, high = z_bits()
    line = gather_line([values], bits)
    going = [values] + [held([v], v.dtype, first_wait) for v in line[1:]]
    over = [over_z(v, high) for v in going]
    line = line + over[:-1] + [held(over[-1:], values.dtype, second_wait)]
    pairs = {}
    for mask, near in zip(masks_of([2 * bit for bit in z_bits()]), line, strict=True):
        if mask & 2 * high:
            aside = over_x(near)
            pairs[mask], pairs[mask + 1] = (near, aside), (over_y(near), over_y(aside))
        else:
            across = over_y(near)
            pairs[mask], pairs[mask + 1] = (near, over_x(near)), (across, over_x(across))
    return [
        (pairs[m][0], over_core(pairs[m][0]), pairs[m][1], over_core(pairs[m][1]))
        for m in token_masks()
    ]


def gather_tp(values):
    other = over_x(values)
    return [values, over_core(values), other, over_core(other)]


def sorted_by_bits(pieces, me):
    bit = 1
    while bit < len(pieces):
        odd = me & bit != 0
        pieces = [jnp.where(odd, pieces[i ^ bit], pieces[i]) for i in range(len(pieces))]
        bit *= 2
    return pieces


def absolute_dp(pieces):
    dp = len(pieces)
    by_mask = [pieces[i // 2 + i % 2 * (dp // 2)] for i in range(dp)]
    return jnp.stack(sorted_by_bits(by_mask, lax.axis_index("dp")))


def absolute_tp(pieces, axis=0):
    return jnp.concatenate(sorted_by_bits(list(pieces), lax.axis_index("tp")), axis=axis)


def added(*terms):
    total = terms[0].astype(f32)
    for term in terms[1:]:
        total = total + term.astype(f32)
    return total


def combined(terms, cut, waits=(), sent=bf16):
    shape = terms[0].shape
    outs = [shape_of((shape[0] - cut,) + shape[1:], sent)]
    if cut:
        outs.insert(0, shape_of((cut,) + shape[1:], f32))

    def kernel(*refs):
        for out, part in zip(refs[len(terms) :], (slice(0, cut), slice(cut, None))[-len(outs) :]):
            out[...] = added(*[ref[part] for ref in refs[: len(terms)]]).astype(out.dtype)

    result = kernel_call(kernel, "combined", [], list(terms), outs, 0, waits=waits)
    return result if cut else result[0]


def held(arrays, dtype, waits):
    def kernel(*refs):
        at = 0
        for ref in refs[:-1]:
            refs[-1][at : at + ref.shape[0], :] = ref[...].astype(dtype)
            at += ref.shape[0]

    rows = sum(array.shape[0] for array in arrays)
    out = shape_of((rows, arrays[0].shape[1]), dtype)
    return kernel_call(kernel, "held", [], list(arrays), [out], 0, waits=waits)[0]


def scatter_tp(parts):
    mine, far = over_core(parts[1]), over_core(parts[3])
    crossing = combined([parts[2], far], 0)
    return (parts[0], mine, over_x(crossing)), crossing


class TokenSums:
    def __init__(self, first, second):
        self.mid = first[0].shape[0] // 2
        self.first, self.second = first, second
        self.first_core = [over_core(first[1]), over_core(first[3])]
        self.second_core = [over_core(second[1]), over_core(second[3])]

    def start(self, *others):
        first, second = self.first, self.second
        self.b0, b0_far = combined([second[0], self.second_core[0]], self.mid, others)
        self.b1, b1_far = combined([second[2], self.second_core[1]], self.mid, others)
        a1 = combined([first[2], self.first_core[1]], 0, others)
        self.sent = [b0_far, b1_far, a1]
        self.came = [over_y(b0_far), over_y(b1_far), over_x(a1)]
        return self

    def turn(self, *others):
        b = combined([self.b1, self.came[1]], 0, others)
        self.a, a = combined([self.first[0], self.first_core[0], self.came[2]], self.mid, others)
        self.sent = [b, a]
        self.turned = [over_x(b), over_y(a)]
        return self

    def top(self, *others):
        self.sent = [combined([self.b0, self.came[0], self.turned[0]], 0, others)]
        self.from_top = over_z(self.sent[0], z_bits()[-1])
        return self

    def last(self, *others):
        terms = [self.a, self.turned[1], self.from_top]
        for bit in reversed(z_bits()[:-1]):
            near, sent = combined(terms, terms[0].shape[0] // 2, others if bit == 1 else ())
            terms = [near, over_z(sent, bit)]
        self.sent = [sent]
        return terms


def reduce_all(near, far):
    terms = [near, over_y(far)]
    for bit in reversed(z_bits()):
        near, sent = combined(terms, bit, sent=f32)
        terms = [near, over_z(sent, bit)]
    return reduce_tp(added(*terms)[0])


def reduce_tp(values):
    values = values + over_core(values)
    return values + over_x(values)


def reduce_heads(values):
    return reduce_tp(values + over_z(values, 1))


class WeightSums:
    def __init__(self, near, far):
        self.near, self.sent = near, far
        self.came = over_y(far)

    def along_z(self, *others):
        for bit in reversed(z_bits()[1:]):
            self.near, self.sent = combined([self.near, self.came], bit, others)
            self.came = over_z(self.sent, bit)
        return self

    def to_mate(self, *others):
        self.near, self.sent = combined([self.near, self.came], 1, others)
        self.came = over_z(self.sent, 1)
        return self

    def in_order(self, here, count, *others):
        _, rows, columns = self.near.shape
        size = columns // count if count else rows
        shape = (rows, 2 * size) if count else (2 * rows, columns)

        def kernel(here_ref, mine_ref, other_ref, *outs):
            for ref, which in ((mine_ref, here_ref[1]), (other_ref, 1 - here_ref[1])):
                part = pl.ds(pl.multiple_of(which * size, size), size)
                for j, out in enumerate(outs):
                    if count:
                        out[:, part] = ref[0, :, j * size : (j + 1) * size].astype(f32)
                    else:
                        out[part, :] = ref[0].astype(f32)

        return kernel_call(
            kernel,
            "in_order",
            [here],
            [self.near, self.came],
            [shape_of(shape, f32)] * max(count, 1),
            0,
            waits=others,
        )


def chosen_slots(table):
    experts, tokens = table.shape
    place = lax.broadcasted_iota(jnp.int32, (experts, CAP, tokens), 1)
    hit = place == table[:, None, :]
    return jnp.where(hit, 1.0, 0.0).astype(bf16).reshape(experts * CAP, tokens)


def rows_of_slots(pieces, table, waits, order=None):
    sequences, experts, tokens = table.shape
    if order is None:
        flat = [piece for group in pieces for piece in group]
        share, width = flat[0].shape
    else:
        flat = pieces
        share, width = tokens // 4, pieces[0].shape[1]
    count = sequences * 4

    def kernel(*refs):
        table_ref, *sources = refs[:-3]
        out_ref, buffer, arrived = refs[-3:]
        step = pl.program_id(0)

        def piece(i):
            if order is None:
                return sources[i]
            return sources[i % 4].at[pl.ds(order[i // 4] * share, share), :]

        @pl.when(step == 0)
        def _():
            for i in range(count):
                pltpu.make_async_copy(
                    piece(i), buffer.at[i // 4, pl.ds(i % 4 * share, share)], arrived.at[i]
                ).start()

        for i in range(4):
            pltpu.make_async_copy(
                piece(i), buffer.at[step, pl.ds(i * share, share)], arrived.at[step * 4 + i]
            ).wait()
        picked = jnp.dot(chosen_slots(table_ref[0]), buffer[step], preferred_element_type=f32)
        out_ref[...] = picked.astype(bf16).reshape(experts, CAP, width)

    return pl.pallas_call(
        without(kernel, 1 + len(flat), len(waits)),
        grid=(sequences,),
        in_specs=[pl.BlockSpec((1, experts, tokens), lambda s: (s, 0, 0))]
        + [pl.BlockSpec(memory_space=pltpu.HBM)] * len(flat)
        + [pl.BlockSpec(memory_space=pl.ANY)] * len(waits),
        out_specs=pl.BlockSpec((experts, CAP, width), lambda s: (0, s, 0)),
        out_shape=jax.ShapeDtypeStruct((experts, sequences * CAP, width), bf16),
        scratch_shapes=[
            pltpu.VMEM((sequences, tokens, width), bf16),
            pltpu.SemaphoreType.DMA((count,)),
        ],
        compiler_params=pltpu.CompilerParams(vmem_limit_bytes=48 << 20),
        cost_estimate=cost(
            flops=2 * experts * CAP * sequences * tokens * width,
            bytes_accessed=2 * sequences * (tokens + experts * CAP) * width,
            transcendentals=0,
        ),
        name="rows_of_slots",
    )(table, *flat, *waits)


def tokens_of_slots(rows, table, first, waits):
    sequences, experts, tokens = table.shape
    width = rows.shape[-1]
    share = tokens // 4

    def kernel(table_ref, rows_ref, *outs):
        picked = chosen_slots(table_ref[0])
        total = lax.dot_general(
            picked,
            rows_ref[...].reshape(experts * CAP, width),
            (((0,), (0,)), ((), ())),
            preferred_element_type=f32,
        ).astype(bf16)
        for q, out in enumerate(outs):
            out[...] = total[q * share : (q + 1) * share]

    return pl.pallas_call(
        without(kernel, 2, len(waits)),
        grid=(sequences,),
        in_specs=[
            pl.BlockSpec((1, experts, tokens), lambda s: (s, 0, 0)),
            pl.BlockSpec((experts, CAP, width), lambda s: (0, s + first, 0)),
        ]
        + [pl.BlockSpec(memory_space=pl.ANY)] * len(waits),
        out_specs=[pl.BlockSpec((share, width), lambda s: (s, 0))] * 4,
        out_shape=[jax.ShapeDtypeStruct((sequences * share, width), bf16)] * 4,
        compiler_params=pltpu.CompilerParams(vmem_limit_bytes=48 << 20),
        cost_estimate=cost(
            flops=2 * experts * CAP * sequences * tokens * width,
            bytes_accessed=2 * sequences * (tokens + experts * CAP) * width,
            transcendentals=0,
        ),
        name="tokens_of_slots",
    )(table, rows, *waits)


def dot_last(a, b):
    return lax.dot_general(a, b, (((1,), (1,)), ((), ())), preferred_element_type=f32)


def dot_first(a, b):
    return lax.dot_general(a, b, (((0,), (0,)), ((), ())), preferred_element_type=f32)


def per_expert(kernel, experts, ins, outs, flops, name, scalars=(), waits=()):
    whole = lambda shape: pl.BlockSpec((1,) + tuple(shape[1:]), lambda e: (e, 0, 0))
    in_specs = [pl.BlockSpec(memory_space=pltpu.SMEM)] * len(scalars)
    moved = 0
    for array, block in ins:
        in_specs.append(pl.BlockSpec((1,) + block, lambda e: (e, 0, 0)))
        moved += experts * math.prod(block) * array.dtype.itemsize
    moved += sum(math.prod(o.shape) * o.dtype.itemsize for o in outs)
    return pl.pallas_call(
        without(kernel, len(in_specs), len(waits)),
        grid=(experts,),
        in_specs=in_specs + [pl.BlockSpec(memory_space=pl.ANY)] * len(waits),
        out_specs=[whole(o.shape) for o in outs],
        out_shape=list(outs),
        compiler_params=pltpu.CompilerParams(vmem_limit_bytes=48 << 20),
        cost_estimate=cost(flops=flops, bytes_accessed=moved, transcendentals=0),
        name=name,
    )(*scalars, *[array for array, _ in ins], *waits)


def grad_of_hidden(cot_rows, down_weight):
    experts, rows, width = cot_rows.shape
    hidden = down_weight.shape[1]

    def kernel(cot_ref, down_ref, out_ref):
        out_ref[0] = dot_last(cot_ref[0], down_ref[0])

    return per_expert(
        kernel,
        experts,
        [(cot_rows, (rows, width)), (down_weight, (hidden, width))],
        [jax.ShapeDtypeStruct((experts, rows, hidden), f32)],
        2 * experts * rows * width * hidden,
        "grad_of_hidden",
    )[0]


def expert_step(x_halves, gate_weight, up_weight, hidden_grad, first_expert):
    experts, half_rows, wide = x_halves[0].shape
    rows = half_rows * 2
    width, hidden = gate_weight.shape[1:]

    def kernel(base_ref, a_ref, b_ref, gate_ref, up_ref, grad_ref, back_ref, act_ref, gate_grad_ref, up_grad_ref):
        mine = base_ref[0] + pl.program_id(0)
        x = jnp.concatenate([a_ref[0, :, :width], b_ref[0, :, :width]])
        lane = lax.broadcasted_iota(jnp.int32, (rows, EXTRA), 1)
        probs = jnp.concatenate([a_ref[0, :, width:], b_ref[0, :, width:]]).astype(f32)
        mix = jnp.sum(
            jnp.where((lane == mine) | (lane == mine + E), probs, 0.0), axis=1, keepdims=True
        )
        gate_act = jnp.dot(x, gate_ref[0], preferred_element_type=f32)
        up_act = jnp.dot(x, up_ref[0], preferred_element_type=f32)
        raw = grad_ref[0]
        sig = jax.nn.sigmoid(gate_act)
        silu = gate_act * sig
        act = silu * up_act
        grad_mix = jnp.sum(act * raw, axis=1, keepdims=True)
        act_ref[0] = (mix * act).astype(bf16)
        weighted = mix * raw
        gate_grad = (weighted * up_act * sig * (1.0 + gate_act * (1.0 - sig))).astype(bf16)
        up_grad = (weighted * silu).astype(bf16)
        gate_grad_ref[0] = gate_grad
        up_grad_ref[0] = up_grad
        back_ref[0, :, :width] = (
            dot_last(gate_grad, gate_ref[0]) + dot_last(up_grad, up_ref[0])
        ).astype(bf16)
        coarse = grad_mix.astype(bf16).astype(f32)
        fine = grad_mix - coarse
        back_ref[0, :, width:] = jnp.where(
            lane == mine, coarse, jnp.where(lane == mine + E, fine, 0.0)
        ).astype(bf16)

    small = jax.ShapeDtypeStruct((experts, rows, hidden), bf16)
    return per_expert(
        kernel,
        experts,
        [
            (x_halves[0], (half_rows, wide)),
            (x_halves[1], (half_rows, wide)),
            (gate_weight, (width, hidden)),
            (up_weight, (width, hidden)),
            (hidden_grad, (rows, hidden)),
        ],
        [jax.ShapeDtypeStruct((experts, rows, wide), bf16), small, small, small],
        8 * experts * rows * width * hidden,
        "expert_step",
        (first_expert,),
    )


def expert_out(act, down_weight, waits):
    experts, rows, hidden = act.shape
    width = down_weight.shape[2]

    def kernel(act_ref, down_ref, out_ref):
        out_ref[0] = jnp.dot(act_ref[0], down_ref[0], preferred_element_type=f32).astype(bf16)

    return per_expert(
        kernel,
        experts,
        [(act, (rows, hidden)), (down_weight, (hidden, width))],
        [jax.ShapeDtypeStruct((experts, rows, width), bf16)],
        2 * experts * rows * width * hidden,
        "expert_out",
        waits=waits,
    )[0]


def expert_weight_grads(x_halves, cot_rows, act, gate_grad, up_grad, first, count, into, waits):
    experts, rows, hidden = act.shape
    width = cot_rows.shape[2]

    def kernel(a_ref, b_ref, cot_ref, act_ref, gate_ref, up_ref, *refs):
        gate_out, up_out, down_out, mark = refs[-4:]
        mark[...] = jnp.zeros_like(mark)
        x = jnp.concatenate([a_ref[0], b_ref[0]])
        gate_out[0] = dot_first(x, gate_ref[0])
        up_out[0] = dot_first(x, up_ref[0])
        down_out[0] = dot_first(act_ref[0], cot_ref[0])

    block = lambda *shape: pl.BlockSpec((1,) + shape, lambda e: (e + first, 0, 0))
    ins = [*x_halves, cot_rows, act, gate_grad, up_grad]
    return pl.pallas_call(
        kernel,
        grid=(count,),
        in_specs=[block(rows // 2, width)] * 2
        + [block(rows, width)]
        + [block(rows, hidden)] * 3
        + [pl.BlockSpec(memory_space=pl.ANY)] * (len(into) + len(waits)),
        out_specs=[block(width, hidden), block(width, hidden), block(hidden, width)]
        + [pl.BlockSpec((8, 128), lambda e: (0, 0))],
        out_shape=[
            jax.ShapeDtypeStruct((experts, width, hidden), f32),
            jax.ShapeDtypeStruct((experts, width, hidden), f32),
            jax.ShapeDtypeStruct((experts, hidden, width), f32),
            jax.ShapeDtypeStruct((8, 128), f32),
        ],
        input_output_aliases={len(ins) + i: i for i in range(len(into))},
        compiler_params=pltpu.CompilerParams(vmem_limit_bytes=48 << 20),
        cost_estimate=cost(
            flops=6 * count * rows * width * hidden,
            bytes_accessed=count * (4 * rows * (width + hidden) + 12 * width * hidden),
            transcendentals=0,
        ),
        name="expert_weight_grads",
    )(*ins, *into, *waits)


def without(kernel, start, count):
    return lambda *refs: kernel(*refs[:start], *refs[start + count :])


def kernel_call(kernel, name, scalars, ins, outs, flops, scratch=(), waits=()):
    moved = sum(a.size * a.dtype.itemsize for a in ins)
    moved += sum(math.prod(o.shape) * o.dtype.itemsize for o in outs)
    large = [i for i, a in enumerate(ins) if a.size * a.dtype.itemsize >= 1 << 16]
    first, last = len(scalars), len(scalars) + len(ins)
    made = last + len(waits)

    def body(*refs):
        given = list(refs[first:last])
        kept = made + len(outs) + len(scratch)
        copies = []
        for k, i in enumerate(large):
            copies.append(pltpu.make_async_copy(given[i], refs[kept + k], refs[-1].at[k]))
            copies[-1].start()
            given[i] = refs[kept + k]
        for copy in copies:
            copy.wait()
        kernel(*refs[:first], *given, *refs[made:kept])

    places = [pl.ANY if i in large else pltpu.VMEM for i in range(len(ins))]
    return pl.pallas_call(
        body,
        in_specs=[pl.BlockSpec(memory_space=pltpu.SMEM)] * len(scalars)
        + [pl.BlockSpec(memory_space=place) for place in places]
        + [pl.BlockSpec(memory_space=pl.ANY)] * len(waits),
        out_specs=[pl.BlockSpec(memory_space=pltpu.VMEM)] * len(outs),
        out_shape=list(outs),
        scratch_shapes=list(scratch)
        + [pltpu.VMEM(ins[i].shape, ins[i].dtype) for i in large]
        + [pltpu.SemaphoreType.DMA((max(len(large), 1),))],
        compiler_params=pltpu.CompilerParams(vmem_limit_bytes=40 << 20),
        cost_estimate=cost(flops=flops, bytes_accessed=moved, transcendentals=0),
        name=name,
    )(*scalars, *ins, *waits)


def shape_of(shape, dtype):
    return jax.ShapeDtypeStruct(shape, dtype)


def row_of(place_ref, dp, tokens, share, q, mate):
    which = (1 - place_ref[dp + 1]) if mate else place_ref[dp + 1]
    return pl.multiple_of(which * tokens + (place_ref[dp] ^ q) * share, share)


def split_heads(weights, here):
    rows, columns = weights[0].shape
    half = columns // 2

    def kernel(here_ref, *refs):
        keep_ref, give_ref, scratch = refs[len(weights) :]
        for j, ref in enumerate(refs[: len(weights)]):
            for i in range(2):
                scratch[i, :, j * half : (j + 1) * half] = ref[:, i * half : (i + 1) * half]
        keep_ref[...] = scratch[here_ref[1]]
        give_ref[...] = scratch[1 - here_ref[1]]

    shape = (rows, half * len(weights))
    return kernel_call(
        kernel,
        "split_heads",
        [here],
        list(weights),
        [shape_of(shape, bf16)] * 2,
        0,
        [pltpu.VMEM((2,) + shape, bf16)],
    )


def paired(own, mates, places, dp):
    share, width = mates[0].shape
    if len(mates) == 1:
        share = share // 4
    tokens = 4 * share
    slab = width // dp

    def kernel(place_ref, *refs):
        out_ref = refs[-1]
        if len(own) == 1:
            start = pl.multiple_of(place_ref[dp + 1] * tokens, tokens)
            for i in range(dp):
                out_ref[i, pl.ds(start, tokens), :] = refs[0][:, i * slab : (i + 1) * slab]
        for q in range(4):
            sources = []
            if len(own) == 4:
                sources.append((refs[q][...], False))
            if len(mates) == 4:
                sources.append((refs[len(own) + q][...], True))
            else:
                sources.append((refs[len(own)][q * share : (q + 1) * share, :], True))
            for rows, mate in sources:
                start = row_of(place_ref, dp, tokens, share, q, mate)
                for i in range(dp):
                    out_ref[i, pl.ds(start, share), :] = rows[:, i * slab : (i + 1) * slab]

    return kernel_call(
        kernel, "paired", [places], [*own, *mates], [shape_of((dp, 2 * tokens, slab), bf16)], 0
    )[0]


def as_rows(first, second):
    lane = lax.broadcasted_iota(jnp.int32, (first.shape[0], 128), 1)
    return jnp.where(lane < 4, first, second).T[:8]


def as_columns(pair):
    wide = jnp.concatenate([pair] * 16).T
    return wide[:, 0:1], wide[:, 4:5]


def project(x_slabs, pieces, places):
    dp, tokens, _ = x_slabs.shape
    columns = pieces[0].shape[1] // 3

    def kernel(place_ref, x_ref, *refs):
        totals = []
        for j in range(3):
            total = None
            for i in range(dp):
                part = jnp.dot(
                    x_ref[place_ref[i]],
                    refs[i][:, j * columns : (j + 1) * columns],
                    preferred_element_type=f32,
                )
                total = part if total is None else total + part
            totals.append(total)
        queries, keys, values = totals
        qk_out, v_out, squares_out = refs[dp:]
        qk_out[0] = queries
        qk_out[1] = keys
        v_out[...] = values.astype(bf16)
        squares_out[...] = as_rows(
            jnp.sum(queries * queries, axis=1, keepdims=True),
            jnp.sum(keys * keys, axis=1, keepdims=True),
        )

    return kernel_call(
        kernel,
        "project",
        [places],
        [x_slabs, *pieces],
        [
            shape_of((2, tokens, columns), f32),
            shape_of((tokens, columns), bf16),
            shape_of((8, tokens), f32),
        ],
        6 * x_slabs.size * columns,
    )


def turned(values):
    return pltpu.roll(values, HD // 2, 1)


def attend(projected, squares, values, gains, tables, bias, places, dp, waits=()):
    _, rows, columns = projected.shape
    tokens = rows // 2
    heads = columns // HD
    lanes = 128 // heads

    def kernel(place_ref, qk_ref, sq_ref, v_ref, gain_ref, table_ref, bias_ref, *refs):
        turned_out, log_out, att_out, keep_out, give_out = refs
        turned_out[2] = v_ref[...]
        cosine, sine = table_ref[0], table_ref[1]
        lane = lax.broadcasted_iota(jnp.int32, (tokens, 128), 1)
        q_squares, k_squares = as_columns(sq_ref[...])
        for which in range(2):
            row = slice(which * tokens, (which + 1) * tokens)
            q_scale = lax.rsqrt(q_squares[row] / D + epsilon)
            k_scale = lax.rsqrt(k_squares[row] / D + epsilon)
            logs = jnp.zeros((tokens, 128), f32)
            for h in range(heads):
                cut = slice(h * HD, (h + 1) * HD)
                q = qk_ref[0, row, cut] * q_scale * gain_ref[0:1, cut]
                k = qk_ref[1, row, cut] * k_scale * gain_ref[1:2, cut]
                q = (q * cosine + turned(q) * sine).astype(bf16)
                k = (k * cosine + turned(k) * sine).astype(bf16)
                turned_out[0, row, cut] = q
                turned_out[1, row, cut] = k
                scores = dot_last(q, k) * (1.0 / math.sqrt(HD)) + bias_ref[which]
                largest = jnp.max(scores, axis=1, keepdims=True)
                raised = jnp.exp(scores - largest)
                total = jnp.sum(raised, axis=1, keepdims=True)
                logs = jnp.where(lane // lanes == h, largest + jnp.log(total), logs)
                probs = (raised / total).astype(bf16)
                att_out[row, cut] = jnp.dot(
                    probs, v_ref[row, cut], preferred_element_type=f32
                ).astype(bf16)
            log_out[row, :] = logs
        upper = place_ref[dp + 1]
        keep_out[...] = att_out[pl.ds(pl.multiple_of(upper * tokens, tokens), tokens), :]
        give_out[...] = att_out[pl.ds(pl.multiple_of((1 - upper) * tokens, tokens), tokens), :]

    part = shape_of((tokens, columns), bf16)
    return kernel_call(
        kernel,
        "attend",
        [places],
        [projected, squares, values, gains, tables, bias],
        [
            shape_of((3, rows, columns), bf16),
            shape_of((rows, 128), f32),
            shape_of((rows, columns), bf16),
            part,
            part,
        ],
        4 * tokens * rows * columns,
        waits=waits,
    )


def output_project(keep, got, pieces, places, waits=()):
    tokens, columns = keep.shape
    dp = len(pieces)
    slab = pieces[0].shape[1]
    share = tokens // 4

    def kernel(place_ref, keep_ref, got_ref, *refs):
        weights, parts, scratch = refs[:dp], refs[dp:-1], refs[-1]
        upper = place_ref[dp + 1]
        mine = pl.ds(pl.multiple_of(upper * columns, columns), columns)
        other = pl.ds(pl.multiple_of((1 - upper) * columns, columns), columns)
        for i in range(dp):
            scratch[place_ref[i]] = (
                jnp.dot(keep_ref[...], weights[i][mine, :], preferred_element_type=f32)
                + jnp.dot(got_ref[...], weights[i][other, :], preferred_element_type=f32)
            ).astype(bf16)
        for q, part in enumerate(parts):
            start = pl.multiple_of((place_ref[dp] ^ q) * share, share)
            for i in range(dp):
                part[:, i * slab : (i + 1) * slab] = scratch[i, pl.ds(start, share), :]

    return kernel_call(
        kernel,
        "output_project",
        [places],
        [keep, got, *pieces],
        [shape_of((share, slab * dp), bf16)] * 4,
        4 * tokens * columns * slab * dp,
        [pltpu.VMEM((dp, tokens, slab), bf16)],
        waits=waits,
    )


def route(terms, hidden, gain, router, waits=()):
    share, width = hidden.shape

    def kernel(a_ref, b_ref, c_ref, hidden_ref, gain_ref, router_ref, middle_ref, x_ref, probs_ref):
        middle = hidden_ref[...] + added(a_ref[...], b_ref[...], c_ref[...])
        middle_ref[...] = middle
        scale = lax.rsqrt(jnp.mean(middle * middle, axis=1, keepdims=True) + epsilon)
        normed = (middle * scale * gain_ref[...]).astype(bf16)
        x_ref[:, :width] = normed
        logits = dot_last(normed, router_ref[...])
        raised = jnp.exp(logits - jnp.max(logits, axis=1, keepdims=True))
        probs = raised / (0.5 * jnp.sum(raised, axis=1, keepdims=True))
        probs_ref[...] = probs
        coarse = probs.astype(bf16).astype(f32)
        lane = lax.broadcasted_iota(jnp.int32, probs.shape, 1)
        x_ref[:, width:] = jnp.where(lane < E, coarse, probs - coarse).astype(bf16)

    return kernel_call(
        kernel,
        "route",
        [],
        [*terms, hidden, gain, router],
        [
            shape_of((share, width), f32),
            shape_of((share, width + EXTRA), bf16),
            shape_of((share, EXTRA), f32),
        ],
        2 * share * width * EXTRA,
        waits=waits,
    )


def route_back(terms, middle, x_piece, probs, cotangent, gain, router, waits=()):
    share, width = middle.shape

    def kernel(a_ref, b_ref, middle_ref, x_ref, probs_ref, cot_ref, gain_ref, router_ref, *outs):
        grad_ref, low_ref, router_out, gain_out = outs
        pair = added(a_ref[:, width:], b_ref[:, width:])
        grad_probs = pair + pltpu.roll(pair, E, 1)
        probs = probs_ref[...]
        inner = 0.5 * jnp.sum(probs * grad_probs, axis=1, keepdims=True)
        grad_logits = probs * (grad_probs - inner)
        middle = middle_ref[...]
        scale = lax.rsqrt(jnp.mean(middle * middle, axis=1, keepdims=True) + epsilon)
        lane = lax.broadcasted_iota(jnp.int32, probs.shape, 1)
        once = jnp.where(lane < E, grad_logits, 0.0)
        normed_grad = added(a_ref[:, :width], b_ref[:, :width]) + lax.dot_general(
            once,
            router_ref[...].astype(f32),
            (((1,), (0,)), ((), ())),
            precision=lax.Precision.HIGHEST,
            preferred_element_type=f32,
        )
        router_out[...] = lax.dot_general(
            once,
            x_ref[:, :width].astype(f32),
            (((0,), (0,)), ((), ())),
            precision=lax.Precision.HIGHEST,
            preferred_element_type=f32,
        )
        gain_out[...] = jnp.sum(normed_grad * middle * scale, axis=0, keepdims=True)
        scaled = normed_grad * gain_ref[...]
        grad = (
            cot_ref[...]
            + scale * scaled
            - middle * (scale * scale * scale) * jnp.mean(scaled * middle, axis=1, keepdims=True)
        )
        grad_ref[...] = grad
        low_ref[...] = grad.astype(bf16)

    return kernel_call(
        kernel,
        "route_back",
        [],
        [*terms, middle, x_piece, probs, cotangent, gain, router],
        [
            shape_of((share, width), f32),
            shape_of((share, width), bf16),
            shape_of((EXTRA, width), f32),
            shape_of((1, width), f32),
        ],
        24 * share * width * EXTRA,
        waits=waits,
    )


def output_back(low_pieces, pieces, places, waits):
    dp = len(pieces)
    columns, slab = pieces[0].shape
    share = low_pieces[0].shape[0]
    tokens = 4 * share
    half = columns // 2

    def kernel(place_ref, *refs):
        lows, weights, (keep_ref, give_ref, scratch, both) = refs[:4], refs[4 : 4 + dp], refs[4 + dp :]
        for q, low in enumerate(lows):
            start = pl.multiple_of((place_ref[dp] ^ q) * share, share)
            for i in range(dp):
                scratch[i, pl.ds(start, share), :] = low[:, i * slab : (i + 1) * slab]
        total = None
        for i in range(dp):
            part = dot_last(scratch[place_ref[i]], weights[i][...])
            total = part if total is None else total + part
        both[0] = total[:, :half].astype(bf16)
        both[1] = total[:, half:].astype(bf16)
        upper = place_ref[dp + 1]
        keep_ref[...] = both[upper]
        give_ref[...] = both[1 - upper]

    return kernel_call(
        kernel,
        "output_back",
        [places],
        [*low_pieces, *pieces],
        [shape_of((tokens, half), bf16)] * 2,
        2 * tokens * columns * slab * dp,
        [pltpu.VMEM((dp, tokens, slab), bf16), pltpu.VMEM((2, tokens, half), bf16)],
        waits=waits,
    )


def attend_back(keep, got, places, dp, turned_rows, logs, projected, squares, gains, tables, bias, waits):
    _, rows, columns = projected.shape
    tokens = rows // 2
    heads = columns // HD
    lanes = 128 // heads

    def kernel(place_ref, keep_ref, got_ref, *refs):
        turned_ref, log_ref, qk_ref, sq_ref, gain_ref, table_ref, bias_ref = refs[:7]
        gv_ref, gqk_ref, inner_ref, gains_ref, scratch = refs[7:]
        upper = place_ref[dp + 1]
        scratch[upper] = keep_ref[...]
        scratch[1 - upper] = got_ref[...]
        cosine, sine = table_ref[0], table_ref[1]
        q_squares, k_squares = as_columns(sq_ref[...])
        for which in range(2):
            row = slice(which * tokens, (which + 1) * tokens)
            q_scale = lax.rsqrt(q_squares[row] / D + epsilon)
            k_scale = lax.rsqrt(k_squares[row] / D + epsilon)
            inner = [jnp.zeros((tokens, 1), f32), jnp.zeros((tokens, 1), f32)]
            for h in range(heads):
                cut = slice(h * HD, (h + 1) * HD)
                qr, kr, v = (turned_ref[i, row, cut] for i in range(3))
                grad = scratch[which, :, cut]
                scores = dot_last(qr, kr) * (1.0 / math.sqrt(HD)) + bias_ref[which]
                probs = jnp.exp(scores - log_ref[row, h * lanes : h * lanes + 1])
                gv_ref[row, cut] = dot_first(probs.astype(bf16), grad).astype(bf16)
                grad_probs = dot_last(grad, v)
                dots = jnp.sum(probs * grad_probs, axis=1, keepdims=True)
                grad_scores = (probs * (grad_probs - dots) * (1.0 / math.sqrt(HD))).astype(bf16)
                gq = jnp.dot(grad_scores, kr, preferred_element_type=f32)
                gk = dot_first(grad_scores, qr)
                gq = gq * cosine - turned(gq) * sine
                gk = gk * cosine - turned(gk) * sine
                q, k = qk_ref[0, row, cut], qk_ref[1, row, cut]
                for i, (grad_sum, value, scale) in enumerate(((gq, q, q_scale), (gk, k, k_scale))):
                    total = jnp.sum(grad_sum * value * scale, axis=0, keepdims=True)
                    if which:
                        total = total + gains_ref[i : i + 1, cut]
                    gains_ref[i : i + 1, cut] = total
                gq = gq * gain_ref[0:1, cut]
                gk = gk * gain_ref[1:2, cut]
                gqk_ref[0, row, cut] = gq
                gqk_ref[1, row, cut] = gk
                inner[0] = inner[0] + jnp.sum(gq * q, axis=1, keepdims=True)
                inner[1] = inner[1] + jnp.sum(gk * k, axis=1, keepdims=True)
            inner_ref[:, row] = as_rows(*inner)

    return kernel_call(
        kernel,
        "attend_back",
        [places],
        [keep, got, turned_rows, logs, projected, squares, gains, tables, bias],
        [
            shape_of((rows, columns), bf16),
            shape_of((2, rows, columns), f32),
            shape_of((8, rows), f32),
            shape_of((2, columns), f32),
        ],
        10 * tokens * rows * columns,
        [pltpu.VMEM((2, tokens, columns), bf16)],
        waits=waits,
    )


def norm_back(grads, projected, squares, inner, waits=()):
    _, tokens, columns = projected.shape

    def kernel(grad_ref, value_ref, sq_ref, inner_ref, *outs):
        squares, inners = as_columns(sq_ref[...]), as_columns(inner_ref[...])
        for i, out in enumerate(outs):
            scale = lax.rsqrt(squares[i] / D + epsilon)
            mean = inners[i] / D
            out[...] = (
                scale * grad_ref[i] - value_ref[i] * (scale * scale * scale) * mean
            ).astype(bf16)

    low = shape_of((tokens, columns), bf16)
    return kernel_call(
        kernel,
        "norm_back",
        [],
        [grads, projected, squares, inner],
        [low, low],
        0,
        waits=waits,
    )


def project_back(grads, weights, places, waits=()):
    rows, columns = grads[0].shape
    tokens = rows // 2
    dp = len(weights)
    slab = weights[0].shape[0]
    share = tokens // 4

    def kernel(place_ref, *refs):
        values = [ref[...] for ref in refs[: len(grads)]]
        pieces = refs[len(grads) : len(grads) + dp]
        parts, scratch = refs[len(grads) + dp : -1], refs[-1]
        for i in range(dp):
            total = None
            for j, value in enumerate(values):
                part = dot_last(value, pieces[i][:, j * columns : (j + 1) * columns])
                total = part if total is None else total + part
            scratch[place_ref[i]] = total.astype(bf16)
        for q, part in enumerate(parts):
            for mate in range(2):
                start = row_of(place_ref, dp, tokens, share, q, mate)
                for i in range(dp):
                    part[mate * share : (mate + 1) * share, i * slab : (i + 1) * slab] = scratch[
                        i, pl.ds(start, share), :
                    ]

    return kernel_call(
        kernel,
        "project_back",
        [places],
        [*grads, *weights],
        [shape_of((2 * share, slab * dp), bf16)] * 4,
        2 * len(grads) * rows * columns * slab * dp,
        [pltpu.VMEM((dp, rows, slab), bf16)],
        waits=waits,
    )


def weight_parts(slabs, wholes, places, slab_first, waits=()):
    dp, rows, slab = slabs.shape
    columns = wholes[0].shape[1]
    half = dp // 2
    shape = (slab, columns * len(wholes)) if slab_first else (columns, slab)

    def kernel(place_ref, slab_ref, *refs):
        outs = refs[len(wholes) :]
        for i in range(dp):
            left = slab_ref[place_ref[i]]
            for j, whole in enumerate(refs[: len(wholes)]):
                pair = (left, whole[...]) if slab_first else (whole[...], left)
                cut = slice(j * columns, (j + 1) * columns) if slab_first else slice(None)
                outs[i // half][i % half, :, cut] = dot_first(*pair).astype(bf16)

    return kernel_call(
        kernel,
        "weight_parts",
        [places],
        [slabs, *wholes],
        [shape_of((half,) + shape, bf16)] * 2,
        2 * slabs.size * columns * len(wholes),
        waits=waits,
    )


def hidden_back(terms, from_mate, hidden, grad_middle, gain, waits=()):
    share, width = hidden.shape

    def kernel(a_ref, b_ref, c_ref, d_ref, hidden_ref, grad_ref, gain_ref, out_ref, gain_out):
        normed_grad = added(a_ref[:share, :], b_ref[:share, :], c_ref[:share, :], d_ref[...])
        hidden = hidden_ref[...]
        scale = lax.rsqrt(jnp.mean(hidden * hidden, axis=1, keepdims=True) + epsilon)
        gain_out[...] = jnp.sum(normed_grad * hidden * scale, axis=0, keepdims=True)
        scaled = normed_grad * gain_ref[...]
        out_ref[...] = (
            grad_ref[...]
            + scale * scaled
            - hidden * (scale * scale * scale) * jnp.mean(scaled * hidden, axis=1, keepdims=True)
        )

    return kernel_call(
        kernel,
        "hidden_back",
        [],
        [*terms, from_mate, hidden, grad_middle, gain],
        [shape_of((share, width), f32), shape_of((1, width), f32)],
        0,
        waits=waits,
    )


def rope_tables(length, head_size):
    half_size = head_size // 2
    inverse = 10000.0 ** (-2.0 * jnp.arange(half_size, dtype=jnp.float32) / head_size)
    angles = jnp.arange(length, dtype=jnp.float32)[:, None] * inverse[None, :]
    cosine, sine = jnp.cos(angles), jnp.sin(angles)
    return jnp.stack(
        [jnp.concatenate([cosine, cosine], axis=1), jnp.concatenate([-sine, sine], axis=1)]
    )


def unpack(pieces, places, rows, experts, heads, half_heads, token_order, waits=()):
    dp = len(pieces)
    tokens = pieces[0].shape[1]
    at = [0]
    for n in rows:
        at.append(at[-1] + n)
    slab = D // dp
    head_slab = HD // dp
    share = tokens // 4

    def kernel(place_ref, *refs):
        parts = refs[:dp]
        router_ref, one_ref, two_ref, gain_ref, table_ref, bias_ref, wide, heads_at = refs[dp:]
        tp, upper = place_ref[dp], place_ref[dp + 1]
        for i in range(dp):
            wide[place_ref[i]] = parts[i][...].astype(f32)
        for j in range(dp):
            cut = slice(j * slab, (j + 1) * slab)
            weight = wide[j, : at[1], :slab].astype(bf16)
            router_ref[: at[1], cut] = weight
            router_ref[at[1] :, cut] = weight
            one_ref[:, cut] = wide[j, at[1] : at[2], :slab]
            two_ref[:, cut] = wide[j, at[2] : at[3], :slab]
            for i in range(2):
                heads_at[i, :heads, j * head_slab : (j + 1) * head_slab] = wide[
                    j, at[3 + i] : at[4 + i], :head_slab
                ]
        for i in range(2):
            for h in range(half_heads):
                gain_ref[i : i + 1, h * HD : (h + 1) * HD] = heads_at[
                    i, pl.ds(upper * half_heads + h, 1), :
                ]
        row = lax.broadcasted_iota(jnp.int32, (tokens, tokens), 0)
        column = lax.broadcasted_iota(jnp.int32, (tokens, tokens), 1)
        before = jnp.where(row < column, 1.0, 0.0).astype(bf16)
        lane = lax.broadcasted_iota(jnp.int32, (at[6] - at[5], tokens), 1)
        first = place_ref[0] * experts
        for at_tokens, i in enumerate(token_order):
            ids = parts[i][at[5] : at[6], :].astype(f32)
            for bit, step in ((1, share), (2, 2 * share)):
                turned_ids = jnp.where(
                    lane // step % 2 == 0,
                    pltpu.roll(ids, tokens - step, 1),
                    pltpu.roll(ids, step, 1),
                )
                ids = jnp.where((tp & bit) != 0, turned_ids, ids)
            named = jnp.concatenate(
                [
                    jnp.sum(
                        jnp.where(ids == (first + e).astype(f32), 1.0, 0.0), axis=0, keepdims=True
                    )
                    for e in range(experts)
                ]
            )
            slot = jnp.dot(named.astype(bf16), before, preferred_element_type=f32)
            table_ref[at_tokens] = jnp.where(named > 0.5, slot, -1.0).astype(jnp.int32)
        for i in range(2):
            line = parts[i][at[6] : at[7], :].astype(f32)
            segments = jnp.broadcast_to(line, (tokens, tokens))
            allowed = (column <= row) & (segments.T == segments)
            bias_ref[upper ^ i] = jnp.where(allowed, 0.0, -1e30)

    return kernel_call(
        kernel,
        "unpack",
        [places],
        pieces,
        [
            shape_of((2 * at[1], D), bf16),
            shape_of((1, D), f32),
            shape_of((1, D), f32),
            shape_of((2, half_heads * HD), f32),
            shape_of((dp, experts, tokens), jnp.int32),
            shape_of((2, tokens, tokens), f32),
        ],
        0,
        [
            pltpu.VMEM((dp,) + pieces[0].shape, f32),
            pltpu.VMEM((2, 8, HD), f32),
        ],
        waits=waits,
    )


def packed_sums(groups, heads, places, dp, waits=()):
    slab = D // dp
    head_slab = HD // dp
    here = 0 if heads is None else heads.shape[1] // HD
    count = 4 * 2 * here
    rows = sum(-(-group.shape[0] // 8) * 8 for group in groups)

    def kernel(place_ref, *refs):
        scratch, by_head = refs[-2:]
        outs = refs[-4:-2]
        scratch[...] = jnp.zeros_like(scratch)
        if here:
            first = place_ref[dp] * 2 * here + place_ref[dp + 1] * here
            by_head[...] = jnp.zeros_like(by_head)
            for i in range(2):
                for h in range(here):
                    by_head[pl.ds(i * count + first + h, 1), :] = refs[len(groups)][
                        i : i + 1, h * HD : (h + 1) * HD
                    ]
        for j in range(dp):
            at = 0
            for ref in refs[: len(groups)]:
                scratch[j, at : at + ref.shape[0], :] = ref[:, j * slab : (j + 1) * slab]
                at += -(-ref.shape[0] // 8) * 8
            if here:
                scratch[j, at:, :head_slab] = by_head[:, j * head_slab : (j + 1) * head_slab]
        for i in range(dp):
            outs[i // (dp // 2)][i % (dp // 2)] = scratch[place_ref[i]]

    shape = (dp, rows + 2 * count, slab)
    return kernel_call(
        kernel,
        "packed_sums",
        [places],
        [*groups] + ([heads] if here else []),
        [shape_of((dp // 2,) + shape[1:], f32)] * 2,
        0,
        [pltpu.VMEM(shape, f32), pltpu.VMEM((max(2 * count, 8), HD), f32)],
        waits=waits,
    )


def per_device(
    hidden_in,
    cotangent,
    segment_ids,
    expert_ids,
    first_gain,
    query_weight,
    key_weight,
    value_weight,
    output_weight,
    query_gain,
    key_gain,
    second_gain,
    router_weight,
    gate_weight,
    up_weight,
    down_weight,
):
    data_size = lax.axis_size("dp")
    tensor_size = lax.axis_size("tp")
    half = data_size // 2
    seq_len, width = hidden_in.shape
    share = seq_len // tensor_size
    slab = width // data_size
    me_dp, me_tp = lax.axis_index("dp"), lax.axis_index("tp")
    upper = me_dp // 2 % 2
    own = lambda values: lax.dynamic_slice_in_dim(values, me_tp * share, share, 0)
    local_experts = E // data_size
    first_expert = (me_dp * local_experts).astype(jnp.int32).reshape(1)
    here = jnp.stack([me_tp, upper]).astype(jnp.int32)
    places = jnp.concatenate([owners(weight_masks()), here])
    token_order = [weight_masks().index(mask) for mask in token_masks()]

    hidden_own, cot_own = own(hidden_in), own(cotangent)
    heads_local, head_slab = query_gain.shape
    small = [
        router_weight.T,
        first_gain[None],
        second_gain[None],
        query_gain,
        key_gain,
        expert_ids.T.astype(bf16),
        segment_ids.astype(bf16),
    ]
    small_rows = [array.shape[0] for array in small]
    wide = [jnp.pad(array, ((0, 0), (0, seq_len - array.shape[1]))) for array in small]
    small = gather_dp(jnp.concatenate(wide))
    column_half = heads_local * HD // 2
    kept, given = split_heads([query_weight, key_weight, value_weight], here)
    head_line = gather_line([kept, over_z(given, 1)], z_bits()[1:])
    head_pieces = head_line + [over_y(v) for v in head_line]
    cot_line = gather_dp(cot_own.astype(bf16))
    output_pieces = gather_dp(held([output_weight], bf16, [head_line[-1]]))
    router, gain_one, gain_two, gains, table, bias = unpack(
        small,
        places,
        small_rows,
        local_experts,
        heads_local,
        heads_local // 2,
        token_order,
        waits=[head_line[1]],
    )
    tables = rope_tables(seq_len, HD)
    first_scale = lax.rsqrt(jnp.mean(hidden_in * hidden_in, axis=-1, keepdims=True) + epsilon)
    normed_one = (hidden_in * first_scale * gain_one).astype(bf16)
    mates = gather_tp(over_z(own(normed_one), 1))
    x_slabs = paired([normed_one], mates, places, data_size)
    cot_near = held(cot_line, bf16, [mates[2]])
    cot_far = over_x(cot_near)
    projected, values, squares = project(
        x_slabs, head_pieces, places
    )
    squares = reduce_heads(squares)
    turned_rows, logs, attended, keep, give = attend(
        projected, squares, values, gains, tables, bias, places, data_size, waits=output_pieces[:half]
    )
    parts = output_project(keep, over_z(give, 1), output_pieces, places)
    middle, x_piece, probs = route(scatter_tp(parts)[0], hidden_own, gain_two, router)

    picks = (slice(0, half), slice(half, None))
    cot_far = held([cot_far], bf16, [x_piece])
    cot_all = [cot_near, over_core(cot_near), cot_far, over_core(cot_far)]
    cot_rows = rows_of_slots(cot_all, table, [], token_order)
    hidden_grad = grad_of_hidden(cot_rows, down_weight)
    x_pieces = gather_all(x_piece, [cot_rows], [hidden_grad])
    x_first = rows_of_slots(x_pieces[picks[0]], table[picks[0]], [hidden_grad])
    x_halves = [x_first, rows_of_slots(x_pieces[picks[1]], table[picks[1]], [x_first])]
    back_rows, act, gate_grad, up_grad = expert_step(
        x_halves, gate_weight, up_weight, hidden_grad, first_expert
    )
    second = tokens_of_slots(back_rows, table[picks[1]], half, [])
    first = tokens_of_slots(back_rows, table[picks[0]], 0, [second[0]])
    back = TokenSums(first, second).start()
    out_rows = expert_out(act, down_weight, back.sent)
    out_second = tokens_of_slots(out_rows, table[picks[1]], half, [])
    back.turn(out_second[0])
    out_first = tokens_of_slots(out_rows, table[picks[0]], 0, back.sent)
    chunk = max(local_experts // 4, 1)
    grads = []

    def some_grads(i, *waits):
        *grads[:], mark = expert_weight_grads(
            x_halves, cot_rows, act, gate_grad, up_grad, i * chunk, chunk, list(grads), waits
        )
        return mark

    mark = some_grads(0, out_first[0])
    back.top(mark)
    moe = TokenSums(out_first, out_second).start(*back.sent)
    mark = some_grads(1, mark, *moe.sent)
    back = back.last(mark)

    grad_middle, grad_low, router_sum, gain_sum = route_back(
        back, middle, x_piece, probs, cot_own, gain_two, router, waits=moe.came
    )
    low_pieces = gather_tp(grad_low)
    keep, give = output_back(low_pieces, output_pieces, places, [])
    moe.turn(keep)
    grad_values, gqk, inner, gain_sums = attend_back(
        keep, over_z(give, 1), places, data_size, turned_rows, logs, projected, squares, gains, tables, bias,
        [],
    )
    moe.top(gain_sums)
    inner = reduce_heads(inner)
    grad_queries, grad_keys = norm_back(gqk, projected, squares, inner, waits=moe.turned)
    head_grads = [grad_queries, grad_keys, grad_values]
    head_sums_at = WeightSums(*weight_parts(x_slabs, head_grads, places, True))
    parts = project_back(head_grads, head_pieces, places, waits=[head_sums_at.sent])
    terms, crossing = scatter_tp(parts)
    for_mate = combined([term[share:] for term in terms], 0)
    from_mate = over_z(for_mate, 1)
    head_sums_at.along_z(moe.from_top)
    mates_low = over_z(held(low_pieces, bf16, [for_mate]), 1)
    mark = some_grads(2, mark, head_sums_at.sent)
    moe = moe.last(head_sums_at.sent)
    low_slabs = paired(low_pieces, [mates_low], places, data_size)
    output_parts = weight_parts(
        low_slabs, [attended], places, False, waits=[head_sums_at.sent]
    )
    output_sums = WeightSums(*output_parts)
    grad_hidden, first_sum = hidden_back(terms, from_mate, hidden_own, grad_middle, gain_one)
    late = packed_sums(
        [router_sum[:E], gain_sum, first_sum],
        gain_sums,
        places,
        data_size,
        [head_sums_at.sent],
    )
    grad_hidden = gather_tp(grad_hidden)
    output_sums.along_z(mark)
    mark = some_grads(3, mark, output_sums.sent)
    head_sums_at.to_mate(output_sums.sent)
    output_sums.to_mate(head_sums_at.sent)
    total = reduce_all(*late)
    grad_hidden = absolute_tp(grad_hidden)
    hidden_out = absolute_tp(gather_tp(combined([middle, *moe], 0, sent=f32)))
    late = total[E + 8 :]
    head_sums = late[8:, :head_slab].reshape(2, heads_local * tensor_size, head_slab)
    head_sums = lax.dynamic_slice_in_dim(head_sums, me_tp * heads_local, heads_local, 1)
    grad_query, grad_key, grad_value = head_sums_at.in_order(here, 3, output_sums.sent)
    (grad_output,) = output_sums.in_order(here, 0)
    return (
        hidden_out,
        grad_hidden,
        late[0],
        grad_query,
        grad_key,
        grad_value,
        grad_output,
        head_sums[0],
        head_sums[1],
        total[E],
        total[:E].T,
        *grads,
    )


def solution(mesh):
    return jax.shard_map(
        per_device,
        mesh=mesh,
        in_specs=(
            P("dp", None),
            P("dp", None),
            P("dp", None),
            P("dp", None),
            P("dp"),
            P("dp", "tp"),
            P("dp", "tp"),
            P("dp", "tp"),
            P("tp", "dp"),
            P("tp", "dp"),
            P("tp", "dp"),
            P("dp"),
            P("dp", None),
            P("dp", None, "tp"),
            P("dp", None, "tp"),
            P("dp", "tp", None),
        ),
        out_specs=(
            P("dp", None),
            P("dp", None),
            P("dp"),
            P("dp", "tp"),
            P("dp", "tp"),
            P("dp", "tp"),
            P("tp", "dp"),
            P("tp", "dp"),
            P("tp", "dp"),
            P("dp"),
            P("dp", None),
            P("dp", None, "tp"),
            P("dp", None, "tp"),
            P("dp", "tp", None),
        ),
        check_vma=False,
    )
```

```python
import math

import jax
import jax.numpy as jnp
from jax import lax
from jax.experimental import pallas as pl
from jax.experimental.pallas import tpu as pltpu
from jax.sharding import PartitionSpec as P

D = 2048
HD = 128
E = 64
TOPK = 8
CAP = 48
EXTRA = 2 * E

bf16 = jnp.bfloat16
f32 = jnp.float32

epsilon = 1e-05


def cost(flops, bytes_accessed, transcendentals):
    return pl.CostEstimate(
        flops=flops // 1000000, bytes_accessed=bytes_accessed // 1000000, transcendentals=0
    )


def swap(values, dp_bits, tp_bits):
    dp, tp = lax.axis_size("dp"), lax.axis_size("tp")
    pairs = [
        (a * tp + b, (a ^ dp_bits) * tp + (b ^ tp_bits)) for a in range(dp) for b in range(tp)
    ]
    return lax.ppermute(values, ("dp", "tp"), pairs)


def over_z(values, bits):
    return swap(values, 2 * bits, 0)


def over_y(values):
    return swap(values, 1, 0)


def over_x(values):
    return swap(values, 0, 2)


def over_core(values):
    return swap(values, 0, 1)


def z_bits():
    half = lax.axis_size("dp") // 2
    return [1 << i for i in range(half.bit_length() - 1)]


def masks_of(bits):
    masks = [0]
    for bit in bits:
        masks = masks + [mask ^ bit for mask in masks]
    return masks


def weight_masks():
    return masks_of([2 * bit for bit in z_bits()] + [1])


def token_masks():
    return masks_of([2 * bit for bit in z_bits()[:-1]] + [1, 2 * z_bits()[-1]])


def owners(masks):
    return lax.axis_index("dp") ^ jnp.array(masks, jnp.int32)


def gather_line(pieces, bits):
    for bit in bits:
        pieces = pieces + [over_z(v, bit) for v in pieces]
    return pieces


def gather_dp(values):
    line = gather_line([values], z_bits())
    return line + [over_y(v) for v in line]


def gather_all(values, first_wait, second_wait):
    *bits, high = z_bits()
    line = gather_line([values], bits)
    going = [values] + [held([v], v.dtype, first_wait) for v in line[1:]]
    over = [over_z(v, high) for v in going]
    line = line + over[:-1] + [held(over[-1:], values.dtype, second_wait)]
    pairs = {}
    for mask, near in zip(masks_of([2 * bit for bit in z_bits()]), line, strict=True):
        if mask & 2 * high:
            aside = over_x(near)
            pairs[mask], pairs[mask + 1] = (near, aside), (over_y(near), over_y(aside))
        else:
            across = over_y(near)
            pairs[mask], pairs[mask + 1] = (near, over_x(near)), (across, over_x(across))
    return [
        (pairs[m][0], over_core(pairs[m][0]), pairs[m][1], over_core(pairs[m][1]))
        for m in token_masks()
    ]


def gather_tp(values):
    other = over_x(values)
    return [values, over_core(values), other, over_core(other)]


def sorted_by_bits(pieces, me):
    bit = 1
    while bit < len(pieces):
        odd = me & bit != 0
        pieces = [jnp.where(odd, pieces[i ^ bit], pieces[i]) for i in range(len(pieces))]
        bit *= 2
    return pieces


def absolute_dp(pieces):
    dp = len(pieces)
    by_mask = [pieces[i // 2 + i % 2 * (dp // 2)] for i in range(dp)]
    return jnp.stack(sorted_by_bits(by_mask, lax.axis_index("dp")))


def absolute_tp(pieces, axis=0):
    return jnp.concatenate(sorted_by_bits(list(pieces), lax.axis_index("tp")), axis=axis)


def added(*terms):
    total = terms[0].astype(f32)
    for term in terms[1:]:
        total = total + term.astype(f32)
    return total


def combined(terms, cut, waits=(), sent=bf16):
    shape = terms[0].shape
    outs = [shape_of((shape[0] - cut,) + shape[1:], sent)]
    if cut:
        outs.insert(0, shape_of((cut,) + shape[1:], f32))

    def kernel(*refs):
        for out, part in zip(refs[len(terms) :], (slice(0, cut), slice(cut, None))[-len(outs) :]):
            out[...] = added(*[ref[part] for ref in refs[: len(terms)]]).astype(out.dtype)

    result = kernel_call(kernel, "combined", [], list(terms), outs, 0, waits=waits)
    return result if cut else result[0]


def held(arrays, dtype, waits):
    def kernel(*refs):
        at = 0
        for ref in refs[:-1]:
            refs[-1][at : at + ref.shape[0], :] = ref[...].astype(dtype)
            at += ref.shape[0]

    rows = sum(array.shape[0] for array in arrays)
    out = shape_of((rows, arrays[0].shape[1]), dtype)
    return kernel_call(kernel, "held", [], list(arrays), [out], 0, waits=waits)[0]


def scatter_tp(parts):
    mine, far = over_core(parts[1]), over_core(parts[3])
    crossing = combined([parts[2], far], 0)
    return (parts[0], mine, over_x(crossing)), crossing


class TokenSums:
    def __init__(self, first, second):
        self.mid = first[0].shape[0] // 2
        self.first, self.second = first, second
        self.first_core = [over_core(first[1]), over_core(first[3])]
        self.second_core = [over_core(second[1]), over_core(second[3])]

    def start(self, *others):
        first, second = self.first, self.second
        self.b0, b0_far = combined([second[0], self.second_core[0]], self.mid, others)
        self.b1, b1_far = combined([second[2], self.second_core[1]], self.mid, others)
        a1 = combined([first[2], self.first_core[1]], 0, others)
        self.sent = [b0_far, b1_far, a1]
        self.came = [over_y(b0_far), over_y(b1_far), over_x(a1)]
        return self

    def turn(self, *others):
        b = combined([self.b1, self.came[1]], 0, others)
        self.a, a = combined([self.first[0], self.first_core[0], self.came[2]], self.mid, others)
        self.sent = [b, a]
        self.turned = [over_x(b), over_y(a)]
        return self

    def top(self, *others):
        self.sent = [combined([self.b0, self.came[0], self.turned[0]], 0, others)]
        self.from_top = over_z(self.sent[0], z_bits()[-1])
        return self

    def last(self, *others):
        terms = [self.a, self.turned[1], self.from_top]
        for bit in reversed(z_bits()[:-1]):
            near, sent = combined(terms, terms[0].shape[0] // 2, others if bit == 1 else ())
            terms = [near, over_z(sent, bit)]
        self.sent = [sent]
        return terms


def reduce_all(near, far, waits):
    terms = [near, over_y(far)]
    for bit in reversed(z_bits()):
        near, sent = combined(terms, bit, waits, sent=f32)
        terms = [near, over_z(sent, bit)]
    return reduce_tp(added(*terms)[0])


def reduce_tp(values):
    values = values + over_core(values)
    return values + over_x(values)


def reduce_heads(values):
    return reduce_tp(values + over_z(values, 1))


class WeightSums:
    def __init__(self, near, far):
        self.near, self.sent = near, far
        self.came = over_y(far)

    def along_z(self, *others):
        for bit in reversed(z_bits()[1:]):
            self.near, self.sent = combined([self.near, self.came], bit, others)
            self.came = over_z(self.sent, bit)
        return self

    def to_mate(self, *others):
        self.near, self.sent = combined([self.near, self.came], 1, others)
        self.came = over_z(self.sent, 1)
        return self

    def in_order(self, here, count, *others):
        _, rows, columns = self.near.shape
        size = columns // count if count else rows
        shape = (rows, 2 * size) if count else (2 * rows, columns)

        def kernel(here_ref, mine_ref, other_ref, *outs):
            for ref, which in ((mine_ref, here_ref[1]), (other_ref, 1 - here_ref[1])):
                part = pl.ds(pl.multiple_of(which * size, size), size)
                for j, out in enumerate(outs):
                    if count:
                        out[:, part] = ref[0, :, j * size : (j + 1) * size].astype(f32)
                    else:
                        out[part, :] = ref[0].astype(f32)

        return kernel_call(
            kernel,
            "in_order",
            [here],
            [self.near, self.came],
            [shape_of(shape, f32)] * max(count, 1),
            0,
            waits=others,
        )


def chosen_slots(table):
    experts, tokens = table.shape
    place = lax.broadcasted_iota(jnp.int32, (experts, CAP, tokens), 1)
    hit = place == table[:, None, :]
    return jnp.where(hit, 1.0, 0.0).astype(bf16).reshape(experts * CAP, tokens)


def rows_of_slots(pieces, table, waits, order=None):
    sequences, experts, tokens = table.shape
    if order is None:
        flat = [piece for group in pieces for piece in group]
        share, width = flat[0].shape
    else:
        flat = pieces
        share, width = tokens // 4, pieces[0].shape[1]
    count = sequences * 4

    def kernel(*refs):
        table_ref, *sources = refs[:-3]
        out_ref, buffer, arrived = refs[-3:]
        step = pl.program_id(0)

        def piece(i):
            if order is None:
                return sources[i]
            return sources[i % 4].at[pl.ds(order[i // 4] * share, share), :]

        @pl.when(step == 0)
        def _():
            for i in range(count):
                pltpu.make_async_copy(
                    piece(i), buffer.at[i // 4, pl.ds(i % 4 * share, share)], arrived.at[i]
                ).start()

        for i in range(4):
            pltpu.make_async_copy(
                piece(i), buffer.at[step, pl.ds(i * share, share)], arrived.at[step * 4 + i]
            ).wait()
        picked = jnp.dot(chosen_slots(table_ref[0]), buffer[step], preferred_element_type=f32)
        out_ref[...] = picked.astype(bf16).reshape(experts, CAP, width)

    return pl.pallas_call(
        without(kernel, 1 + len(flat), len(waits)),
        grid=(sequences,),
        in_specs=[pl.BlockSpec((1, experts, tokens), lambda s: (s, 0, 0))]
        + [pl.BlockSpec(memory_space=pltpu.HBM)] * len(flat)
        + [pl.BlockSpec(memory_space=pl.ANY)] * len(waits),
        out_specs=pl.BlockSpec((experts, CAP, width), lambda s: (0, s, 0)),
        out_shape=jax.ShapeDtypeStruct((experts, sequences * CAP, width), bf16),
        scratch_shapes=[
            pltpu.VMEM((sequences, tokens, width), bf16),
            pltpu.SemaphoreType.DMA((count,)),
        ],
        compiler_params=pltpu.CompilerParams(vmem_limit_bytes=48 << 20),
        cost_estimate=cost(
            flops=2 * experts * CAP * sequences * tokens * width,
            bytes_accessed=2 * sequences * (tokens + experts * CAP) * width,
            transcendentals=0,
        ),
        name="rows_of_slots",
    )(table, *flat, *waits)


def tokens_of_slots(rows, table, first, waits):
    sequences, experts, tokens = table.shape
    width = rows.shape[-1]
    share = tokens // 4

    def kernel(table_ref, rows_ref, *outs):
        picked = chosen_slots(table_ref[0])
        total = lax.dot_general(
            picked,
            rows_ref[...].reshape(experts * CAP, width),
            (((0,), (0,)), ((), ())),
            preferred_element_type=f32,
        ).astype(bf16)
        for q, out in enumerate(outs):
            out[...] = total[q * share : (q + 1) * share]

    return pl.pallas_call(
        without(kernel, 2, len(waits)),
        grid=(sequences,),
        in_specs=[
            pl.BlockSpec((1, experts, tokens), lambda s: (s, 0, 0)),
            pl.BlockSpec((experts, CAP, width), lambda s: (0, s + first, 0)),
        ]
        + [pl.BlockSpec(memory_space=pl.ANY)] * len(waits),
        out_specs=[pl.BlockSpec((share, width), lambda s: (s, 0))] * 4,
        out_shape=[jax.ShapeDtypeStruct((sequences * share, width), bf16)] * 4,
        compiler_params=pltpu.CompilerParams(vmem_limit_bytes=48 << 20),
        cost_estimate=cost(
            flops=2 * experts * CAP * sequences * tokens * width,
            bytes_accessed=2 * sequences * (tokens + experts * CAP) * width,
            transcendentals=0,
        ),
        name="tokens_of_slots",
    )(table, rows, *waits)


def dot_last(a, b):
    return lax.dot_general(a, b, (((1,), (1,)), ((), ())), preferred_element_type=f32)


def dot_first(a, b):
    return lax.dot_general(a, b, (((0,), (0,)), ((), ())), preferred_element_type=f32)


def per_expert(kernel, experts, ins, outs, flops, name, scalars=(), waits=()):
    whole = lambda shape: pl.BlockSpec((1,) + tuple(shape[1:]), lambda e: (e, 0, 0))
    in_specs = [pl.BlockSpec(memory_space=pltpu.SMEM)] * len(scalars)
    moved = 0
    for array, block in ins:
        in_specs.append(pl.BlockSpec((1,) + block, lambda e: (e, 0, 0)))
        moved += experts * math.prod(block) * array.dtype.itemsize
    moved += sum(math.prod(o.shape) * o.dtype.itemsize for o in outs)
    return pl.pallas_call(
        without(kernel, len(in_specs), len(waits)),
        grid=(experts,),
        in_specs=in_specs + [pl.BlockSpec(memory_space=pl.ANY)] * len(waits),
        out_specs=[whole(o.shape) for o in outs],
        out_shape=list(outs),
        compiler_params=pltpu.CompilerParams(vmem_limit_bytes=48 << 20),
        cost_estimate=cost(flops=flops, bytes_accessed=moved, transcendentals=0),
        name=name,
    )(*scalars, *[array for array, _ in ins], *waits)


def grad_of_hidden(cot_rows, down_weight):
    experts, rows, width = cot_rows.shape
    hidden = down_weight.shape[1]

    def kernel(cot_ref, down_ref, out_ref):
        out_ref[0] = dot_last(cot_ref[0], down_ref[0])

    return per_expert(
        kernel,
        experts,
        [(cot_rows, (rows, width)), (down_weight, (hidden, width))],
        [jax.ShapeDtypeStruct((experts, rows, hidden), f32)],
        2 * experts * rows * width * hidden,
        "grad_of_hidden",
    )[0]


def expert_step(x_halves, gate_weight, up_weight, hidden_grad, first_expert):
    experts, half_rows, wide = x_halves[0].shape
    rows = half_rows * 2
    width, hidden = gate_weight.shape[1:]

    def kernel(base_ref, a_ref, b_ref, gate_ref, up_ref, grad_ref, back_ref, act_ref, gate_grad_ref, up_grad_ref):
        mine = base_ref[0] + pl.program_id(0)
        x = jnp.concatenate([a_ref[0, :, :width], b_ref[0, :, :width]])
        lane = lax.broadcasted_iota(jnp.int32, (rows, EXTRA), 1)
        probs = jnp.concatenate([a_ref[0, :, width:], b_ref[0, :, width:]]).astype(f32)
        mix = jnp.sum(
            jnp.where((lane == mine) | (lane == mine + E), probs, 0.0), axis=1, keepdims=True
        )
        gate_act = jnp.dot(x, gate_ref[0], preferred_element_type=f32)
        up_act = jnp.dot(x, up_ref[0], preferred_element_type=f32)
        raw = grad_ref[0]
        sig = jax.nn.sigmoid(gate_act)
        silu = gate_act * sig
        act = silu * up_act
        grad_mix = jnp.sum(act * raw, axis=1, keepdims=True)
        act_ref[0] = (mix * act).astype(bf16)
        weighted = mix * raw
        gate_grad = (weighted * up_act * sig * (1.0 + gate_act * (1.0 - sig))).astype(bf16)
        up_grad = (weighted * silu).astype(bf16)
        gate_grad_ref[0] = gate_grad
        up_grad_ref[0] = up_grad
        back_ref[0, :, :width] = (
            dot_last(gate_grad, gate_ref[0]) + dot_last(up_grad, up_ref[0])
        ).astype(bf16)
        coarse = grad_mix.astype(bf16).astype(f32)
        fine = grad_mix - coarse
        back_ref[0, :, width:] = jnp.where(
            lane == mine, coarse, jnp.where(lane == mine + E, fine, 0.0)
        ).astype(bf16)

    small = jax.ShapeDtypeStruct((experts, rows, hidden), bf16)
    return per_expert(
        kernel,
        experts,
        [
            (x_halves[0], (half_rows, wide)),
            (x_halves[1], (half_rows, wide)),
            (gate_weight, (width, hidden)),
            (up_weight, (width, hidden)),
            (hidden_grad, (rows, hidden)),
        ],
        [jax.ShapeDtypeStruct((experts, rows, wide), bf16), small, small, small],
        8 * experts * rows * width * hidden,
        "expert_step",
        (first_expert,),
    )


def expert_out(act, down_weight, waits):
    experts, rows, hidden = act.shape
    width = down_weight.shape[2]

    def kernel(act_ref, down_ref, out_ref):
        out_ref[0] = jnp.dot(act_ref[0], down_ref[0], preferred_element_type=f32).astype(bf16)

    return per_expert(
        kernel,
        experts,
        [(act, (rows, hidden)), (down_weight, (hidden, width))],
        [jax.ShapeDtypeStruct((experts, rows, width), bf16)],
        2 * experts * rows * width * hidden,
        "expert_out",
        waits=waits,
    )[0]


def expert_weight_grads(x_halves, cot_rows, act, gate_grad, up_grad, first, count, into, waits):
    experts, rows, hidden = act.shape
    width = cot_rows.shape[2]

    def kernel(a_ref, b_ref, cot_ref, act_ref, gate_ref, up_ref, *refs):
        gate_out, up_out, down_out, mark = refs[-4:]
        mark[...] = jnp.zeros_like(mark)
        x = jnp.concatenate([a_ref[0], b_ref[0]])
        gate_out[0] = dot_first(x, gate_ref[0])
        up_out[0] = dot_first(x, up_ref[0])
        down_out[0] = dot_first(act_ref[0], cot_ref[0])

    block = lambda *shape: pl.BlockSpec((1,) + shape, lambda e: (e + first, 0, 0))
    ins = [*x_halves, cot_rows, act, gate_grad, up_grad]
    return pl.pallas_call(
        kernel,
        grid=(count,),
        in_specs=[block(rows // 2, width)] * 2
        + [block(rows, width)]
        + [block(rows, hidden)] * 3
        + [pl.BlockSpec(memory_space=pl.ANY)] * (len(into) + len(waits)),
        out_specs=[block(width, hidden), block(width, hidden), block(hidden, width)]
        + [pl.BlockSpec((8, 128), lambda e: (0, 0))],
        out_shape=[
            jax.ShapeDtypeStruct((experts, width, hidden), f32),
            jax.ShapeDtypeStruct((experts, width, hidden), f32),
            jax.ShapeDtypeStruct((experts, hidden, width), f32),
            jax.ShapeDtypeStruct((8, 128), f32),
        ],
        input_output_aliases={len(ins) + i: i for i in range(len(into))},
        compiler_params=pltpu.CompilerParams(vmem_limit_bytes=48 << 20),
        cost_estimate=cost(
            flops=6 * count * rows * width * hidden,
            bytes_accessed=count * (4 * rows * (width + hidden) + 12 * width * hidden),
            transcendentals=0,
        ),
        name="expert_weight_grads",
    )(*ins, *into, *waits)


def without(kernel, start, count):
    return lambda *refs: kernel(*refs[:start], *refs[start + count :])


def kernel_call(kernel, name, scalars, ins, outs, flops, scratch=(), waits=()):
    moved = sum(a.size * a.dtype.itemsize for a in ins)
    moved += sum(math.prod(o.shape) * o.dtype.itemsize for o in outs)
    large = [i for i, a in enumerate(ins) if a.size * a.dtype.itemsize >= 1 << 16]
    first, last = len(scalars), len(scalars) + len(ins)
    made = last + len(waits)

    def body(*refs):
        given = list(refs[first:last])
        kept = made + len(outs) + len(scratch)
        copies = []
        for k, i in enumerate(large):
            copies.append(pltpu.make_async_copy(given[i], refs[kept + k], refs[-1].at[k]))
            copies[-1].start()
            given[i] = refs[kept + k]
        for copy in copies:
            copy.wait()
        kernel(*refs[:first], *given, *refs[made:kept])

    places = [pl.ANY if i in large else pltpu.VMEM for i in range(len(ins))]
    return pl.pallas_call(
        body,
        in_specs=[pl.BlockSpec(memory_space=pltpu.SMEM)] * len(scalars)
        + [pl.BlockSpec(memory_space=place) for place in places]
        + [pl.BlockSpec(memory_space=pl.ANY)] * len(waits),
        out_specs=[pl.BlockSpec(memory_space=pltpu.VMEM)] * len(outs),
        out_shape=list(outs),
        scratch_shapes=list(scratch)
        + [pltpu.VMEM(ins[i].shape, ins[i].dtype) for i in large]
        + [pltpu.SemaphoreType.DMA((max(len(large), 1),))],
        compiler_params=pltpu.CompilerParams(vmem_limit_bytes=40 << 20),
        cost_estimate=cost(flops=flops, bytes_accessed=moved, transcendentals=0),
        name=name,
    )(*scalars, *ins, *waits)


def shape_of(shape, dtype):
    return jax.ShapeDtypeStruct(shape, dtype)


def row_of(place_ref, dp, tokens, share, q, mate):
    which = (1 - place_ref[dp + 1]) if mate else place_ref[dp + 1]
    return pl.multiple_of(which * tokens + (place_ref[dp] ^ q) * share, share)


def split_heads(weights, here):
    rows, columns = weights[0].shape
    half = columns // 2

    def kernel(here_ref, *refs):
        keep_ref, give_ref, scratch = refs[len(weights) :]
        for j, ref in enumerate(refs[: len(weights)]):
            for i in range(2):
                scratch[i, :, j * half : (j + 1) * half] = ref[:, i * half : (i + 1) * half]
        keep_ref[...] = scratch[here_ref[1]]
        give_ref[...] = scratch[1 - here_ref[1]]

    shape = (rows, half * len(weights))
    return kernel_call(
        kernel,
        "split_heads",
        [here],
        list(weights),
        [shape_of(shape, bf16)] * 2,
        0,
        [pltpu.VMEM((2,) + shape, bf16)],
    )


def paired(own, mates, places, dp):
    share, width = mates[0].shape
    if len(mates) == 1:
        share = share // 4
    tokens = 4 * share
    slab = width // dp

    def kernel(place_ref, *refs):
        out_ref = refs[-1]
        if len(own) == 1:
            start = pl.multiple_of(place_ref[dp + 1] * tokens, tokens)
            for i in range(dp):
                out_ref[i, pl.ds(start, tokens), :] = refs[0][:, i * slab : (i + 1) * slab]
        for q in range(4):
            sources = []
            if len(own) == 4:
                sources.append((refs[q][...], False))
            if len(mates) == 4:
                sources.append((refs[len(own) + q][...], True))
            else:
                sources.append((refs[len(own)][q * share : (q + 1) * share, :], True))
            for rows, mate in sources:
                start = row_of(place_ref, dp, tokens, share, q, mate)
                for i in range(dp):
                    out_ref[i, pl.ds(start, share), :] = rows[:, i * slab : (i + 1) * slab]

    return kernel_call(
        kernel, "paired", [places], [*own, *mates], [shape_of((dp, 2 * tokens, slab), bf16)], 0
    )[0]


def as_rows(first, second):
    lane = lax.broadcasted_iota(jnp.int32, (first.shape[0], 128), 1)
    return jnp.where(lane < 4, first, second).T[:8]


def as_columns(pair):
    wide = jnp.concatenate([pair] * 16).T
    return wide[:, 0:1], wide[:, 4:5]


def project(x_slabs, pieces, places):
    dp, tokens, _ = x_slabs.shape
    columns = pieces[0].shape[1] // 3

    def kernel(place_ref, x_ref, *refs):
        totals = []
        for j in range(3):
            total = None
            for i in range(dp):
                part = jnp.dot(
                    x_ref[place_ref[i]],
                    refs[i][:, j * columns : (j + 1) * columns],
                    preferred_element_type=f32,
                )
                total = part if total is None else total + part
            totals.append(total)
        queries, keys, values = totals
        qk_out, v_out, squares_out = refs[dp:]
        qk_out[0] = queries
        qk_out[1] = keys
        v_out[...] = values.astype(bf16)
        squares_out[...] = as_rows(
            jnp.sum(queries * queries, axis=1, keepdims=True),
            jnp.sum(keys * keys, axis=1, keepdims=True),
        )

    return kernel_call(
        kernel,
        "project",
        [places],
        [x_slabs, *pieces],
        [
            shape_of((2, tokens, columns), f32),
            shape_of((tokens, columns), bf16),
            shape_of((8, tokens), f32),
        ],
        6 * x_slabs.size * columns,
    )


def turned(values):
    return pltpu.roll(values, HD // 2, 1)


def attend(projected, squares, values, gains, tables, bias, places, dp, waits=()):
    _, rows, columns = projected.shape
    tokens = rows // 2
    heads = columns // HD
    lanes = 128 // heads

    def kernel(place_ref, qk_ref, sq_ref, v_ref, gain_ref, table_ref, bias_ref, *refs):
        turned_out, log_out, att_out, keep_out, give_out = refs
        turned_out[2] = v_ref[...]
        cosine, sine = table_ref[0], table_ref[1]
        lane = lax.broadcasted_iota(jnp.int32, (tokens, 128), 1)
        q_squares, k_squares = as_columns(sq_ref[...])
        for which in range(2):
            row = slice(which * tokens, (which + 1) * tokens)
            q_scale = lax.rsqrt(q_squares[row] / D + epsilon)
            k_scale = lax.rsqrt(k_squares[row] / D + epsilon)
            logs = jnp.zeros((tokens, 128), f32)
            for h in range(heads):
                cut = slice(h * HD, (h + 1) * HD)
                q = qk_ref[0, row, cut] * q_scale * gain_ref[0:1, cut]
                k = qk_ref[1, row, cut] * k_scale * gain_ref[1:2, cut]
                q = (q * cosine + turned(q) * sine).astype(bf16)
                k = (k * cosine + turned(k) * sine).astype(bf16)
                turned_out[0, row, cut] = q
                turned_out[1, row, cut] = k
                scores = dot_last(q, k) * (1.0 / math.sqrt(HD)) + bias_ref[which]
                largest = jnp.max(scores, axis=1, keepdims=True)
                raised = jnp.exp(scores - largest)
                total = jnp.sum(raised, axis=1, keepdims=True)
                logs = jnp.where(lane // lanes == h, largest + jnp.log(total), logs)
                probs = (raised / total).astype(bf16)
                att_out[row, cut] = jnp.dot(
                    probs, v_ref[row, cut], preferred_element_type=f32
                ).astype(bf16)
            log_out[row, :] = logs
        upper = place_ref[dp + 1]
        keep_out[...] = att_out[pl.ds(pl.multiple_of(upper * tokens, tokens), tokens), :]
        give_out[...] = att_out[pl.ds(pl.multiple_of((1 - upper) * tokens, tokens), tokens), :]

    part = shape_of((tokens, columns), bf16)
    return kernel_call(
        kernel,
        "attend",
        [places],
        [projected, squares, values, gains, tables, bias],
        [
            shape_of((3, rows, columns), bf16),
            shape_of((rows, 128), f32),
            shape_of((rows, columns), bf16),
            part,
            part,
        ],
        4 * tokens * rows * columns,
        waits=waits,
    )


def output_project(keep, got, pieces, places, waits=()):
    tokens, columns = keep.shape
    dp = len(pieces)
    slab = pieces[0].shape[1]
    share = tokens // 4

    def kernel(place_ref, keep_ref, got_ref, *refs):
        weights, parts, scratch = refs[:dp], refs[dp:-1], refs[-1]
        upper = place_ref[dp + 1]
        mine = pl.ds(pl.multiple_of(upper * columns, columns), columns)
        other = pl.ds(pl.multiple_of((1 - upper) * columns, columns), columns)
        for i in range(dp):
            scratch[place_ref[i]] = (
                jnp.dot(keep_ref[...], weights[i][mine, :], preferred_element_type=f32)
                + jnp.dot(got_ref[...], weights[i][other, :], preferred_element_type=f32)
            ).astype(bf16)
        for q, part in enumerate(parts):
            start = pl.multiple_of((place_ref[dp] ^ q) * share, share)
            for i in range(dp):
                part[:, i * slab : (i + 1) * slab] = scratch[i, pl.ds(start, share), :]

    return kernel_call(
        kernel,
        "output_project",
        [places],
        [keep, got, *pieces],
        [shape_of((share, slab * dp), bf16)] * 4,
        4 * tokens * columns * slab * dp,
        [pltpu.VMEM((dp, tokens, slab), bf16)],
        waits=waits,
    )


def route(terms, hidden, gain, router, waits=()):
    share, width = hidden.shape

    def kernel(a_ref, b_ref, c_ref, hidden_ref, gain_ref, router_ref, middle_ref, x_ref, probs_ref):
        middle = hidden_ref[...] + added(a_ref[...], b_ref[...], c_ref[...])
        middle_ref[...] = middle
        scale = lax.rsqrt(jnp.mean(middle * middle, axis=1, keepdims=True) + epsilon)
        normed = (middle * scale * gain_ref[...]).astype(bf16)
        x_ref[:, :width] = normed
        logits = dot_last(normed, router_ref[...])
        raised = jnp.exp(logits - jnp.max(logits, axis=1, keepdims=True))
        probs = raised / (0.5 * jnp.sum(raised, axis=1, keepdims=True))
        probs_ref[...] = probs
        coarse = probs.astype(bf16).astype(f32)
        lane = lax.broadcasted_iota(jnp.int32, probs.shape, 1)
        x_ref[:, width:] = jnp.where(lane < E, coarse, probs - coarse).astype(bf16)

    return kernel_call(
        kernel,
        "route",
        [],
        [*terms, hidden, gain, router],
        [
            shape_of((share, width), f32),
            shape_of((share, width + EXTRA), bf16),
            shape_of((share, EXTRA), f32),
        ],
        2 * share * width * EXTRA,
        waits=waits,
    )


def route_back(terms, middle, x_piece, probs, cotangent, gain, router, waits=()):
    share, width = middle.shape

    def kernel(a_ref, b_ref, middle_ref, x_ref, probs_ref, cot_ref, gain_ref, router_ref, *outs):
        grad_ref, low_ref, router_out, gain_out = outs
        pair = added(a_ref[:, width:], b_ref[:, width:])
        grad_probs = pair + pltpu.roll(pair, E, 1)
        probs = probs_ref[...]
        inner = 0.5 * jnp.sum(probs * grad_probs, axis=1, keepdims=True)
        grad_logits = probs * (grad_probs - inner)
        middle = middle_ref[...]
        scale = lax.rsqrt(jnp.mean(middle * middle, axis=1, keepdims=True) + epsilon)
        lane = lax.broadcasted_iota(jnp.int32, probs.shape, 1)
        once = jnp.where(lane < E, grad_logits, 0.0)
        normed_grad = added(a_ref[:, :width], b_ref[:, :width]) + lax.dot_general(
            once,
            router_ref[...].astype(f32),
            (((1,), (0,)), ((), ())),
            precision=lax.Precision.HIGHEST,
            preferred_element_type=f32,
        )
        router_out[...] = lax.dot_general(
            once,
            x_ref[:, :width].astype(f32),
            (((0,), (0,)), ((), ())),
            precision=lax.Precision.HIGHEST,
            preferred_element_type=f32,
        )
        gain_out[...] = jnp.sum(normed_grad * middle * scale, axis=0, keepdims=True)
        scaled = normed_grad * gain_ref[...]
        grad = (
            cot_ref[...]
            + scale * scaled
            - middle * (scale * scale * scale) * jnp.mean(scaled * middle, axis=1, keepdims=True)
        )
        grad_ref[...] = grad
        low_ref[...] = grad.astype(bf16)

    return kernel_call(
        kernel,
        "route_back",
        [],
        [*terms, middle, x_piece, probs, cotangent, gain, router],
        [
            shape_of((share, width), f32),
            shape_of((share, width), bf16),
            shape_of((EXTRA, width), f32),
            shape_of((1, width), f32),
        ],
        24 * share * width * EXTRA,
        waits=waits,
    )


def output_back(low_pieces, pieces, places, waits):
    dp = len(pieces)
    columns, slab = pieces[0].shape
    share = low_pieces[0].shape[0]
    tokens = 4 * share
    half = columns // 2

    def kernel(place_ref, *refs):
        lows, weights, (keep_ref, give_ref, scratch, both) = refs[:4], refs[4 : 4 + dp], refs[4 + dp :]
        for q, low in enumerate(lows):
            start = pl.multiple_of((place_ref[dp] ^ q) * share, share)
            for i in range(dp):
                scratch[i, pl.ds(start, share), :] = low[:, i * slab : (i + 1) * slab]
        total = None
        for i in range(dp):
            part = dot_last(scratch[place_ref[i]], weights[i][...])
            total = part if total is None else total + part
        both[0] = total[:, :half].astype(bf16)
        both[1] = total[:, half:].astype(bf16)
        upper = place_ref[dp + 1]
        keep_ref[...] = both[upper]
        give_ref[...] = both[1 - upper]

    return kernel_call(
        kernel,
        "output_back",
        [places],
        [*low_pieces, *pieces],
        [shape_of((tokens, half), bf16)] * 2,
        2 * tokens * columns * slab * dp,
        [pltpu.VMEM((dp, tokens, slab), bf16), pltpu.VMEM((2, tokens, half), bf16)],
        waits=waits,
    )


def attend_back(keep, got, places, dp, turned_rows, logs, projected, squares, gains, tables, bias, waits):
    _, rows, columns = projected.shape
    tokens = rows // 2
    heads = columns // HD
    lanes = 128 // heads

    def kernel(place_ref, keep_ref, got_ref, *refs):
        turned_ref, log_ref, qk_ref, sq_ref, gain_ref, table_ref, bias_ref = refs[:7]
        gv_ref, gqk_ref, inner_ref, gains_ref, scratch = refs[7:]
        upper = place_ref[dp + 1]
        scratch[upper] = keep_ref[...]
        scratch[1 - upper] = got_ref[...]
        cosine, sine = table_ref[0], table_ref[1]
        q_squares, k_squares = as_columns(sq_ref[...])
        for which in range(2):
            row = slice(which * tokens, (which + 1) * tokens)
            q_scale = lax.rsqrt(q_squares[row] / D + epsilon)
            k_scale = lax.rsqrt(k_squares[row] / D + epsilon)
            inner = [jnp.zeros((tokens, 1), f32), jnp.zeros((tokens, 1), f32)]
            for h in range(heads):
                cut = slice(h * HD, (h + 1) * HD)
                qr, kr, v = (turned_ref[i, row, cut] for i in range(3))
                grad = scratch[which, :, cut]
                scores = dot_last(qr, kr) * (1.0 / math.sqrt(HD)) + bias_ref[which]
                probs = jnp.exp(scores - log_ref[row, h * lanes : h * lanes + 1])
                gv_ref[row, cut] = dot_first(probs.astype(bf16), grad).astype(bf16)
                grad_probs = dot_last(grad, v)
                dots = jnp.sum(probs * grad_probs, axis=1, keepdims=True)
                grad_scores = (probs * (grad_probs - dots) * (1.0 / math.sqrt(HD))).astype(bf16)
                gq = jnp.dot(grad_scores, kr, preferred_element_type=f32)
                gk = dot_first(grad_scores, qr)
                gq = gq * cosine - turned(gq) * sine
                gk = gk * cosine - turned(gk) * sine
                q, k = qk_ref[0, row, cut], qk_ref[1, row, cut]
                for i, (grad_sum, value, scale) in enumerate(((gq, q, q_scale), (gk, k, k_scale))):
                    total = jnp.sum(grad_sum * value * scale, axis=0, keepdims=True)
                    if which:
                        total = total + gains_ref[i : i + 1, cut]
                    gains_ref[i : i + 1, cut] = total
                gq = gq * gain_ref[0:1, cut]
                gk = gk * gain_ref[1:2, cut]
                gqk_ref[0, row, cut] = gq
                gqk_ref[1, row, cut] = gk
                inner[0] = inner[0] + jnp.sum(gq * q, axis=1, keepdims=True)
                inner[1] = inner[1] + jnp.sum(gk * k, axis=1, keepdims=True)
            inner_ref[:, row] = as_rows(*inner)

    return kernel_call(
        kernel,
        "attend_back",
        [places],
        [keep, got, turned_rows, logs, projected, squares, gains, tables, bias],
        [
            shape_of((rows, columns), bf16),
            shape_of((2, rows, columns), f32),
            shape_of((8, rows), f32),
            shape_of((2, columns), f32),
        ],
        10 * tokens * rows * columns,
        [pltpu.VMEM((2, tokens, columns), bf16)],
        waits=waits,
    )


def norm_back(grads, projected, squares, inner, waits=()):
    _, tokens, columns = projected.shape

    def kernel(grad_ref, value_ref, sq_ref, inner_ref, *outs):
        squares, inners = as_columns(sq_ref[...]), as_columns(inner_ref[...])
        for i, out in enumerate(outs):
            scale = lax.rsqrt(squares[i] / D + epsilon)
            mean = inners[i] / D
            out[...] = (
                scale * grad_ref[i] - value_ref[i] * (scale * scale * scale) * mean
            ).astype(bf16)

    low = shape_of((tokens, columns), bf16)
    return kernel_call(
        kernel,
        "norm_back",
        [],
        [grads, projected, squares, inner],
        [low, low],
        0,
        waits=waits,
    )


def project_back(grads, weights, places, waits=()):
    rows, columns = grads[0].shape
    tokens = rows // 2
    dp = len(weights)
    slab = weights[0].shape[0]
    share = tokens // 4

    def kernel(place_ref, *refs):
        values = [ref[...] for ref in refs[: len(grads)]]
        pieces = refs[len(grads) : len(grads) + dp]
        parts, scratch = refs[len(grads) + dp : -1], refs[-1]
        for i in range(dp):
            total = None
            for j, value in enumerate(values):
                part = dot_last(value, pieces[i][:, j * columns : (j + 1) * columns])
                total = part if total is None else total + part
            scratch[place_ref[i]] = total.astype(bf16)
        for q, part in enumerate(parts):
            for mate in range(2):
                start = row_of(place_ref, dp, tokens, share, q, mate)
                for i in range(dp):
                    part[mate * share : (mate + 1) * share, i * slab : (i + 1) * slab] = scratch[
                        i, pl.ds(start, share), :
                    ]

    return kernel_call(
        kernel,
        "project_back",
        [places],
        [*grads, *weights],
        [shape_of((2 * share, slab * dp), bf16)] * 4,
        2 * len(grads) * rows * columns * slab * dp,
        [pltpu.VMEM((dp, rows, slab), bf16)],
        waits=waits,
    )


def weight_parts(slabs, wholes, places, slab_first, waits=()):
    dp, rows, slab = slabs.shape
    columns = wholes[0].shape[1]
    half = dp // 2
    shape = (slab, columns * len(wholes)) if slab_first else (columns, slab)

    def kernel(place_ref, slab_ref, *refs):
        outs = refs[len(wholes) :]
        for i in range(dp):
            left = slab_ref[place_ref[i]]
            for j, whole in enumerate(refs[: len(wholes)]):
                pair = (left, whole[...]) if slab_first else (whole[...], left)
                cut = slice(j * columns, (j + 1) * columns) if slab_first else slice(None)
                outs[i // half][i % half, :, cut] = dot_first(*pair).astype(bf16)

    return kernel_call(
        kernel,
        "weight_parts",
        [places],
        [slabs, *wholes],
        [shape_of((half,) + shape, bf16)] * 2,
        2 * slabs.size * columns * len(wholes),
        waits=waits,
    )


def hidden_back(terms, from_mate, hidden, grad_middle, gain, waits=()):
    share, width = hidden.shape

    def kernel(a_ref, b_ref, c_ref, d_ref, hidden_ref, grad_ref, gain_ref, out_ref, gain_out):
        normed_grad = added(a_ref[:share, :], b_ref[:share, :], c_ref[:share, :], d_ref[...])
        hidden = hidden_ref[...]
        scale = lax.rsqrt(jnp.mean(hidden * hidden, axis=1, keepdims=True) + epsilon)
        gain_out[...] = jnp.sum(normed_grad * hidden * scale, axis=0, keepdims=True)
        scaled = normed_grad * gain_ref[...]
        out_ref[...] = (
            grad_ref[...]
            + scale * scaled
            - hidden * (scale * scale * scale) * jnp.mean(scaled * hidden, axis=1, keepdims=True)
        )

    return kernel_call(
        kernel,
        "hidden_back",
        [],
        [*terms, from_mate, hidden, grad_middle, gain],
        [shape_of((share, width), f32), shape_of((1, width), f32)],
        0,
        waits=waits,
    )


def rope_tables(length, head_size):
    half_size = head_size // 2
    inverse = 10000.0 ** (-2.0 * jnp.arange(half_size, dtype=jnp.float32) / head_size)
    angles = jnp.arange(length, dtype=jnp.float32)[:, None] * inverse[None, :]
    cosine, sine = jnp.cos(angles), jnp.sin(angles)
    return jnp.stack(
        [jnp.concatenate([cosine, cosine], axis=1), jnp.concatenate([-sine, sine], axis=1)]
    )


def unpack(pieces, places, rows, experts, heads, half_heads, token_order, waits=()):
    dp = len(pieces)
    tokens = pieces[0].shape[1]
    at = [0]
    for n in rows:
        at.append(at[-1] + n)
    slab = D // dp
    head_slab = HD // dp
    share = tokens // 4

    def kernel(place_ref, *refs):
        parts = refs[:dp]
        router_ref, one_ref, two_ref, gain_ref, table_ref, bias_ref, wide, heads_at = refs[dp:]
        tp, upper = place_ref[dp], place_ref[dp + 1]
        for i in range(dp):
            wide[place_ref[i]] = parts[i][...].astype(f32)
        for j in range(dp):
            cut = slice(j * slab, (j + 1) * slab)
            weight = wide[j, : at[1], :slab].astype(bf16)
            router_ref[: at[1], cut] = weight
            router_ref[at[1] :, cut] = weight
            one_ref[:, cut] = wide[j, at[1] : at[2], :slab]
            two_ref[:, cut] = wide[j, at[2] : at[3], :slab]
            for i in range(2):
                heads_at[i, :heads, j * head_slab : (j + 1) * head_slab] = wide[
                    j, at[3 + i] : at[4 + i], :head_slab
                ]
        for i in range(2):
            for h in range(half_heads):
                gain_ref[i : i + 1, h * HD : (h + 1) * HD] = heads_at[
                    i, pl.ds(upper * half_heads + h, 1), :
                ]
        row = lax.broadcasted_iota(jnp.int32, (tokens, tokens), 0)
        column = lax.broadcasted_iota(jnp.int32, (tokens, tokens), 1)
        before = jnp.where(row < column, 1.0, 0.0).astype(bf16)
        lane = lax.broadcasted_iota(jnp.int32, (at[6] - at[5], tokens), 1)
        first = place_ref[0] * experts
        for at_tokens, i in enumerate(token_order):
            ids = parts[i][at[5] : at[6], :].astype(f32)
            for bit, step in ((1, share), (2, 2 * share)):
                turned_ids = jnp.where(
                    lane // step % 2 == 0,
                    pltpu.roll(ids, tokens - step, 1),
                    pltpu.roll(ids, step, 1),
                )
                ids = jnp.where((tp & bit) != 0, turned_ids, ids)
            named = jnp.concatenate(
                [
                    jnp.sum(
                        jnp.where(ids == (first + e).astype(f32), 1.0, 0.0), axis=0, keepdims=True
                    )
                    for e in range(experts)
                ]
            )
            slot = jnp.dot(named.astype(bf16), before, preferred_element_type=f32)
            table_ref[at_tokens] = jnp.where(named > 0.5, slot, -1.0).astype(jnp.int32)
        for i in range(2):
            line = parts[i][at[6] : at[7], :].astype(f32)
            segments = jnp.broadcast_to(line, (tokens, tokens))
            allowed = (column <= row) & (segments.T == segments)
            bias_ref[upper ^ i] = jnp.where(allowed, 0.0, -1e30)

    return kernel_call(
        kernel,
        "unpack",
        [places],
        pieces,
        [
            shape_of((2 * at[1], D), bf16),
            shape_of((1, D), f32),
            shape_of((1, D), f32),
            shape_of((2, half_heads * HD), f32),
            shape_of((dp, experts, tokens), jnp.int32),
            shape_of((2, tokens, tokens), f32),
        ],
        0,
        [
            pltpu.VMEM((dp,) + pieces[0].shape, f32),
            pltpu.VMEM((2, 8, HD), f32),
        ],
        waits=waits,
    )


def packed_sums(groups, heads, places, dp, waits=()):
    slab = D // dp
    head_slab = HD // dp
    here = 0 if heads is None else heads.shape[1] // HD
    count = 4 * 2 * here
    rows = sum(-(-group.shape[0] // 8) * 8 for group in groups)

    def kernel(place_ref, *refs):
        scratch, by_head = refs[-2:]
        outs = refs[-4:-2]
        scratch[...] = jnp.zeros_like(scratch)
        if here:
            first = place_ref[dp] * 2 * here + place_ref[dp + 1] * here
            by_head[...] = jnp.zeros_like(by_head)
            for i in range(2):
                for h in range(here):
                    by_head[pl.ds(i * count + first + h, 1), :] = refs[len(groups)][
                        i : i + 1, h * HD : (h + 1) * HD
                    ]
        for j in range(dp):
            at = 0
            for ref in refs[: len(groups)]:
                scratch[j, at : at + ref.shape[0], :] = ref[:, j * slab : (j + 1) * slab]
                at += -(-ref.shape[0] // 8) * 8
            if here:
                scratch[j, at:, :head_slab] = by_head[:, j * head_slab : (j + 1) * head_slab]
        for i in range(dp):
            outs[i // (dp // 2)][i % (dp // 2)] = scratch[place_ref[i]]

    shape = (dp, rows + 2 * count, slab)
    return kernel_call(
        kernel,
        "packed_sums",
        [places],
        [*groups] + ([heads] if here else []),
        [shape_of((dp // 2,) + shape[1:], f32)] * 2,
        0,
        [pltpu.VMEM(shape, f32), pltpu.VMEM((max(2 * count, 8), HD), f32)],
        waits=waits,
    )


def per_device(
    hidden_in,
    cotangent,
    segment_ids,
    expert_ids,
    first_gain,
    query_weight,
    key_weight,
    value_weight,
    output_weight,
    query_gain,
    key_gain,
    second_gain,
    router_weight,
    gate_weight,
    up_weight,
    down_weight,
):
    data_size = lax.axis_size("dp")
    tensor_size = lax.axis_size("tp")
    half = data_size // 2
    seq_len, width = hidden_in.shape
    share = seq_len // tensor_size
    slab = width // data_size
    me_dp, me_tp = lax.axis_index("dp"), lax.axis_index("tp")
    upper = me_dp // 2 % 2
    own = lambda values: lax.dynamic_slice_in_dim(values, me_tp * share, share, 0)
    local_experts = E // data_size
    first_expert = (me_dp * local_experts).astype(jnp.int32).reshape(1)
    here = jnp.stack([me_tp, upper]).astype(jnp.int32)
    places = jnp.concatenate([owners(weight_masks()), here])
    token_order = [weight_masks().index(mask) for mask in token_masks()]

    hidden_own, cot_own = own(hidden_in), own(cotangent)
    heads_local, head_slab = query_gain.shape
    small = [
        router_weight.T,
        first_gain[None],
        second_gain[None],
        query_gain,
        key_gain,
        expert_ids.T.astype(bf16),
        segment_ids.astype(bf16),
    ]
    small_rows = [array.shape[0] for array in small]
    wide = [jnp.pad(array, ((0, 0), (0, seq_len - array.shape[1]))) for array in small]
    small = gather_dp(jnp.concatenate(wide))
    column_half = heads_local * HD // 2
    kept, given = split_heads([query_weight, key_weight, value_weight], here)
    head_line = gather_line([kept, over_z(given, 1)], z_bits()[1:])
    head_pieces = head_line + [over_y(v) for v in head_line]
    cot_line = gather_dp(cot_own.astype(bf16))
    output_pieces = gather_dp(held([output_weight], bf16, [head_line[-1]]))
    router, gain_one, gain_two, gains, table, bias = unpack(
        small,
        places,
        small_rows,
        local_experts,
        heads_local,
        heads_local // 2,
        token_order,
        waits=[head_line[1]],
    )
    tables = rope_tables(seq_len, HD)
    first_scale = lax.rsqrt(jnp.mean(hidden_in * hidden_in, axis=-1, keepdims=True) + epsilon)
    normed_one = (hidden_in * first_scale * gain_one).astype(bf16)
    mates = gather_tp(over_z(own(normed_one), 1))
    x_slabs = paired([normed_one], mates, places, data_size)
    cot_near = held(cot_line, bf16, [mates[2]])
    cot_far = over_x(cot_near)
    projected, values, squares = project(
        x_slabs, head_pieces, places
    )
    squares = reduce_heads(squares)
    turned_rows, logs, attended, keep, give = attend(
        projected, squares, values, gains, tables, bias, places, data_size, waits=output_pieces[:half]
    )
    parts = output_project(keep, over_z(give, 1), output_pieces, places)
    middle, x_piece, probs = route(scatter_tp(parts)[0], hidden_own, gain_two, router)

    picks = (slice(0, half), slice(half, None))
    cot_far = held([cot_far], bf16, [x_piece])
    cot_all = [cot_near, over_core(cot_near), cot_far, over_core(cot_far)]
    cot_rows = rows_of_slots(cot_all, table, [], token_order)
    hidden_grad = grad_of_hidden(cot_rows, down_weight)
    x_pieces = gather_all(x_piece, [cot_rows], [hidden_grad])
    x_first = rows_of_slots(x_pieces[picks[0]], table[picks[0]], [hidden_grad])
    x_halves = [x_first, rows_of_slots(x_pieces[picks[1]], table[picks[1]], [x_first])]
    back_rows, act, gate_grad, up_grad = expert_step(
        x_halves, gate_weight, up_weight, hidden_grad, first_expert
    )
    second = tokens_of_slots(back_rows, table[picks[1]], half, [])
    first = tokens_of_slots(back_rows, table[picks[0]], 0, [second[0]])
    back = TokenSums(first, second).start()
    out_rows = expert_out(act, down_weight, back.sent)
    out_second = tokens_of_slots(out_rows, table[picks[1]], half, [])
    back.turn(out_second[0])
    out_first = tokens_of_slots(out_rows, table[picks[0]], 0, back.sent)
    chunk = max(local_experts // 4, 1)
    grads = []

    def some_grads(i, *waits):
        *grads[:], mark = expert_weight_grads(
            x_halves, cot_rows, act, gate_grad, up_grad, i * chunk, chunk, list(grads), waits
        )
        return mark

    back.top()
    mark = some_grads(0, *back.sent)
    moe = TokenSums(out_first, out_second).start(*back.sent)
    mark = some_grads(1, mark, *moe.sent)
    back = back.last(mark)

    grad_middle, grad_low, router_sum, gain_sum = route_back(
        back, middle, x_piece, probs, cot_own, gain_two, router, waits=[moe.came[0]]
    )
    low_pieces = gather_tp(grad_low)
    keep, give = output_back(low_pieces, output_pieces, places, [])
    moe.turn(keep)
    grad_values, gqk, inner, gain_sums = attend_back(
        keep, over_z(give, 1), places, data_size, turned_rows, logs, projected, squares, gains, tables, bias,
        [],
    )
    moe.top(gain_sums)
    inner = reduce_heads(inner)
    grad_queries, grad_keys = norm_back(gqk, projected, squares, inner, waits=moe.turned)
    head_grads = [grad_queries, grad_keys, grad_values]
    head_sums_at = WeightSums(*weight_parts(x_slabs, head_grads, places, True))
    parts = project_back(head_grads, head_pieces, places, waits=[head_sums_at.sent])
    terms, crossing = scatter_tp(parts)
    for_mate = combined([term[share:] for term in terms], 0)
    from_mate = over_z(for_mate, 1)
    head_sums_at.along_z(moe.from_top, from_mate)
    mates_low = over_z(held(low_pieces, bf16, [for_mate]), 1)
    mark = some_grads(2, mark, head_sums_at.sent)
    moe = moe.last(head_sums_at.came)
    low_slabs = paired(low_pieces, [mates_low], places, data_size)
    output_parts = weight_parts(
        low_slabs, [attended], places, False, waits=[head_sums_at.sent]
    )
    output_sums = WeightSums(*output_parts)
    grad_hidden, first_sum = hidden_back(terms, from_mate, hidden_own, grad_middle, gain_one)
    late = packed_sums(
        [router_sum[:E], gain_sum, first_sum],
        gain_sums,
        places,
        data_size,
        [],
    )
    grad_hidden = gather_tp(grad_hidden)
    mark = some_grads(3, mark, head_sums_at.sent)
    came = head_sums_at.came
    head_sums_at.to_mate(mark)
    output_sums.along_z(head_sums_at.sent).to_mate()
    total = reduce_all(*late, [came, mark])
    grad_hidden = absolute_tp(grad_hidden)
    hidden_out = absolute_tp(gather_tp(combined([middle, *moe], 0, sent=f32)))
    late = total[E + 8 :]
    head_sums = late[8:, :head_slab].reshape(2, heads_local * tensor_size, head_slab)
    head_sums = lax.dynamic_slice_in_dim(head_sums, me_tp * heads_local, heads_local, 1)
    grad_query, grad_key, grad_value = head_sums_at.in_order(here, 3, output_sums.sent)
    (grad_output,) = output_sums.in_order(here, 0)
    return (
        hidden_out,
        grad_hidden,
        late[0],
        grad_query,
        grad_key,
        grad_value,
        grad_output,
        head_sums[0],
        head_sums[1],
        total[E],
        total[:E].T,
        *grads,
    )


def solution(mesh):
    return jax.shard_map(
        per_device,
        mesh=mesh,
        in_specs=(
            P("dp", None),
            P("dp", None),
            P("dp", None),
            P("dp", None),
            P("dp"),
            P("dp", "tp"),
            P("dp", "tp"),
            P("dp", "tp"),
            P("tp", "dp"),
            P("tp", "dp"),
            P("tp", "dp"),
            P("dp"),
            P("dp", None),
            P("dp", None, "tp"),
            P("dp", None, "tp"),
            P("dp", "tp", None),
        ),
        out_specs=(
            P("dp", None),
            P("dp", None),
            P("dp"),
            P("dp", "tp"),
            P("dp", "tp"),
            P("dp", "tp"),
            P("tp", "dp"),
            P("tp", "dp"),
            P("tp", "dp"),
            P("dp"),
            P("dp", None),
            P("dp", None, "tp"),
            P("dp", None, "tp"),
            P("dp", "tp", None),
        ),
        check_vma=False,
    )
```

```python
import math

import jax
import jax.numpy as jnp
from jax import lax
from jax.experimental import pallas as pl
from jax.experimental.pallas import tpu as pltpu
from jax.sharding import PartitionSpec as P

D = 2048
HD = 128
E = 64
TOPK = 8
CAP = 48
EXTRA = 2 * E

bf16 = jnp.bfloat16
f32 = jnp.float32

epsilon = 1e-05


def cost(flops, bytes_accessed, transcendentals):
    return pl.CostEstimate(
        flops=flops // 1000000, bytes_accessed=bytes_accessed // 1000000, transcendentals=0
    )


def swap(values, dp_bits, tp_bits):
    dp, tp = lax.axis_size("dp"), lax.axis_size("tp")
    pairs = [
        (a * tp + b, (a ^ dp_bits) * tp + (b ^ tp_bits)) for a in range(dp) for b in range(tp)
    ]
    return lax.ppermute(values, ("dp", "tp"), pairs)


def over_z(values, bits):
    return swap(values, 2 * bits, 0)


def over_y(values):
    return swap(values, 1, 0)


def over_x(values):
    return swap(values, 0, 2)


def over_core(values):
    return swap(values, 0, 1)


def z_bits():
    half = lax.axis_size("dp") // 2
    return [1 << i for i in range(half.bit_length() - 1)]


def masks_of(bits):
    masks = [0]
    for bit in bits:
        masks = masks + [mask ^ bit for mask in masks]
    return masks


def weight_masks():
    return masks_of([2 * bit for bit in z_bits()] + [1])


def token_masks():
    return masks_of([2 * bit for bit in z_bits()[:-1]] + [1, 2 * z_bits()[-1]])


def owners(masks):
    return lax.axis_index("dp") ^ jnp.array(masks, jnp.int32)


def gather_line(pieces, bits):
    for bit in bits:
        pieces = pieces + [over_z(v, bit) for v in pieces]
    return pieces


def gather_dp(values):
    line = gather_line([values], z_bits())
    return line + [over_y(v) for v in line]


def gather_all(values, first_wait, second_wait):
    *bits, high = z_bits()
    line = gather_line([values], bits)
    going = [values] + [held([v], v.dtype, first_wait) for v in line[1:]]
    over = [over_z(v, high) for v in going]
    line = line + over[:-1] + [held(over[-1:], values.dtype, second_wait)]
    pairs = {}
    for mask, near in zip(masks_of([2 * bit for bit in z_bits()]), line, strict=True):
        if mask & 2 * high:
            aside = over_x(near)
            pairs[mask], pairs[mask + 1] = (near, aside), (over_y(near), over_y(aside))
        else:
            across = over_y(near)
            pairs[mask], pairs[mask + 1] = (near, over_x(near)), (across, over_x(across))
    return [
        (pairs[m][0], over_core(pairs[m][0]), pairs[m][1], over_core(pairs[m][1]))
        for m in token_masks()
    ]


def gather_tp(values):
    other = over_x(values)
    return [values, over_core(values), other, over_core(other)]


def sorted_by_bits(pieces, me):
    bit = 1
    while bit < len(pieces):
        odd = me & bit != 0
        pieces = [jnp.where(odd, pieces[i ^ bit], pieces[i]) for i in range(len(pieces))]
        bit *= 2
    return pieces


def absolute_dp(pieces):
    dp = len(pieces)
    by_mask = [pieces[i // 2 + i % 2 * (dp // 2)] for i in range(dp)]
    return jnp.stack(sorted_by_bits(by_mask, lax.axis_index("dp")))


def absolute_tp(pieces, axis=0):
    return jnp.concatenate(sorted_by_bits(list(pieces), lax.axis_index("tp")), axis=axis)


def added(*terms):
    total = terms[0].astype(f32)
    for term in terms[1:]:
        total = total + term.astype(f32)
    return total


def combined(terms, cut, waits=(), sent=bf16):
    shape = terms[0].shape
    outs = [shape_of((shape[0] - cut,) + shape[1:], sent)]
    if cut:
        outs.insert(0, shape_of((cut,) + shape[1:], f32))

    def kernel(*refs):
        for out, part in zip(refs[len(terms) :], (slice(0, cut), slice(cut, None))[-len(outs) :]):
            out[...] = added(*[ref[part] for ref in refs[: len(terms)]]).astype(out.dtype)

    result = kernel_call(kernel, "combined", [], list(terms), outs, 0, waits=waits)
    return result if cut else result[0]


def held(arrays, dtype, waits):
    def kernel(*refs):
        at = 0
        for ref in refs[:-1]:
            refs[-1][at : at + ref.shape[0], :] = ref[...].astype(dtype)
            at += ref.shape[0]

    rows = sum(array.shape[0] for array in arrays)
    out = shape_of((rows, arrays[0].shape[1]), dtype)
    return kernel_call(kernel, "held", [], list(arrays), [out], 0, waits=waits)[0]


def scatter_tp(parts):
    mine, far = over_core(parts[1]), over_core(parts[3])
    crossing = combined([parts[2], far], 0)
    return (parts[0], mine, over_x(crossing)), crossing


class TokenSums:
    def __init__(self, first, second):
        self.mid = first[0].shape[0] // 2
        self.first, self.second = first, second
        self.first_core = [over_core(first[1]), over_core(first[3])]
        self.second_core = [over_core(second[1]), over_core(second[3])]

    def start(self, *others):
        first, second = self.first, self.second
        self.b0, b0_far = combined([second[0], self.second_core[0]], self.mid, others)
        self.b1, b1_far = combined([second[2], self.second_core[1]], self.mid, others)
        a1 = combined([first[2], self.first_core[1]], 0, others)
        self.sent = [b0_far, b1_far, a1]
        self.came = [over_y(b0_far), over_y(b1_far), over_x(a1)]
        return self

    def turn(self, *others):
        b = combined([self.b1, self.came[1]], 0, others)
        self.a, a = combined([self.first[0], self.first_core[0], self.came[2]], self.mid, others)
        self.sent = [b, a]
        self.turned = [over_x(b), over_y(a)]
        return self

    def top(self, *others):
        self.sent = [combined([self.b0, self.came[0], self.turned[0]], 0, others)]
        self.from_top = over_z(self.sent[0], z_bits()[-1])
        return self

    def last(self, *others):
        terms = [self.a, self.turned[1], self.from_top]
        for bit in reversed(z_bits()[:-1]):
            near, sent = combined(terms, terms[0].shape[0] // 2, others if bit == 1 else ())
            terms = [near, over_z(sent, bit)]
        self.sent = [sent]
        return terms


def reduce_all(near, far, waits):
    terms = [near, over_y(far)]
    for bit in reversed(z_bits()):
        near, sent = combined(terms, bit, waits, sent=f32)
        terms = [near, over_z(sent, bit)]
    return reduce_tp(added(*terms)[0])


def reduce_tp(values):
    values = values + over_core(values)
    return values + over_x(values)


def reduce_heads(values):
    return reduce_tp(values + over_z(values, 1))


class WeightSums:
    def __init__(self, near, far):
        self.near, self.sent = near, far
        self.came = over_y(far)

    def along_z(self, *others):
        for bit in reversed(z_bits()[1:]):
            self.near, self.sent = combined([self.near, self.came], bit, others)
            self.came = over_z(self.sent, bit)
        return self

    def to_mate(self, *others):
        self.near, self.sent = combined([self.near, self.came], 1, others)
        self.came = over_z(self.sent, 1)
        return self

    def in_order(self, here, count, *others):
        _, rows, columns = self.near.shape
        size = columns // count if count else rows
        shape = (rows, 2 * size) if count else (2 * rows, columns)

        def kernel(here_ref, mine_ref, other_ref, *outs):
            for ref, which in ((mine_ref, here_ref[1]), (other_ref, 1 - here_ref[1])):
                part = pl.ds(pl.multiple_of(which * size, size), size)
                for j, out in enumerate(outs):
                    if count:
                        out[:, part] = ref[0, :, j * size : (j + 1) * size].astype(f32)
                    else:
                        out[part, :] = ref[0].astype(f32)

        return kernel_call(
            kernel,
            "in_order",
            [here],
            [self.near, self.came],
            [shape_of(shape, f32)] * max(count, 1),
            0,
            waits=others,
        )


def chosen_slots(table):
    experts, tokens = table.shape
    place = lax.broadcasted_iota(jnp.int32, (experts, CAP, tokens), 1)
    hit = place == table[:, None, :]
    return jnp.where(hit, 1.0, 0.0).astype(bf16).reshape(experts * CAP, tokens)


def rows_of_slots(pieces, table, waits, order=None):
    sequences, experts, tokens = table.shape
    if order is None:
        flat = [piece for group in pieces for piece in group]
        share, width = flat[0].shape
    else:
        flat = pieces
        share, width = tokens // 4, pieces[0].shape[1]
    count = sequences * 4

    def kernel(*refs):
        table_ref, *sources = refs[:-3]
        out_ref, buffer, arrived = refs[-3:]
        step = pl.program_id(0)

        def piece(i):
            if order is None:
                return sources[i]
            return sources[i % 4].at[pl.ds(order[i // 4] * share, share), :]

        @pl.when(step == 0)
        def _():
            for i in range(count):
                pltpu.make_async_copy(
                    piece(i), buffer.at[i // 4, pl.ds(i % 4 * share, share)], arrived.at[i]
                ).start()

        for i in range(4):
            pltpu.make_async_copy(
                piece(i), buffer.at[step, pl.ds(i * share, share)], arrived.at[step * 4 + i]
            ).wait()
        picked = jnp.dot(chosen_slots(table_ref[0]), buffer[step], preferred_element_type=f32)
        out_ref[...] = picked.astype(bf16).reshape(experts, CAP, width)

    return pl.pallas_call(
        without(kernel, 1 + len(flat), len(waits)),
        grid=(sequences,),
        in_specs=[pl.BlockSpec((1, experts, tokens), lambda s: (s, 0, 0))]
        + [pl.BlockSpec(memory_space=pltpu.HBM)] * len(flat)
        + [pl.BlockSpec(memory_space=pl.ANY)] * len(waits),
        out_specs=pl.BlockSpec((experts, CAP, width), lambda s: (0, s, 0)),
        out_shape=jax.ShapeDtypeStruct((experts, sequences * CAP, width), bf16),
        scratch_shapes=[
            pltpu.VMEM((sequences, tokens, width), bf16),
            pltpu.SemaphoreType.DMA((count,)),
        ],
        compiler_params=pltpu.CompilerParams(vmem_limit_bytes=48 << 20),
        cost_estimate=cost(
            flops=2 * experts * CAP * sequences * tokens * width,
            bytes_accessed=2 * sequences * (tokens + experts * CAP) * width,
            transcendentals=0,
        ),
        name="rows_of_slots",
    )(table, *flat, *waits)


def tokens_of_slots(rows, table, first, waits):
    sequences, experts, tokens = table.shape
    width = rows.shape[-1]
    share = tokens // 4

    def kernel(table_ref, rows_ref, *outs):
        picked = chosen_slots(table_ref[0])
        total = lax.dot_general(
            picked,
            rows_ref[...].reshape(experts * CAP, width),
            (((0,), (0,)), ((), ())),
            preferred_element_type=f32,
        ).astype(bf16)
        for q, out in enumerate(outs):
            out[...] = total[q * share : (q + 1) * share]

    return pl.pallas_call(
        without(kernel, 2, len(waits)),
        grid=(sequences,),
        in_specs=[
            pl.BlockSpec((1, experts, tokens), lambda s: (s, 0, 0)),
            pl.BlockSpec((experts, CAP, width), lambda s: (0, s + first, 0)),
        ]
        + [pl.BlockSpec(memory_space=pl.ANY)] * len(waits),
        out_specs=[pl.BlockSpec((share, width), lambda s: (s, 0))] * 4,
        out_shape=[jax.ShapeDtypeStruct((sequences * share, width), bf16)] * 4,
        compiler_params=pltpu.CompilerParams(vmem_limit_bytes=48 << 20),
        cost_estimate=cost(
            flops=2 * experts * CAP * sequences * tokens * width,
            bytes_accessed=2 * sequences * (tokens + experts * CAP) * width,
            transcendentals=0,
        ),
        name="tokens_of_slots",
    )(table, rows, *waits)


def dot_last(a, b):
    return lax.dot_general(a, b, (((1,), (1,)), ((), ())), preferred_element_type=f32)


def dot_first(a, b):
    return lax.dot_general(a, b, (((0,), (0,)), ((), ())), preferred_element_type=f32)


def per_expert(kernel, experts, ins, outs, flops, name, scalars=(), waits=()):
    whole = lambda shape: pl.BlockSpec((1,) + tuple(shape[1:]), lambda e: (e, 0, 0))
    in_specs = [pl.BlockSpec(memory_space=pltpu.SMEM)] * len(scalars)
    moved = 0
    for array, block in ins:
        in_specs.append(pl.BlockSpec((1,) + block, lambda e: (e, 0, 0)))
        moved += experts * math.prod(block) * array.dtype.itemsize
    moved += sum(math.prod(o.shape) * o.dtype.itemsize for o in outs)
    return pl.pallas_call(
        without(kernel, len(in_specs), len(waits)),
        grid=(experts,),
        in_specs=in_specs + [pl.BlockSpec(memory_space=pl.ANY)] * len(waits),
        out_specs=[whole(o.shape) for o in outs],
        out_shape=list(outs),
        compiler_params=pltpu.CompilerParams(vmem_limit_bytes=48 << 20),
        cost_estimate=cost(flops=flops, bytes_accessed=moved, transcendentals=0),
        name=name,
    )(*scalars, *[array for array, _ in ins], *waits)


def grad_of_hidden(cot_rows, down_weight):
    experts, rows, width = cot_rows.shape
    hidden = down_weight.shape[1]

    def kernel(cot_ref, down_ref, out_ref):
        out_ref[0] = dot_last(cot_ref[0], down_ref[0])

    return per_expert(
        kernel,
        experts,
        [(cot_rows, (rows, width)), (down_weight, (hidden, width))],
        [jax.ShapeDtypeStruct((experts, rows, hidden), f32)],
        2 * experts * rows * width * hidden,
        "grad_of_hidden",
    )[0]


def expert_step(x_halves, gate_weight, up_weight, hidden_grad, first_expert):
    experts, half_rows, wide = x_halves[0].shape
    rows = half_rows * 2
    width, hidden = gate_weight.shape[1:]

    def kernel(base_ref, a_ref, b_ref, gate_ref, up_ref, grad_ref, back_ref, act_ref, gate_grad_ref, up_grad_ref):
        mine = base_ref[0] + pl.program_id(0)
        x = jnp.concatenate([a_ref[0, :, :width], b_ref[0, :, :width]])
        lane = lax.broadcasted_iota(jnp.int32, (rows, EXTRA), 1)
        probs = jnp.concatenate([a_ref[0, :, width:], b_ref[0, :, width:]]).astype(f32)
        mix = jnp.sum(
            jnp.where((lane == mine) | (lane == mine + E), probs, 0.0), axis=1, keepdims=True
        )
        gate_act = jnp.dot(x, gate_ref[0], preferred_element_type=f32)
        up_act = jnp.dot(x, up_ref[0], preferred_element_type=f32)
        raw = grad_ref[0]
        sig = jax.nn.sigmoid(gate_act)
        silu = gate_act * sig
        act = silu * up_act
        grad_mix = jnp.sum(act * raw, axis=1, keepdims=True)
        act_ref[0] = (mix * act).astype(bf16)
        weighted = mix * raw
        gate_grad = (weighted * up_act * sig * (1.0 + gate_act * (1.0 - sig))).astype(bf16)
        up_grad = (weighted * silu).astype(bf16)
        gate_grad_ref[0] = gate_grad
        up_grad_ref[0] = up_grad
        back_ref[0, :, :width] = (
            dot_last(gate_grad, gate_ref[0]) + dot_last(up_grad, up_ref[0])
        ).astype(bf16)
        coarse = grad_mix.astype(bf16).astype(f32)
        fine = grad_mix - coarse
        back_ref[0, :, width:] = jnp.where(
            lane == mine, coarse, jnp.where(lane == mine + E, fine, 0.0)
        ).astype(bf16)

    small = jax.ShapeDtypeStruct((experts, rows, hidden), bf16)
    return per_expert(
        kernel,
        experts,
        [
            (x_halves[0], (half_rows, wide)),
            (x_halves[1], (half_rows, wide)),
            (gate_weight, (width, hidden)),
            (up_weight, (width, hidden)),
            (hidden_grad, (rows, hidden)),
        ],
        [jax.ShapeDtypeStruct((experts, rows, wide), bf16), small, small, small],
        8 * experts * rows * width * hidden,
        "expert_step",
        (first_expert,),
    )


def expert_out(act, down_weight, waits):
    experts, rows, hidden = act.shape
    width = down_weight.shape[2]

    def kernel(act_ref, down_ref, out_ref):
        out_ref[0] = jnp.dot(act_ref[0], down_ref[0], preferred_element_type=f32).astype(bf16)

    return per_expert(
        kernel,
        experts,
        [(act, (rows, hidden)), (down_weight, (hidden, width))],
        [jax.ShapeDtypeStruct((experts, rows, width), bf16)],
        2 * experts * rows * width * hidden,
        "expert_out",
        waits=waits,
    )[0]


def expert_weight_grads(x_halves, cot_rows, act, gate_grad, up_grad, first, count, into, waits):
    experts, rows, hidden = act.shape
    width = cot_rows.shape[2]

    def kernel(a_ref, b_ref, cot_ref, act_ref, gate_ref, up_ref, *refs):
        gate_out, up_out, down_out, mark = refs[-4:]
        mark[...] = jnp.zeros_like(mark)
        x = jnp.concatenate([a_ref[0], b_ref[0]])
        gate_out[0] = dot_first(x, gate_ref[0])
        up_out[0] = dot_first(x, up_ref[0])
        down_out[0] = dot_first(act_ref[0], cot_ref[0])

    block = lambda *shape: pl.BlockSpec((1,) + shape, lambda e: (e + first, 0, 0))
    ins = [*x_halves, cot_rows, act, gate_grad, up_grad]
    return pl.pallas_call(
        kernel,
        grid=(count,),
        in_specs=[block(rows // 2, width)] * 2
        + [block(rows, width)]
        + [block(rows, hidden)] * 3
        + [pl.BlockSpec(memory_space=pl.ANY)] * (len(into) + len(waits)),
        out_specs=[block(width, hidden), block(width, hidden), block(hidden, width)]
        + [pl.BlockSpec((8, 128), lambda e: (0, 0))],
        out_shape=[
            jax.ShapeDtypeStruct((experts, width, hidden), f32),
            jax.ShapeDtypeStruct((experts, width, hidden), f32),
            jax.ShapeDtypeStruct((experts, hidden, width), f32),
            jax.ShapeDtypeStruct((8, 128), f32),
        ],
        input_output_aliases={len(ins) + i: i for i in range(len(into))},
        compiler_params=pltpu.CompilerParams(vmem_limit_bytes=48 << 20),
        cost_estimate=cost(
            flops=6 * count * rows * width * hidden,
            bytes_accessed=count * (4 * rows * (width + hidden) + 12 * width * hidden),
            transcendentals=0,
        ),
        name="expert_weight_grads",
    )(*ins, *into, *waits)


def without(kernel, start, count):
    return lambda *refs: kernel(*refs[:start], *refs[start + count :])


def kernel_call(kernel, name, scalars, ins, outs, flops, scratch=(), waits=()):
    moved = sum(a.size * a.dtype.itemsize for a in ins)
    moved += sum(math.prod(o.shape) * o.dtype.itemsize for o in outs)
    large = [i for i, a in enumerate(ins) if a.size * a.dtype.itemsize >= 1 << 16]
    first, last = len(scalars), len(scalars) + len(ins)
    made = last + len(waits)

    def body(*refs):
        given = list(refs[first:last])
        kept = made + len(outs) + len(scratch)
        copies = []
        for k, i in enumerate(large):
            copies.append(pltpu.make_async_copy(given[i], refs[kept + k], refs[-1].at[k]))
            copies[-1].start()
            given[i] = refs[kept + k]
        for copy in copies:
            copy.wait()
        kernel(*refs[:first], *given, *refs[made:kept])

    places = [pl.ANY if i in large else pltpu.VMEM for i in range(len(ins))]
    return pl.pallas_call(
        body,
        in_specs=[pl.BlockSpec(memory_space=pltpu.SMEM)] * len(scalars)
        + [pl.BlockSpec(memory_space=place) for place in places]
        + [pl.BlockSpec(memory_space=pl.ANY)] * len(waits),
        out_specs=[pl.BlockSpec(memory_space=pltpu.VMEM)] * len(outs),
        out_shape=list(outs),
        scratch_shapes=list(scratch)
        + [pltpu.VMEM(ins[i].shape, ins[i].dtype) for i in large]
        + [pltpu.SemaphoreType.DMA((max(len(large), 1),))],
        compiler_params=pltpu.CompilerParams(vmem_limit_bytes=40 << 20),
        cost_estimate=cost(flops=flops, bytes_accessed=moved, transcendentals=0),
        name=name,
    )(*scalars, *ins, *waits)


def shape_of(shape, dtype):
    return jax.ShapeDtypeStruct(shape, dtype)


def row_of(place_ref, dp, tokens, share, q, mate):
    which = (1 - place_ref[dp + 1]) if mate else place_ref[dp + 1]
    return pl.multiple_of(which * tokens + (place_ref[dp] ^ q) * share, share)


def split_heads(weights, here):
    rows, columns = weights[0].shape
    half = columns // 2

    def kernel(here_ref, *refs):
        keep_ref, give_ref, scratch = refs[len(weights) :]
        for j, ref in enumerate(refs[: len(weights)]):
            for i in range(2):
                scratch[i, :, j * half : (j + 1) * half] = ref[:, i * half : (i + 1) * half]
        keep_ref[...] = scratch[here_ref[1]]
        give_ref[...] = scratch[1 - here_ref[1]]

    shape = (rows, half * len(weights))
    return kernel_call(
        kernel,
        "split_heads",
        [here],
        list(weights),
        [shape_of(shape, bf16)] * 2,
        0,
        [pltpu.VMEM((2,) + shape, bf16)],
    )


def paired(own, mates, places, dp):
    share, width = mates[0].shape
    if len(mates) == 1:
        share = share // 4
    tokens = 4 * share
    slab = width // dp

    def kernel(place_ref, *refs):
        out_ref = refs[-1]
        if len(own) == 1:
            start = pl.multiple_of(place_ref[dp + 1] * tokens, tokens)
            for i in range(dp):
                out_ref[i, pl.ds(start, tokens), :] = refs[0][:, i * slab : (i + 1) * slab]
        for q in range(4):
            sources = []
            if len(own) == 4:
                sources.append((refs[q][...], False))
            if len(mates) == 4:
                sources.append((refs[len(own) + q][...], True))
            else:
                sources.append((refs[len(own)][q * share : (q + 1) * share, :], True))
            for rows, mate in sources:
                start = row_of(place_ref, dp, tokens, share, q, mate)
                for i in range(dp):
                    out_ref[i, pl.ds(start, share), :] = rows[:, i * slab : (i + 1) * slab]

    return kernel_call(
        kernel, "paired", [places], [*own, *mates], [shape_of((dp, 2 * tokens, slab), bf16)], 0
    )[0]


def as_rows(first, second):
    lane = lax.broadcasted_iota(jnp.int32, (first.shape[0], 128), 1)
    return jnp.where(lane < 4, first, second).T[:8]


def as_columns(pair):
    wide = jnp.concatenate([pair] * 16).T
    return wide[:, 0:1], wide[:, 4:5]


def project(x_slabs, pieces, places):
    dp, tokens, _ = x_slabs.shape
    columns = pieces[0].shape[1] // 3

    def kernel(place_ref, x_ref, *refs):
        totals = []
        for j in range(3):
            total = None
            for i in range(dp):
                part = jnp.dot(
                    x_ref[place_ref[i]],
                    refs[i][:, j * columns : (j + 1) * columns],
                    preferred_element_type=f32,
                )
                total = part if total is None else total + part
            totals.append(total)
        queries, keys, values = totals
        qk_out, v_out, squares_out = refs[dp:]
        qk_out[0] = queries
        qk_out[1] = keys
        v_out[...] = values.astype(bf16)
        squares_out[...] = as_rows(
            jnp.sum(queries * queries, axis=1, keepdims=True),
            jnp.sum(keys * keys, axis=1, keepdims=True),
        )

    return kernel_call(
        kernel,
        "project",
        [places],
        [x_slabs, *pieces],
        [
            shape_of((2, tokens, columns), f32),
            shape_of((tokens, columns), bf16),
            shape_of((8, tokens), f32),
        ],
        6 * x_slabs.size * columns,
    )


def turned(values):
    return pltpu.roll(values, HD // 2, 1)


def attend(projected, squares, values, gains, tables, bias, places, dp, waits=()):
    _, rows, columns = projected.shape
    tokens = rows // 2
    heads = columns // HD
    lanes = 128 // heads

    def kernel(place_ref, qk_ref, sq_ref, v_ref, gain_ref, table_ref, bias_ref, *refs):
        turned_out, log_out, att_out, keep_out, give_out = refs
        turned_out[2] = v_ref[...]
        cosine, sine = table_ref[0], table_ref[1]
        lane = lax.broadcasted_iota(jnp.int32, (tokens, 128), 1)
        q_squares, k_squares = as_columns(sq_ref[...])
        for which in range(2):
            row = slice(which * tokens, (which + 1) * tokens)
            q_scale = lax.rsqrt(q_squares[row] / D + epsilon)
            k_scale = lax.rsqrt(k_squares[row] / D + epsilon)
            logs = jnp.zeros((tokens, 128), f32)
            for h in range(heads):
                cut = slice(h * HD, (h + 1) * HD)
                q = qk_ref[0, row, cut] * q_scale * gain_ref[0:1, cut]
                k = qk_ref[1, row, cut] * k_scale * gain_ref[1:2, cut]
                q = (q * cosine + turned(q) * sine).astype(bf16)
                k = (k * cosine + turned(k) * sine).astype(bf16)
                turned_out[0, row, cut] = q
                turned_out[1, row, cut] = k
                scores = dot_last(q, k) * (1.0 / math.sqrt(HD)) + bias_ref[which]
                largest = jnp.max(scores, axis=1, keepdims=True)
                raised = jnp.exp(scores - largest)
                total = jnp.sum(raised, axis=1, keepdims=True)
                logs = jnp.where(lane // lanes == h, largest + jnp.log(total), logs)
                probs = (raised / total).astype(bf16)
                att_out[row, cut] = jnp.dot(
                    probs, v_ref[row, cut], preferred_element_type=f32
                ).astype(bf16)
            log_out[row, :] = logs
        upper = place_ref[dp + 1]
        keep_out[...] = att_out[pl.ds(pl.multiple_of(upper * tokens, tokens), tokens), :]
        give_out[...] = att_out[pl.ds(pl.multiple_of((1 - upper) * tokens, tokens), tokens), :]

    part = shape_of((tokens, columns), bf16)
    return kernel_call(
        kernel,
        "attend",
        [places],
        [projected, squares, values, gains, tables, bias],
        [
            shape_of((3, rows, columns), bf16),
            shape_of((rows, 128), f32),
            shape_of((rows, columns), bf16),
            part,
            part,
        ],
        4 * tokens * rows * columns,
        waits=waits,
    )


def output_project(keep, got, pieces, places, waits=()):
    tokens, columns = keep.shape
    dp = len(pieces)
    slab = pieces[0].shape[1]
    share = tokens // 4

    def kernel(place_ref, keep_ref, got_ref, *refs):
        weights, parts, scratch = refs[:dp], refs[dp:-1], refs[-1]
        upper = place_ref[dp + 1]
        mine = pl.ds(pl.multiple_of(upper * columns, columns), columns)
        other = pl.ds(pl.multiple_of((1 - upper) * columns, columns), columns)
        for i in range(dp):
            scratch[place_ref[i]] = (
                jnp.dot(keep_ref[...], weights[i][mine, :], preferred_element_type=f32)
                + jnp.dot(got_ref[...], weights[i][other, :], preferred_element_type=f32)
            ).astype(bf16)
        for q, part in enumerate(parts):
            start = pl.multiple_of((place_ref[dp] ^ q) * share, share)
            for i in range(dp):
                part[:, i * slab : (i + 1) * slab] = scratch[i, pl.ds(start, share), :]

    return kernel_call(
        kernel,
        "output_project",
        [places],
        [keep, got, *pieces],
        [shape_of((share, slab * dp), bf16)] * 4,
        4 * tokens * columns * slab * dp,
        [pltpu.VMEM((dp, tokens, slab), bf16)],
        waits=waits,
    )


def route(terms, hidden, gain, router, waits=()):
    share, width = hidden.shape

    def kernel(a_ref, b_ref, c_ref, hidden_ref, gain_ref, router_ref, middle_ref, x_ref, probs_ref):
        middle = hidden_ref[...] + added(a_ref[...], b_ref[...], c_ref[...])
        middle_ref[...] = middle
        scale = lax.rsqrt(jnp.mean(middle * middle, axis=1, keepdims=True) + epsilon)
        normed = (middle * scale * gain_ref[...]).astype(bf16)
        x_ref[:, :width] = normed
        logits = dot_last(normed, router_ref[...])
        raised = jnp.exp(logits - jnp.max(logits, axis=1, keepdims=True))
        probs = raised / (0.5 * jnp.sum(raised, axis=1, keepdims=True))
        probs_ref[...] = probs
        coarse = probs.astype(bf16).astype(f32)
        lane = lax.broadcasted_iota(jnp.int32, probs.shape, 1)
        x_ref[:, width:] = jnp.where(lane < E, coarse, probs - coarse).astype(bf16)

    return kernel_call(
        kernel,
        "route",
        [],
        [*terms, hidden, gain, router],
        [
            shape_of((share, width), f32),
            shape_of((share, width + EXTRA), bf16),
            shape_of((share, EXTRA), f32),
        ],
        2 * share * width * EXTRA,
        waits=waits,
    )


def route_back(terms, middle, x_piece, probs, cotangent, gain, router, waits=()):
    share, width = middle.shape

    def kernel(a_ref, b_ref, middle_ref, x_ref, probs_ref, cot_ref, gain_ref, router_ref, *outs):
        grad_ref, low_ref, router_out, gain_out = outs
        pair = added(a_ref[:, width:], b_ref[:, width:])
        grad_probs = pair + pltpu.roll(pair, E, 1)
        probs = probs_ref[...]
        inner = 0.5 * jnp.sum(probs * grad_probs, axis=1, keepdims=True)
        grad_logits = probs * (grad_probs - inner)
        middle = middle_ref[...]
        scale = lax.rsqrt(jnp.mean(middle * middle, axis=1, keepdims=True) + epsilon)
        lane = lax.broadcasted_iota(jnp.int32, probs.shape, 1)
        once = jnp.where(lane < E, grad_logits, 0.0)
        normed_grad = added(a_ref[:, :width], b_ref[:, :width]) + lax.dot_general(
            once,
            router_ref[...].astype(f32),
            (((1,), (0,)), ((), ())),
            precision=lax.Precision.HIGHEST,
            preferred_element_type=f32,
        )
        router_out[...] = lax.dot_general(
            once,
            x_ref[:, :width].astype(f32),
            (((0,), (0,)), ((), ())),
            precision=lax.Precision.HIGHEST,
            preferred_element_type=f32,
        )
        gain_out[...] = jnp.sum(normed_grad * middle * scale, axis=0, keepdims=True)
        scaled = normed_grad * gain_ref[...]
        grad = (
            cot_ref[...]
            + scale * scaled
            - middle * (scale * scale * scale) * jnp.mean(scaled * middle, axis=1, keepdims=True)
        )
        grad_ref[...] = grad
        low_ref[...] = grad.astype(bf16)

    return kernel_call(
        kernel,
        "route_back",
        [],
        [*terms, middle, x_piece, probs, cotangent, gain, router],
        [
            shape_of((share, width), f32),
            shape_of((share, width), bf16),
            shape_of((EXTRA, width), f32),
            shape_of((1, width), f32),
        ],
        24 * share * width * EXTRA,
        waits=waits,
    )


def output_back(low_pieces, pieces, places, waits):
    dp = len(pieces)
    columns, slab = pieces[0].shape
    share = low_pieces[0].shape[0]
    tokens = 4 * share
    half = columns // 2

    def kernel(place_ref, *refs):
        lows, weights, (keep_ref, give_ref, scratch, both) = refs[:4], refs[4 : 4 + dp], refs[4 + dp :]
        for q, low in enumerate(lows):
            start = pl.multiple_of((place_ref[dp] ^ q) * share, share)
            for i in range(dp):
                scratch[i, pl.ds(start, share), :] = low[:, i * slab : (i + 1) * slab]
        total = None
        for i in range(dp):
            part = dot_last(scratch[place_ref[i]], weights[i][...])
            total = part if total is None else total + part
        both[0] = total[:, :half].astype(bf16)
        both[1] = total[:, half:].astype(bf16)
        upper = place_ref[dp + 1]
        keep_ref[...] = both[upper]
        give_ref[...] = both[1 - upper]

    return kernel_call(
        kernel,
        "output_back",
        [places],
        [*low_pieces, *pieces],
        [shape_of((tokens, half), bf16)] * 2,
        2 * tokens * columns * slab * dp,
        [pltpu.VMEM((dp, tokens, slab), bf16), pltpu.VMEM((2, tokens, half), bf16)],
        waits=waits,
    )


def attend_back(keep, got, places, dp, turned_rows, logs, projected, squares, gains, tables, bias, waits):
    _, rows, columns = projected.shape
    tokens = rows // 2
    heads = columns // HD
    lanes = 128 // heads

    def kernel(place_ref, keep_ref, got_ref, *refs):
        turned_ref, log_ref, qk_ref, sq_ref, gain_ref, table_ref, bias_ref = refs[:7]
        gv_ref, gqk_ref, inner_ref, gains_ref, scratch = refs[7:]
        upper = place_ref[dp + 1]
        scratch[upper] = keep_ref[...]
        scratch[1 - upper] = got_ref[...]
        cosine, sine = table_ref[0], table_ref[1]
        q_squares, k_squares = as_columns(sq_ref[...])
        for which in range(2):
            row = slice(which * tokens, (which + 1) * tokens)
            q_scale = lax.rsqrt(q_squares[row] / D + epsilon)
            k_scale = lax.rsqrt(k_squares[row] / D + epsilon)
            inner = [jnp.zeros((tokens, 1), f32), jnp.zeros((tokens, 1), f32)]
            for h in range(heads):
                cut = slice(h * HD, (h + 1) * HD)
                qr, kr, v = (turned_ref[i, row, cut] for i in range(3))
                grad = scratch[which, :, cut]
                scores = dot_last(qr, kr) * (1.0 / math.sqrt(HD)) + bias_ref[which]
                probs = jnp.exp(scores - log_ref[row, h * lanes : h * lanes + 1])
                gv_ref[row, cut] = dot_first(probs.astype(bf16), grad).astype(bf16)
                grad_probs = dot_last(grad, v)
                dots = jnp.sum(probs * grad_probs, axis=1, keepdims=True)
                grad_scores = (probs * (grad_probs - dots) * (1.0 / math.sqrt(HD))).astype(bf16)
                gq = jnp.dot(grad_scores, kr, preferred_element_type=f32)
                gk = dot_first(grad_scores, qr)
                gq = gq * cosine - turned(gq) * sine
                gk = gk * cosine - turned(gk) * sine
                q, k = qk_ref[0, row, cut], qk_ref[1, row, cut]
                for i, (grad_sum, value, scale) in enumerate(((gq, q, q_scale), (gk, k, k_scale))):
                    total = jnp.sum(grad_sum * value * scale, axis=0, keepdims=True)
                    if which:
                        total = total + gains_ref[i : i + 1, cut]
                    gains_ref[i : i + 1, cut] = total
                gq = gq * gain_ref[0:1, cut]
                gk = gk * gain_ref[1:2, cut]
                gqk_ref[0, row, cut] = gq
                gqk_ref[1, row, cut] = gk
                inner[0] = inner[0] + jnp.sum(gq * q, axis=1, keepdims=True)
                inner[1] = inner[1] + jnp.sum(gk * k, axis=1, keepdims=True)
            inner_ref[:, row] = as_rows(*inner)

    return kernel_call(
        kernel,
        "attend_back",
        [places],
        [keep, got, turned_rows, logs, projected, squares, gains, tables, bias],
        [
            shape_of((rows, columns), bf16),
            shape_of((2, rows, columns), f32),
            shape_of((8, rows), f32),
            shape_of((2, columns), f32),
        ],
        10 * tokens * rows * columns,
        [pltpu.VMEM((2, tokens, columns), bf16)],
        waits=waits,
    )


def norm_back(grads, projected, squares, inner, waits=()):
    _, tokens, columns = projected.shape

    def kernel(grad_ref, value_ref, sq_ref, inner_ref, *outs):
        squares, inners = as_columns(sq_ref[...]), as_columns(inner_ref[...])
        for i, out in enumerate(outs):
            scale = lax.rsqrt(squares[i] / D + epsilon)
            mean = inners[i] / D
            out[...] = (
                scale * grad_ref[i] - value_ref[i] * (scale * scale * scale) * mean
            ).astype(bf16)

    low = shape_of((tokens, columns), bf16)
    return kernel_call(
        kernel,
        "norm_back",
        [],
        [grads, projected, squares, inner],
        [low, low],
        0,
        waits=waits,
    )


def project_back(grads, weights, places, waits=()):
    rows, columns = grads[0].shape
    tokens = rows // 2
    dp = len(weights)
    slab = weights[0].shape[0]
    share = tokens // 4

    def kernel(place_ref, *refs):
        values = [ref[...] for ref in refs[: len(grads)]]
        pieces = refs[len(grads) : len(grads) + dp]
        parts, scratch = refs[len(grads) + dp : -1], refs[-1]
        for i in range(dp):
            total = None
            for j, value in enumerate(values):
                part = dot_last(value, pieces[i][:, j * columns : (j + 1) * columns])
                total = part if total is None else total + part
            scratch[place_ref[i]] = total.astype(bf16)
        for q, part in enumerate(parts):
            for mate in range(2):
                start = row_of(place_ref, dp, tokens, share, q, mate)
                for i in range(dp):
                    part[mate * share : (mate + 1) * share, i * slab : (i + 1) * slab] = scratch[
                        i, pl.ds(start, share), :
                    ]

    return kernel_call(
        kernel,
        "project_back",
        [places],
        [*grads, *weights],
        [shape_of((2 * share, slab * dp), bf16)] * 4,
        2 * len(grads) * rows * columns * slab * dp,
        [pltpu.VMEM((dp, rows, slab), bf16)],
        waits=waits,
    )


def weight_parts(slabs, wholes, places, slab_first, waits=()):
    dp, rows, slab = slabs.shape
    columns = wholes[0].shape[1]
    half = dp // 2
    shape = (slab, columns * len(wholes)) if slab_first else (columns, slab)

    def kernel(place_ref, slab_ref, *refs):
        outs = refs[len(wholes) :]
        for i in range(dp):
            left = slab_ref[place_ref[i]]
            for j, whole in enumerate(refs[: len(wholes)]):
                pair = (left, whole[...]) if slab_first else (whole[...], left)
                cut = slice(j * columns, (j + 1) * columns) if slab_first else slice(None)
                outs[i // half][i % half, :, cut] = dot_first(*pair).astype(bf16)

    return kernel_call(
        kernel,
        "weight_parts",
        [places],
        [slabs, *wholes],
        [shape_of((half,) + shape, bf16)] * 2,
        2 * slabs.size * columns * len(wholes),
        waits=waits,
    )


def hidden_back(terms, from_mate, hidden, grad_middle, gain, waits=()):
    share, width = hidden.shape

    def kernel(a_ref, b_ref, c_ref, d_ref, hidden_ref, grad_ref, gain_ref, out_ref, gain_out):
        normed_grad = added(a_ref[:share, :], b_ref[:share, :], c_ref[:share, :], d_ref[...])
        hidden = hidden_ref[...]
        scale = lax.rsqrt(jnp.mean(hidden * hidden, axis=1, keepdims=True) + epsilon)
        gain_out[...] = jnp.sum(normed_grad * hidden * scale, axis=0, keepdims=True)
        scaled = normed_grad * gain_ref[...]
        out_ref[...] = (
            grad_ref[...]
            + scale * scaled
            - hidden * (scale * scale * scale) * jnp.mean(scaled * hidden, axis=1, keepdims=True)
        )

    return kernel_call(
        kernel,
        "hidden_back",
        [],
        [*terms, from_mate, hidden, grad_middle, gain],
        [shape_of((share, width), f32), shape_of((1, width), f32)],
        0,
        waits=waits,
    )


def rope_tables(length, head_size):
    half_size = head_size // 2
    inverse = 10000.0 ** (-2.0 * jnp.arange(half_size, dtype=jnp.float32) / head_size)
    angles = jnp.arange(length, dtype=jnp.float32)[:, None] * inverse[None, :]
    cosine, sine = jnp.cos(angles), jnp.sin(angles)
    return jnp.stack(
        [jnp.concatenate([cosine, cosine], axis=1), jnp.concatenate([-sine, sine], axis=1)]
    )


def unpack(pieces, places, rows, experts, heads, half_heads, token_order, waits=()):
    dp = len(pieces)
    tokens = pieces[0].shape[1]
    at = [0]
    for n in rows:
        at.append(at[-1] + n)
    slab = D // dp
    head_slab = HD // dp
    share = tokens // 4

    def kernel(place_ref, *refs):
        parts = refs[:dp]
        router_ref, one_ref, two_ref, gain_ref, table_ref, bias_ref, wide, heads_at = refs[dp:]
        tp, upper = place_ref[dp], place_ref[dp + 1]
        for i in range(dp):
            wide[place_ref[i]] = parts[i][...].astype(f32)
        for j in range(dp):
            cut = slice(j * slab, (j + 1) * slab)
            weight = wide[j, : at[1], :slab].astype(bf16)
            router_ref[: at[1], cut] = weight
            router_ref[at[1] :, cut] = weight
            one_ref[:, cut] = wide[j, at[1] : at[2], :slab]
            two_ref[:, cut] = wide[j, at[2] : at[3], :slab]
            for i in range(2):
                heads_at[i, :heads, j * head_slab : (j + 1) * head_slab] = wide[
                    j, at[3 + i] : at[4 + i], :head_slab
                ]
        for i in range(2):
            for h in range(half_heads):
                gain_ref[i : i + 1, h * HD : (h + 1) * HD] = heads_at[
                    i, pl.ds(upper * half_heads + h, 1), :
                ]
        row = lax.broadcasted_iota(jnp.int32, (tokens, tokens), 0)
        column = lax.broadcasted_iota(jnp.int32, (tokens, tokens), 1)
        before = jnp.where(row < column, 1.0, 0.0).astype(bf16)
        lane = lax.broadcasted_iota(jnp.int32, (at[6] - at[5], tokens), 1)
        first = place_ref[0] * experts
        for at_tokens, i in enumerate(token_order):
            ids = parts[i][at[5] : at[6], :].astype(f32)
            for bit, step in ((1, share), (2, 2 * share)):
                turned_ids = jnp.where(
                    lane // step % 2 == 0,
                    pltpu.roll(ids, tokens - step, 1),
                    pltpu.roll(ids, step, 1),
                )
                ids = jnp.where((tp & bit) != 0, turned_ids, ids)
            named = jnp.concatenate(
                [
                    jnp.sum(
                        jnp.where(ids == (first + e).astype(f32), 1.0, 0.0), axis=0, keepdims=True
                    )
                    for e in range(experts)
                ]
            )
            slot = jnp.dot(named.astype(bf16), before, preferred_element_type=f32)
            table_ref[at_tokens] = jnp.where(named > 0.5, slot, -1.0).astype(jnp.int32)
        for i in range(2):
            line = parts[i][at[6] : at[7], :].astype(f32)
            segments = jnp.broadcast_to(line, (tokens, tokens))
            allowed = (column <= row) & (segments.T == segments)
            bias_ref[upper ^ i] = jnp.where(allowed, 0.0, -1e30)

    return kernel_call(
        kernel,
        "unpack",
        [places],
        pieces,
        [
            shape_of((2 * at[1], D), bf16),
            shape_of((1, D), f32),
            shape_of((1, D), f32),
            shape_of((2, half_heads * HD), f32),
            shape_of((dp, experts, tokens), jnp.int32),
            shape_of((2, tokens, tokens), f32),
        ],
        0,
        [
            pltpu.VMEM((dp,) + pieces[0].shape, f32),
            pltpu.VMEM((2, 8, HD), f32),
        ],
        waits=waits,
    )


def packed_sums(groups, heads, places, dp, waits=()):
    slab = D // dp
    head_slab = HD // dp
    here = 0 if heads is None else heads.shape[1] // HD
    count = 4 * 2 * here
    rows = sum(-(-group.shape[0] // 8) * 8 for group in groups)

    def kernel(place_ref, *refs):
        scratch, by_head = refs[-2:]
        outs = refs[-4:-2]
        scratch[...] = jnp.zeros_like(scratch)
        if here:
            first = place_ref[dp] * 2 * here + place_ref[dp + 1] * here
            by_head[...] = jnp.zeros_like(by_head)
            for i in range(2):
                for h in range(here):
                    by_head[pl.ds(i * count + first + h, 1), :] = refs[len(groups)][
                        i : i + 1, h * HD : (h + 1) * HD
                    ]
        for j in range(dp):
            at = 0
            for ref in refs[: len(groups)]:
                scratch[j, at : at + ref.shape[0], :] = ref[:, j * slab : (j + 1) * slab]
                at += -(-ref.shape[0] // 8) * 8
            if here:
                scratch[j, at:, :head_slab] = by_head[:, j * head_slab : (j + 1) * head_slab]
        for i in range(dp):
            outs[i // (dp // 2)][i % (dp // 2)] = scratch[place_ref[i]]

    shape = (dp, rows + 2 * count, slab)
    return kernel_call(
        kernel,
        "packed_sums",
        [places],
        [*groups] + ([heads] if here else []),
        [shape_of((dp // 2,) + shape[1:], f32)] * 2,
        0,
        [pltpu.VMEM(shape, f32), pltpu.VMEM((max(2 * count, 8), HD), f32)],
        waits=waits,
    )


def per_device(
    hidden_in,
    cotangent,
    segment_ids,
    expert_ids,
    first_gain,
    query_weight,
    key_weight,
    value_weight,
    output_weight,
    query_gain,
    key_gain,
    second_gain,
    router_weight,
    gate_weight,
    up_weight,
    down_weight,
):
    data_size = lax.axis_size("dp")
    tensor_size = lax.axis_size("tp")
    half = data_size // 2
    seq_len, width = hidden_in.shape
    share = seq_len // tensor_size
    slab = width // data_size
    me_dp, me_tp = lax.axis_index("dp"), lax.axis_index("tp")
    upper = me_dp // 2 % 2
    own = lambda values: lax.dynamic_slice_in_dim(values, me_tp * share, share, 0)
    local_experts = E // data_size
    first_expert = (me_dp * local_experts).astype(jnp.int32).reshape(1)
    here = jnp.stack([me_tp, upper]).astype(jnp.int32)
    places = jnp.concatenate([owners(weight_masks()), here])
    token_order = [weight_masks().index(mask) for mask in token_masks()]

    hidden_own, cot_own = own(hidden_in), own(cotangent)
    heads_local, head_slab = query_gain.shape
    small = [
        router_weight.T,
        first_gain[None],
        second_gain[None],
        query_gain,
        key_gain,
        expert_ids.T.astype(bf16),
        segment_ids.astype(bf16),
    ]
    small_rows = [array.shape[0] for array in small]
    wide = [jnp.pad(array, ((0, 0), (0, seq_len - array.shape[1]))) for array in small]
    small = gather_dp(jnp.concatenate(wide))
    column_half = heads_local * HD // 2
    kept, given = split_heads([query_weight, key_weight, value_weight], here)
    head_line = gather_line([kept, over_z(given, 1)], z_bits()[1:])
    head_pieces = head_line + [over_y(v) for v in head_line]
    cot_line = gather_dp(cot_own.astype(bf16))
    output_pieces = gather_dp(held([output_weight], bf16, [head_line[-1]]))
    router, gain_one, gain_two, gains, table, bias = unpack(
        small,
        places,
        small_rows,
        local_experts,
        heads_local,
        heads_local // 2,
        token_order,
        waits=[head_line[1]],
    )
    tables = rope_tables(seq_len, HD)
    first_scale = lax.rsqrt(jnp.mean(hidden_in * hidden_in, axis=-1, keepdims=True) + epsilon)
    normed_one = (hidden_in * first_scale * gain_one).astype(bf16)
    mates = gather_tp(over_z(own(normed_one), 1))
    x_slabs = paired([normed_one], mates, places, data_size)
    cot_near = held(cot_line, bf16, [mates[2]])
    cot_far = over_x(cot_near)
    projected, values, squares = project(
        x_slabs, head_pieces, places
    )
    squares = reduce_heads(squares)
    turned_rows, logs, attended, keep, give = attend(
        projected, squares, values, gains, tables, bias, places, data_size, waits=output_pieces[:half]
    )
    parts = output_project(keep, over_z(give, 1), output_pieces, places)
    middle, x_piece, probs = route(scatter_tp(parts)[0], hidden_own, gain_two, router)

    picks = (slice(0, half), slice(half, None))
    cot_far = held([cot_far], bf16, [x_piece])
    cot_all = [cot_near, over_core(cot_near), cot_far, over_core(cot_far)]
    cot_rows = rows_of_slots(cot_all, table, [], token_order)
    hidden_grad = grad_of_hidden(cot_rows, down_weight)
    x_pieces = gather_all(x_piece, [cot_rows], [hidden_grad])
    x_first = rows_of_slots(x_pieces[picks[0]], table[picks[0]], [hidden_grad])
    x_halves = [x_first, rows_of_slots(x_pieces[picks[1]], table[picks[1]], [x_first])]
    back_rows, act, gate_grad, up_grad = expert_step(
        x_halves, gate_weight, up_weight, hidden_grad, first_expert
    )
    second = tokens_of_slots(back_rows, table[picks[1]], half, [])
    first = tokens_of_slots(back_rows, table[picks[0]], 0, [second[0]])
    back = TokenSums(first, second).start()
    out_rows = expert_out(act, down_weight, back.sent)
    out_second = tokens_of_slots(out_rows, table[picks[1]], half, [])
    back.turn(out_second[0])
    out_first = tokens_of_slots(out_rows, table[picks[0]], 0, back.sent)
    chunk = max(local_experts // 4, 1)
    grads = []

    def some_grads(i, *waits):
        *grads[:], mark = expert_weight_grads(
            x_halves, cot_rows, act, gate_grad, up_grad, i * chunk, chunk, list(grads), waits
        )
        return mark

    back.top()
    mark = some_grads(0, *back.sent)
    moe = TokenSums(out_first, out_second).start(*back.sent)
    mark = some_grads(1, mark, *moe.sent)
    back = back.last(mark)

    grad_middle, grad_low, router_sum, gain_sum = route_back(
        back, middle, x_piece, probs, cot_own, gain_two, router, waits=[moe.came[0]]
    )
    low_pieces = gather_tp(grad_low)
    keep, give = output_back(low_pieces, output_pieces, places, [])
    moe.turn(keep)
    grad_values, gqk, inner, gain_sums = attend_back(
        keep, over_z(give, 1), places, data_size, turned_rows, logs, projected, squares, gains, tables, bias,
        [],
    )
    moe.top(gain_sums)
    inner = reduce_heads(inner)
    grad_queries, grad_keys = norm_back(gqk, projected, squares, inner, waits=moe.turned)
    head_grads = [grad_queries, grad_keys, grad_values]
    head_sums_at = WeightSums(*weight_parts(x_slabs, head_grads, places, True))
    parts = project_back(head_grads, head_pieces, places, waits=[head_sums_at.sent])
    terms, crossing = scatter_tp(parts)
    for_mate = combined([term[share:] for term in terms], 0)
    from_mate = over_z(for_mate, 1)
    head_sums_at.along_z(moe.from_top, from_mate)
    mates_low = over_z(held(low_pieces, bf16, [inner]), 1)
    mark = some_grads(2, mark, head_sums_at.sent)
    moe = moe.last(head_sums_at.came)
    low_slabs = paired(low_pieces, [mates_low], places, data_size)
    output_parts = weight_parts(
        low_slabs, [attended], places, False, waits=[head_sums_at.sent]
    )
    output_sums = WeightSums(*output_parts)
    grad_hidden, first_sum = hidden_back(terms, from_mate, hidden_own, grad_middle, gain_one)
    late = packed_sums(
        [router_sum[:E], gain_sum, first_sum],
        gain_sums,
        places,
        data_size,
        [],
    )
    grad_hidden = gather_tp(grad_hidden)
    mark = some_grads(3, mark, head_sums_at.sent)
    came = head_sums_at.came
    head_sums_at.to_mate(mark)
    output_sums.along_z(head_sums_at.sent).to_mate()
    total = reduce_all(*late, [came, mark])
    grad_hidden = absolute_tp(grad_hidden)
    hidden_out = absolute_tp(gather_tp(combined([middle, *moe], 0, sent=f32)))
    late = total[E + 8 :]
    head_sums = late[8:, :head_slab].reshape(2, heads_local * tensor_size, head_slab)
    head_sums = lax.dynamic_slice_in_dim(head_sums, me_tp * heads_local, heads_local, 1)
    grad_query, grad_key, grad_value = head_sums_at.in_order(here, 3, output_sums.sent)
    (grad_output,) = output_sums.in_order(here, 0)
    return (
        hidden_out,
        grad_hidden,
        late[0],
        grad_query,
        grad_key,
        grad_value,
        grad_output,
        head_sums[0],
        head_sums[1],
        total[E],
        total[:E].T,
        *grads,
    )


def solution(mesh):
    return jax.shard_map(
        per_device,
        mesh=mesh,
        in_specs=(
            P("dp", None),
            P("dp", None),
            P("dp", None),
            P("dp", None),
            P("dp"),
            P("dp", "tp"),
            P("dp", "tp"),
            P("dp", "tp"),
            P("tp", "dp"),
            P("tp", "dp"),
            P("tp", "dp"),
            P("dp"),
            P("dp", None),
            P("dp", None, "tp"),
            P("dp", None, "tp"),
            P("dp", "tp", None),
        ),
        out_specs=(
            P("dp", None),
            P("dp", None),
            P("dp"),
            P("dp", "tp"),
            P("dp", "tp"),
            P("dp", "tp"),
            P("tp", "dp"),
            P("tp", "dp"),
            P("tp", "dp"),
            P("dp"),
            P("dp", None),
            P("dp", None, "tp"),
            P("dp", None, "tp"),
            P("dp", "tp", None),
        ),
        check_vma=False,
    )
```
